32 devices in a mesh: fsdp: 16 (over z, y, x), tp: 2 (over core).
Axes of the slice: x: 2, y: 2, z: 4, core: 2. Of those that a mesh axis runs over, the one named last changes fastest.
Arguments:
- hidden_in: bfloat16 [8192, 1024], P(('fsdp', 'tp')), may hold values from -6 to 6
- segment_ids: int32 [8192], P(('fsdp', 'tp')), may hold values from 0 to 2, as said below
- positions: int32 [8192], P(('fsdp', 'tp')), may hold values from 0 to 399, as said below
- query_weight: float32 [1024, 1024], P('fsdp', 'tp'), may hold values from -0.1875 to 0.1875
- key_weight: float32 [1024, 1024], P('fsdp', 'tp'), may hold values from -0.1875 to 0.1875
- value_weight: float32 [1024, 1024], P('fsdp', 'tp'), may hold values from -0.1875 to 0.1875
- output_weight: float32 [1024, 1024], P('tp', 'fsdp'), may hold values from -1.5 to 1.5
- up_weight: float32 [1024, 4096], P('fsdp', 'tp'), may hold values from -0.1875 to 0.1875
- down_weight: float32 [4096, 1024], P('tp', 'fsdp'), may hold values from -0.09375 to 0.09375
- query_bias: float32 [1024], P(('fsdp', 'tp')), may hold values from -1.8 to 1.8
- key_bias: float32 [1024], P(('fsdp', 'tp')), may hold values from -1.8 to 1.8
- value_bias: float32 [1024], P(('fsdp', 'tp')), may hold values from -1.8 to 1.8
- output_bias: float32 [1024], P(('fsdp', 'tp')), may hold values from -1.8 to 1.8
- up_bias: float32 [4096], P(('fsdp', 'tp')), may hold values from -3 to 3
- down_bias: float32 [1024], P(('fsdp', 'tp')), may hold values from -1.8 to 1.8
- attn_gain: float32 [1024], P(('fsdp', 'tp')), may hold values from 0.1 to 1.9
- attn_shift: float32 [1024], P(('fsdp', 'tp')), may hold values from -1.8 to 1.8
- ffn_gain: float32 [1024], P(('fsdp', 'tp')), may hold values from 0.1 to 1.9
- ffn_shift: float32 [1024], P(('fsdp', 'tp')), may hold values from -1.8 to 1.8
- proj_wide: float32 [1024, 128], P(('fsdp', 'tp')), may hold values from -0.1875 to 0.1875
- proj_mid: float32 [1024, 96], P(('fsdp', 'tp')), may hold values from -0.1875 to 0.1875
- proj_narrow: float32 [1024, 64], P(('fsdp', 'tp')), may hold values from -0.1875 to 0.1875
- cot_wide: bfloat16 [8192, 128], P(('fsdp', 'tp')), may hold values from -6 to 6
- cot_mid: bfloat16 [8192, 96], P(('fsdp', 'tp')), may hold values from -6 to 6
- cot_narrow: bfloat16 [8192, 64], P(('fsdp', 'tp')), may hold values from -6 to 6
Outputs:
- embed_wide: float32 [8192, 128], P(('fsdp', 'tp'))
- embed_mid: float32 [8192, 96], P(('fsdp', 'tp'))
- embed_narrow: float32 [8192, 64], P(('fsdp', 'tp'))
- grad_hidden: float32 [8192, 1024], P(('fsdp', 'tp'))
- grad_query_weight: float32 [1024, 1024], P('fsdp', 'tp')
- grad_key_weight: float32 [1024, 1024], P('fsdp', 'tp')
- grad_value_weight: float32 [1024, 1024], P('fsdp', 'tp')
- grad_output_weight: float32 [1024, 1024], P('tp', 'fsdp')
- grad_up_weight: float32 [1024, 4096], P('fsdp', 'tp')
- grad_down_weight: float32 [4096, 1024], P('tp', 'fsdp')
- grad_query_bias: float32 [1024], P(('fsdp', 'tp'))
- grad_key_bias: float32 [1024], P(('fsdp', 'tp'))
- grad_value_bias: float32 [1024], P(('fsdp', 'tp'))
- grad_output_bias: float32 [1024], P(('fsdp', 'tp'))
- grad_up_bias: float32 [4096], P(('fsdp', 'tp'))
- grad_down_bias: float32 [1024], P(('fsdp', 'tp'))
- grad_attn_gain: float32 [1024], P(('fsdp', 'tp'))
- grad_attn_shift: float32 [1024], P(('fsdp', 'tp'))
- grad_ffn_gain: float32 [1024], P(('fsdp', 'tp'))
- grad_ffn_shift: float32 [1024], P(('fsdp', 'tp'))
- grad_proj_wide: float32 [1024, 128], P(('fsdp', 'tp'))
- grad_proj_mid: float32 [1024, 96], P(('fsdp', 'tp'))
- grad_proj_narrow: float32 [1024, 64], P(('fsdp', 'tp'))
The draws below stay inside these ranges and needn't reach their ends.
Inputs may be any that keep to these rules, and one draw needn't show every extreme that they name: `segment_ids`: within each sequence of 512 consecutive tokens documents are numbered 0, 1, 2 and so on in order and never falling; each document has 60 to 400 tokens except the last of a sequence, which may be cut short, and each sequence holds one document of exactly 400 tokens. In the first sequence every other document has exactly 60 tokens, save the cut last one. `positions`: each token's place within its document, counting from 0 at the document's first token.
All inputs are finite; a program needn't handle non-finite values.
Results may differ from the reference program's by a relative error of at most 0.024.
Values may be sent and summed in bfloat16 or wider, within the bound.
No kernel may reach another device: no remote copies, remote signals or barrier semaphores. Data moves between devices by JAX's collectives and lax.ppermute only.
A program may use at most 128 MiB of HBM per device.

```python
import math
import jax
import jax.numpy as jnp
from jax import lax

D = 1024
HEADS = 16
HD = 64
FF = 4096
P1 = 128
P2 = 96
P3 = 64
SEQ_LEN = 512
DOC_MIN = 60
DOC_MOST = 400
TOKENS = 8192


def document_layout(key):
    total_seqs = TOKENS // SEQ_LEN
    most_docs = SEQ_LEN // DOC_MIN + 2
    doc_sizes = jax.random.randint(jax.random.fold_in(key, 11), (total_seqs, most_docs), DOC_MIN, DOC_MOST + 1)
    seq_index = jnp.arange(total_seqs)[:, None]
    doc_sizes = jnp.where(seq_index == 0, DOC_MIN, doc_sizes)
    chosen = jax.random.randint(jax.random.fold_in(key, 12), (total_seqs, 1), 0, 2)
    doc_slot = jnp.arange(most_docs)[None, :]
    doc_cap = jnp.where((doc_slot == 0) & (chosen == 1), SEQ_LEN - DOC_MOST, DOC_MOST)
    doc_sizes = jnp.minimum(doc_sizes, doc_cap)
    doc_sizes = jnp.where(doc_slot == chosen, DOC_MOST, doc_sizes)
    doc_ends = jnp.cumsum(doc_sizes, axis=1)
    token_place = jnp.arange(SEQ_LEN)[None, :, None]
    passed = token_place >= doc_ends[:, None, :]
    segment = jnp.sum(passed.astype(jnp.int32), axis=-1)
    begin = jnp.sum(jnp.where(passed, doc_sizes[:, None, :], 0), axis=-1)
    place_in_doc = token_place[:, :, 0] - begin
    return (segment.reshape(-1).astype(jnp.int32), place_in_doc.reshape(-1).astype(jnp.int32))


def draw_segment_ids(key, part):
    return document_layout(jax.random.fold_in(key, 5))[0]


def draw_positions(key, part):
    return document_layout(jax.random.fold_in(key, 5))[1]


def level_of(key, extent, split, low, high):
    def one(axis_at, shards_of):
        steps = jax.random.uniform(jax.random.fold_in(jax.random.fold_in(key, 6), axis_at), (shards_of,), jnp.float32, low / len(split), high / len(split))
        return jnp.repeat(jnp.exp(steps), extent[axis_at] // shards_of).reshape((-1,) + (1,) * (len(extent) - axis_at - 1))

    loudness = one(*split[0])
    for cut in split[1:]:
        loudness = loudness * one(*cut)
    return loudness


def noise(key, shape, deviation, limit, split=(), kind=jnp.bfloat16):
    values = jax.random.normal(key, shape, jnp.float32) * deviation
    if len(split) > 0:
        values = level_of(key, shape, split, -0.22, 0.18) * values
    return jnp.clip(values, min=-limit, max=limit).astype(kind)


def setup_inputs(seed: int = 0) -> dict:
    key_of = jax.random.split(jax.random.key(seed), 26)
    hidden_in = noise(key_of[0], (TOKENS, D), 1.0, 6.0, ((0, 32),))
    segment_ids = draw_segment_ids(jax.random.fold_in(key_of[25], 71), 0)
    positions = draw_positions(jax.random.fold_in(key_of[25], 71), 0)
    query_weight = noise(key_of[3], (D, D), D ** -0.5, 0.1875, ((0, 16), (1, 2)), jnp.float32)
    key_weight = noise(key_of[4], (D, D), D ** -0.5, 0.1875, ((0, 16), (1, 2)), jnp.float32)
    value_weight = noise(key_of[5], (D, D), D ** -0.5, 0.1875, ((0, 16), (1, 2)), jnp.float32)
    output_weight = noise(key_of[6], (D, D), (D // 64) ** -0.5, 1.5, ((0, 2), (1, 16)), jnp.float32)
    up_weight = noise(key_of[7], (D, FF), D ** -0.5, 0.1875, ((0, 16), (1, 2)), jnp.float32)
    down_weight = noise(key_of[8], (FF, D), FF ** -0.5, 0.09375, ((0, 2), (1, 16)), jnp.float32)
    query_bias = noise(key_of[9], (D,), 0.3, 1.8, ((0, 32),), jnp.float32)
    key_bias = noise(key_of[10], (D,), 0.3, 1.8, ((0, 32),), jnp.float32)
    value_bias = noise(key_of[11], (D,), 0.3, 1.8, ((0, 32),), jnp.float32)
    output_bias = noise(key_of[12], (D,), 0.3, 1.8, ((0, 32),), jnp.float32)
    up_bias = noise(key_of[13], (FF,), 0.5, 3.0, ((0, 32),), jnp.float32)
    down_bias = noise(key_of[14], (D,), 0.3, 1.8, ((0, 32),), jnp.float32)
    attn_gain = jnp.clip(1.0 + 0.18 * jax.random.normal(key_of[15], (D,), jnp.float32), 0.1, 1.9)
    attn_shift = noise(key_of[16], (D,), 0.3, 1.8, ((0, 32),), jnp.float32)
    ffn_gain = jnp.clip(1.0 + 0.18 * jax.random.normal(key_of[17], (D,), jnp.float32), 0.1, 1.9)
    ffn_shift = noise(key_of[18], (D,), 0.3, 1.8, ((0, 32),), jnp.float32)
    proj_wide = noise(key_of[19], (D, P1), D ** -0.5, 0.1875, ((0, 32),), jnp.float32)
    proj_mid = noise(key_of[20], (D, P2), D ** -0.5, 0.1875, ((0, 32),), jnp.float32)
    proj_narrow = noise(key_of[21], (D, P3), D ** -0.5, 0.1875, ((0, 32),), jnp.float32)
    cot_wide = noise(key_of[22], (TOKENS, P1), 1.0, 6.0, ((0, 32),))
    cot_mid = noise(key_of[23], (TOKENS, P2), 1.0, 6.0, ((0, 32),))
    cot_narrow = noise(key_of[24], (TOKENS, P3), 1.0, 6.0, ((0, 32),))
    return dict(hidden_in=hidden_in, segment_ids=segment_ids, positions=positions, query_weight=query_weight, key_weight=key_weight, value_weight=value_weight, output_weight=output_weight, up_weight=up_weight, down_weight=down_weight, query_bias=query_bias, key_bias=key_bias, value_bias=value_bias, output_bias=output_bias, up_bias=up_bias, down_bias=down_bias, attn_gain=attn_gain, attn_shift=attn_shift, ffn_gain=ffn_gain, ffn_shift=ffn_shift, proj_wide=proj_wide, proj_mid=proj_mid, proj_narrow=proj_narrow, cot_wide=cot_wide, cot_mid=cot_mid, cot_narrow=cot_narrow)


@jax.custom_vjp
def low(v):
    return lax.optimization_barrier(v.astype(jnp.bfloat16)).astype(jnp.float32)

@jax.custom_vjp
def low_back(v):
    return v

def low_keep(v):
    return (low(v), None)

def low_pass(kept, grad):
    return (grad,)

def back_keep(v):
    return (v, None)

def back_low(kept, grad):
    return (low(grad),)
low.defvjp(low_keep, low_pass)
low_back.defvjp(back_keep, back_low)
EPSILON = 1e-05
MASKED_SCORE = -1e+30
ROPE_BASE = 10000.0
HIGHEST_PRECISION = lax.Precision.HIGHEST

def product(left_side, right_side):
    return jnp.dot(left_side, right_side, precision=HIGHEST_PRECISION, preferred_element_type=jnp.float32)

def rope_tables(places, head_width):
    half_width = head_width // 2
    inv_freq = jnp.exp(jnp.arange(half_width, dtype=jnp.float32) * (-2.0 * math.log(ROPE_BASE) / head_width))
    angles = places.astype(jnp.float32)[:, None] * inv_freq[None, :]
    cos_table = jnp.cos(angles)
    sin_table = jnp.sin(angles)
    return (jnp.concatenate([cos_table, cos_table], axis=-1), jnp.concatenate([sin_table, sin_table], axis=-1))

def rotate(values, cos_table, sin_table):
    half_width = values.shape[-1] // 2
    turned = jnp.concatenate([-values[..., half_width:], values[..., :half_width]], axis=-1)
    return values * cos_table + turned * sin_table

def normalize(values, norm_gain, norm_shift):
    row_mean = lax.optimization_barrier(jnp.mean(values, axis=-1, keepdims=True))
    centered = values - row_mean
    variance = lax.optimization_barrier(jnp.mean(centered * centered, axis=-1, keepdims=True))
    return centered * lax.rsqrt(variance + EPSILON) * norm_gain + norm_shift

def attend(query_rot, key_rot, value_low, segments):
    raw_scores = low_back(jnp.einsum('qhd,khd->hqk', query_rot, key_rot, precision=HIGHEST_PRECISION))
    same_doc = segments[:, None] == segments[None, :]
    scores = jnp.where(same_doc[None], raw_scores * HD ** (-0.5), MASKED_SCORE)
    attention_weights = jax.nn.softmax(scores, axis=-1)
    return jnp.einsum('hqk,khd->qhd', low(attention_weights), value_low, precision=HIGHEST_PRECISION)

def attend_item(seq_item):
    return attend(seq_item[0], seq_item[1], seq_item[2], seq_item[3])

def block_forward(group_rows, segments, places, rounded):
    query_weight, key_weight, value_weight, output_weight, up_weight, down_weight, query_bias, key_bias, value_bias, output_bias, up_bias, down_bias, attn_gain, attn_shift, ffn_gain, ffn_shift, proj_wide, proj_mid, proj_narrow = rounded
    row_total = group_rows.shape[0]
    seq_count = row_total // SEQ_LEN
    query_pre = low_back(product(group_rows, query_weight) + query_bias)
    key_pre = low_back(product(group_rows, key_weight) + key_bias)
    value_pre = low(low_back(product(group_rows, value_weight) + value_bias))
    cos_table, sin_table = rope_tables(places, HD)
    cos_table = cos_table[:, None, :]
    sin_table = sin_table[:, None, :]
    query_rot = low(rotate(query_pre.reshape(row_total, HEADS, HD), cos_table, sin_table))
    key_rot = low(rotate(key_pre.reshape(row_total, HEADS, HD), cos_table, sin_table))

    def by_sequence(values):
        return values.reshape(seq_count, SEQ_LEN, HEADS, HD)
    context = lax.map(jax.checkpoint(attend_item), (by_sequence(query_rot), by_sequence(key_rot), by_sequence(value_pre), segments.reshape(seq_count, SEQ_LEN)))
    context = low_back(low(context.reshape(row_total, D)))
    attn_branch = low_back(product(context, output_weight))
    mid_norm = normalize(group_rows + attn_branch + output_bias, attn_gain, attn_shift)
    up_pre = low_back(product(low(mid_norm), up_weight) + up_bias)
    act_low = low(jax.nn.gelu(up_pre, approximate=False))
    ffn_branch = low_back(product(act_low, down_weight))
    top_low = low(normalize(mid_norm + ffn_branch + down_bias, ffn_gain, ffn_shift))
    return (product(top_low, proj_wide), product(top_low, proj_mid), product(top_low, proj_narrow))

def reference(hidden_in, segment_ids, positions, query_weight, key_weight, value_weight, output_weight, up_weight, down_weight, query_bias, key_bias, value_bias, output_bias, up_bias, down_bias, attn_gain, attn_shift, ffn_gain, ffn_shift, proj_wide, proj_mid, proj_narrow, cot_wide, cot_mid, cot_narrow):
    masters = (query_weight, key_weight, value_weight, output_weight, up_weight, down_weight, query_bias, key_bias, value_bias, output_bias, up_bias, down_bias, attn_gain, attn_shift, ffn_gain, ffn_shift, proj_wide, proj_mid, proj_narrow)
    masters = tuple((master.astype(jnp.float32) for master in masters))
    total_seqs = TOKENS // SEQ_LEN
    group_seqs = math.gcd(total_seqs, max(1, 4096 // SEQ_LEN))
    group_count = total_seqs // group_seqs
    group_size = group_seqs * SEQ_LEN
    seg_groups = segment_ids.reshape(group_count, group_size)
    pos_groups = positions.reshape(group_count, group_size)

    def whole_layer(inputs, params):
        rounded = tuple((low(master_value) for master_value in params))

        def one_group(group_item):
            return block_forward(group_item[0], group_item[1], group_item[2], rounded)
        outputs = lax.map(jax.checkpoint(one_group), (inputs.reshape(group_count, group_size, D), seg_groups, pos_groups))
        return tuple((result.reshape(TOKENS, result.shape[-1]) for result in outputs))
    embeds, pull_back = jax.vjp(whole_layer, hidden_in.astype(jnp.float32), masters)
    grad_inputs, grad_masters = pull_back((cot_wide.astype(jnp.float32), cot_mid.astype(jnp.float32), cot_narrow.astype(jnp.float32)))
    return (embeds[0], embeds[1], embeds[2], grad_inputs, grad_masters[0], grad_masters[1], grad_masters[2], grad_masters[3], grad_masters[4], grad_masters[5], grad_masters[6], grad_masters[7], grad_masters[8], grad_masters[9], grad_masters[10], grad_masters[11], grad_masters[12], grad_masters[13], grad_masters[14], grad_masters[15], grad_masters[16], grad_masters[17], grad_masters[18])
```

```python
import functools
import math

import jax
import jax.numpy as jnp
from jax import lax
from jax.experimental import pallas as pl
from jax.experimental.pallas import tpu as pltpu
from jax.sharding import PartitionSpec as P

HD = 64
SEQ_LEN = 512


EPSILON = 1e-05
MASKED_SCORE = -1e30
ROPE_BASE = 10000.0


def rope_tables(places, head_width):
    half_width = head_width // 2
    inv_freq = jnp.exp(
        jnp.arange(half_width, dtype=jnp.float32) * (-2.0 * math.log(ROPE_BASE) / head_width)
    )
    angles = places.astype(jnp.float32)[:, None] * inv_freq[None, :]
    cos_table = jnp.cos(angles)
    sin_table = jnp.sin(angles)
    return (
        jnp.concatenate([cos_table, cos_table], axis=-1),
        jnp.concatenate([sin_table, sin_table], axis=-1),
    )


def rotate(values, cos_table, sin_table):
    half_width = values.shape[-1] // 2
    turned = jnp.concatenate([-values[..., half_width:], values[..., :half_width]], axis=-1)
    return values * cos_table + turned * sin_table


def rotate_back(gradient, cos_table, sin_table):
    half_width = gradient.shape[-1] // 2
    turned = gradient * sin_table
    return gradient * cos_table + jnp.concatenate(
        [turned[..., half_width:], -turned[..., :half_width]], axis=-1
    )


def normalize(values, norm_gain, norm_shift):
    row_mean = jnp.mean(values, axis=-1, keepdims=True)
    centered = values - row_mean
    variance = jnp.mean(centered * centered, axis=-1, keepdims=True)
    inv_std = lax.rsqrt(variance + EPSILON)
    unit_rows = centered * inv_std
    return (unit_rows * norm_gain + norm_shift, unit_rows, inv_std)


def normalize_back(gradient, unit_rows, inv_std, norm_gain):
    scaled = gradient * norm_gain
    return inv_std * (
        scaled
        - jnp.mean(scaled, axis=-1, keepdims=True)
        - unit_rows * jnp.mean(scaled * unit_rows, axis=-1, keepdims=True)
    )


def product(left_side, right_side):
    return jnp.dot(left_side, right_side, preferred_element_type=jnp.float32)


def product_tn(left_side, right_side):
    return lax.dot_general(
        left_side, right_side, (((0,), (0,)), ((), ())), preferred_element_type=jnp.float32
    )


def product_nt(left_side, right_side):
    return lax.dot_general(
        left_side, right_side, (((1,), (1,)), ((), ())), preferred_element_type=jnp.float32
    )


def gelu_exact(values):
    return jax.nn.gelu(values, approximate=False)

ROUNDS = (
    {"x": (0, 0, 1), "z": (3, 0, 0), "y": (0, 1, 0)},
    {"x": (3, 0, 1), "y": (3, 1, 0), "z": (2, 0, 0)},
    {"z": (2, 1, 0), "x": (2, 0, 1), "y": (3, 1, 1)},
    {"y": (2, 1, 1), "x": (0, 1, 1), "z": (1, 0, 0)},
    {"x": (1, 0, 1), "y": (1, 1, 0), "z": (1, 1, 1)},
)
KEYS = tuple((z, y, x) for z in range(4) for y in range(2) for x in range(2))
OWN = (0, 0, 0)


def place(z, y, x):
    return (z * 2 + y) * 2 + x


def hop(link):
    def target(z, y, x):
        if link == "x":
            return place(z, y, 1 - x)
        if link == "y":
            return place(z, 1 - y, x)
        return place((z + 1) % 4, y, x)

    return [(place(*k), target(*k)) for k in KEYS]


HOPS = {link: hop(link) for link in "xyz"}
BACK = {link: [(b, a) for a, b in pairs] for link, pairs in HOPS.items()}


def sender_key(key, link):
    z, y, x = key
    if link == "x":
        return (z, y, 1 - x)
    if link == "y":
        return (z, 1 - y, x)
    return ((z + 1) % 4, y, x)


def gridded():
    return lax.axis_size("fsdp") == 16


def gather_rows(shard):
    if not gridded():
        return lax.all_gather(shard, "fsdp", axis=0, tiled=True)
    have = {OWN: shard}
    for step in ROUNDS:
        have.update(
            {
                key: lax.ppermute(have[sender_key(key, link)], "fsdp", HOPS[link])
                for link, key in step.items()
            }
        )
    return jnp.concatenate([have[key] for key in KEYS], axis=0)


def scatter_rows(full):
    if not gridded():
        return lax.psum_scatter(full, "fsdp", scatter_dimension=0, tiled=True)
    rows = full.shape[0] // 16
    held = {key: full[rows * i : rows * (i + 1)] for i, key in enumerate(KEYS)}
    for step in ROUNDS[::-1]:
        moved = [
            (sender_key(key, link), lax.ppermute(held.pop(key), "fsdp", BACK[link]))
            for link, key in step.items()
        ]
        for key, part in moved:
            held[key] = held[key] + part
    return held[OWN]


def other_core(values):
    return lax.ppermute(values, "tp", [(0, 1), (1, 0)])


def reorder_kernel(inverse, place_ref, in_ref, out_ref):
    z, y, x = place_ref[0], place_ref[1], place_ref[2]
    turn = x == 1
    for block in range(8):
        zb, yb = block // 2, block % 2
        away = (zb + 4 - z) % 4 if inverse else (zb + z) % 4
        source = pl.multiple_of((away * 2 + (yb + y) % 2) * 128, 128)
        part = in_ref[:, pl.ds(source, 128)].astype(jnp.float32)
        part = jnp.where(turn, pltpu.roll(part, 64, 1), part)
        out_ref[:, block * 128 : block * 128 + 128] = part.astype(out_ref.dtype)


def reorder(values, inverse):
    if not gridded():
        return values
    me = lax.axis_index("fsdp")
    places = jnp.stack([me // 4, (me // 2) % 2, me % 2]).astype(jnp.int32)
    return pl.pallas_call(
        functools.partial(reorder_kernel, inverse),
        out_shape=jax.ShapeDtypeStruct(values.shape, values.dtype),
        in_specs=[
            pl.BlockSpec(memory_space=pltpu.SMEM),
            pl.BlockSpec(memory_space=pltpu.VMEM),
        ],
        out_specs=pl.BlockSpec(memory_space=pltpu.VMEM),
    )(places, values)


def halves(values):
    first = lax.axis_index("tp") == 0
    other = other_core(values)
    return jnp.concatenate(
        [jnp.where(first, values, other), jnp.where(first, other, values)], axis=0
    )


def swap_halves(values):
    half = values.shape[0] // 2
    return jnp.concatenate([values[half:], values[:half]], axis=0)


def sum_cores(partial_rows):
    low = partial_rows.astype(jnp.bfloat16)
    return low.astype(jnp.float32) + swap_halves(other_core(low)).astype(jnp.float32)


def local(
    hidden_in,
    segment_ids,
    positions,
    query_weight,
    key_weight,
    value_weight,
    output_weight,
    up_weight,
    down_weight,
    query_bias,
    key_bias,
    value_bias,
    output_bias,
    up_bias,
    down_bias,
    attn_gain,
    attn_shift,
    ffn_gain,
    ffn_shift,
    proj_wide,
    proj_mid,
    proj_narrow,
    cot_wide,
    cot_mid,
    cot_narrow,
):
    low, wide = jnp.bfloat16, jnp.float32
    tp_rank = lax.axis_index("tp")
    own_rows = hidden_in.shape[0]
    width = hidden_in.shape[1]
    head_width = query_weight.shape[1]
    heads_here = head_width // HD
    hidden_here = up_weight.shape[1]
    piece = query_bias.shape[0]

    vectors = jnp.stack(
        [query_bias, key_bias, value_bias, output_bias, down_bias, attn_gain, attn_shift, ffn_gain, ffn_shift],
        axis=1,
    )
    small = jnp.concatenate(
        [vectors, up_bias.reshape(piece, -1), jnp.zeros((piece, 115), wide), proj_wide, proj_mid, proj_narrow],
        axis=1,
    ).astype(low)
    small = halves(small)
    first_group = jnp.concatenate(
        [w.astype(low) for w in (query_weight, key_weight, value_weight, output_weight.T)] + [small[:, :128]],
        axis=1,
    )
    attn_all = gather_rows(first_group)
    up_all = gather_rows(up_weight.astype(low))
    last_group = jnp.concatenate([down_weight.T.astype(low), small[:, 128:]], axis=1)
    down_group = gather_rows(last_group)
    down_all = down_group[:, :hidden_here]
    proj_all = down_group[:, hidden_here:]
    qkv_all = attn_all[:, : 3 * head_width]
    out_all = attn_all[:, 3 * head_width : 4 * head_width]
    vector_rows = attn_all[:, 4 * head_width :].T.astype(wide)[:16]
    plain = reorder(vector_rows, True)
    qkv_shift = lax.dynamic_slice_in_dim(plain[:3], tp_rank * head_width, head_width, 1).reshape(1, -1)
    up_shift = lax.dynamic_slice_in_dim(
        plain[9:13].T.reshape(1, -1), tp_rank * hidden_here, hidden_here, 1
    )
    bias_output, bias_down, gain_attn, shift_attn, gain_ffn, shift_ffn = (
        vector_rows[i : i + 1] for i in range(3, 9)
    )

    tags = jnp.stack([segment_ids, positions])
    tags = jnp.concatenate([tags, other_core(tags)], axis=1)
    segments, places = tags[0], tags[1]
    x_all = reorder(jnp.concatenate([hidden_in, other_core(hidden_in)], axis=0), False)
    cot_own = jnp.concatenate([cot_wide, cot_mid, cot_narrow], axis=1)
    cot_all = jnp.concatenate([cot_own, other_core(cot_own)], axis=0)
    total_rows = 2 * own_rows

    cos_table, sin_table = rope_tables(places, HD)
    cos_table = cos_table[:, None, :]
    sin_table = sin_table[:, None, :]
    score_scale = HD ** (-0.5)
    qkv_pre = (product(x_all, qkv_all) + qkv_shift).reshape(total_rows, 3, heads_here, HD)
    query_rot = rotate(qkv_pre[:, 0], cos_table, sin_table).astype(low)
    key_rot = rotate(qkv_pre[:, 1], cos_table, sin_table).astype(low)
    value_low = qkv_pre[:, 2].astype(low)

    def block_scores():
        raw_scores = jnp.einsum("qhd,khd->hqk", query_rot, key_rot, preferred_element_type=wide)
        same_doc = (segments[:, None] == segments[None, :])[None]
        return jnp.where(same_doc, raw_scores * score_scale, MASKED_SCORE)

    scores = block_scores()
    row_max = jnp.max(scores, axis=-1, keepdims=True)
    shifted_exp = jnp.exp(scores - row_max)
    row_sum = jnp.sum(shifted_exp, axis=-1, keepdims=True)
    attention = (shifted_exp / row_sum).astype(low)
    context = jnp.einsum("hqk,khd->qhd", attention, value_low, preferred_element_type=wide)
    context_flat = context.astype(low).reshape(total_rows, head_width)
    attn_sum = sum_cores(product_nt(context_flat, out_all))
    mid_pre = x_all.astype(wide) + attn_sum + bias_output
    mid_norm, unit_one, inv_one = normalize(mid_pre, gain_attn, shift_attn)
    mid_low = mid_norm.astype(low)
    up_pre = product(mid_low, up_all) + up_shift
    act_low = gelu_exact(up_pre).astype(low)
    ffn_sum = sum_cores(product_nt(act_low, down_all))
    top_pre = mid_norm + ffn_sum + bias_down
    top_norm, unit_two, inv_two = normalize(top_pre, gain_ffn, shift_ffn)
    top_low = top_norm.astype(low)
    wide_cols, mid_cols = proj_wide.shape[1], proj_mid.shape[1]
    embed_all = product(top_low[:own_rows], proj_all)
    embed_wide = embed_all[:, :wide_cols]
    embed_mid = embed_all[:, wide_cols : wide_cols + mid_cols]
    embed_narrow = embed_all[:, wide_cols + mid_cols :]

    proj_cols = cot_all.shape[1]
    share = 192
    cot_share = lax.dynamic_slice_in_dim(
        jnp.pad(cot_all, ((0, 0), (0, 2 * share - proj_cols))), tp_rank * share, share, 1
    )
    grad_proj = product_tn(top_low, cot_share)
    grad_out_norm = product_nt(cot_all, proj_all)
    grad_ffn_gain = jnp.sum(grad_out_norm * unit_two, axis=0)
    grad_ffn_shift = jnp.sum(grad_out_norm, axis=0)
    grad_top = normalize_back(grad_out_norm, unit_two, inv_two, gain_ffn)
    grad_down_shift = jnp.sum(grad_top, axis=0)
    grad_top_low = grad_top.astype(low)
    down_part = scatter_rows(product_tn(grad_top_low, act_low).astype(low))
    grad_act = product(grad_top_low, down_all)
    gelu_value, gelu_pull = jax.vjp(gelu_exact, up_pre)
    grad_up_pre = gelu_pull(grad_act)[0].astype(low)
    grad_up_shift = jnp.sum(grad_up_pre, axis=0, dtype=wide)
    up_part = scatter_rows(product_tn(mid_low, grad_up_pre).astype(low))
    grad_mid = grad_top + sum_cores(product_nt(grad_up_pre, up_all))
    grad_attn_gain = jnp.sum(grad_mid * unit_one, axis=0)
    grad_attn_shift = jnp.sum(grad_mid, axis=0)
    grad_mid_pre = normalize_back(grad_mid, unit_one, inv_one, gain_attn)
    grad_output_shift = jnp.sum(grad_mid_pre, axis=0)
    grad_mid_low = grad_mid_pre.astype(low)
    grad_context = product(grad_mid_low, out_all).astype(low).reshape(total_rows, heads_here, HD)
    grad_output = product_tn(grad_mid_low, context_flat)

    attention_wide = jnp.exp(block_scores() - (row_max + jnp.log(row_sum)))
    grad_prob = jnp.einsum("qhd,khd->hqk", grad_context, value_low, preferred_element_type=wide)
    row_delta = jnp.sum(attention_wide * grad_prob, axis=-1, keepdims=True)
    grad_raw = (attention_wide * (grad_prob - row_delta) * score_scale).astype(low)
    grad_query = jnp.einsum("hqk,khd->qhd", grad_raw, key_rot, preferred_element_type=wide)
    grad_key = jnp.einsum("hqk,qhd->khd", grad_raw, query_rot, preferred_element_type=wide)
    grad_value = jnp.einsum("hqk,qhd->khd", attention_wide.astype(low), grad_context, preferred_element_type=wide)
    grad_qkv = jnp.concatenate(
        [
            rotate_back(grad_query, cos_table, sin_table).reshape(total_rows, head_width).astype(low),
            rotate_back(grad_key, cos_table, sin_table).reshape(total_rows, head_width).astype(low),
            grad_value.reshape(total_rows, head_width).astype(low),
        ],
        axis=1,
    )
    grad_qkv_shift = jnp.sum(grad_qkv, axis=0, dtype=wide).reshape(3, head_width)
    grad_qkv_weight = product_tn(x_all, grad_qkv)

    mine = jnp.concatenate([grad_qkv_shift, grad_up_shift.reshape(-1, head_width)], axis=0).astype(low)
    both = halves(mine[None])
    both_qkv = both[:, :3].transpose(1, 0, 2).reshape(3, width)
    both_up = both[:, 3:].reshape(width, -1).T
    moved = reorder(jnp.concatenate([both_qkv, both_up, jnp.zeros((9, width), low)], axis=0).astype(wide), False)
    vector_grads = jnp.concatenate(
        [
            moved[:3],
            jnp.stack([grad_output_shift, grad_down_shift, grad_attn_gain, grad_attn_shift, grad_ffn_gain, grad_ffn_shift]),
            moved[3:7],
        ],
        axis=0,
    )
    last_share = jnp.concatenate(
        [
            grad_proj[:, : proj_cols - share],
            vector_grads.T,
            jnp.zeros((width, 2 * share - proj_cols - 13), wide),
        ],
        axis=1,
    )
    share_grads = jnp.where(tp_rank == 1, last_share, grad_proj)
    attn_part = scatter_rows(
        jnp.concatenate([grad_qkv_weight, grad_output, share_grads], axis=1).astype(low)
    )
    grad_x = product_nt(grad_qkv, qkv_all).astype(low)
    grad_x_own = (
        grad_mid_pre[:own_rows]
        + grad_x[:own_rows].astype(wide)
        + other_core(grad_x[own_rows:]).astype(wide)
    )
    grad_hidden = reorder(grad_x_own, True)

    small_part = attn_part[:, 4 * head_width :]
    small_other = other_core(small_part)
    joined = jnp.where(
        tp_rank == 0,
        jnp.concatenate([small_part, small_other], axis=1),
        jnp.concatenate([small_other, small_part], axis=1),
    ).astype(wide)
    joined = lax.dynamic_slice_in_dim(joined, tp_rank * piece, piece, 0)
    attn_part = attn_part.astype(wide)
    columns = [joined[:, proj_cols + i] for i in range(9)]
    return (
        embed_wide,
        embed_mid,
        embed_narrow,
        grad_hidden,
        attn_part[:, :head_width],
        attn_part[:, head_width : 2 * head_width],
        attn_part[:, 2 * head_width : 3 * head_width],
        attn_part[:, 3 * head_width : 4 * head_width].T,
        up_part.astype(wide),
        down_part.astype(wide).T,
        columns[0],
        columns[1],
        columns[2],
        columns[3],
        joined[:, proj_cols + 9 : proj_cols + 13].reshape(-1),
        columns[4],
        columns[5],
        columns[6],
        columns[7],
        columns[8],
        joined[:, :wide_cols],
        joined[:, wide_cols : wide_cols + mid_cols],
        joined[:, wide_cols + mid_cols : proj_cols],
    )


def solution(mesh):
    return jax.shard_map(
        local,
        mesh=mesh,
        in_specs=(
            P(("fsdp", "tp"), None),
            P(("fsdp", "tp")),
            P(("fsdp", "tp")),
            P("fsdp", "tp"),
            P("fsdp", "tp"),
            P("fsdp", "tp"),
            P("tp", "fsdp"),
            P("fsdp", "tp"),
            P("tp", "fsdp"),
            P(("fsdp", "tp")),
            P(("fsdp", "tp")),
            P(("fsdp", "tp")),
            P(("fsdp", "tp")),
            P(("fsdp", "tp")),
            P(("fsdp", "tp")),
            P(("fsdp", "tp")),
            P(("fsdp", "tp")),
            P(("fsdp", "tp")),
            P(("fsdp", "tp")),
            P(("fsdp", "tp"), None),
            P(("fsdp", "tp"), None),
            P(("fsdp", "tp"), None),
            P(("fsdp", "tp"), None),
            P(("fsdp", "tp"), None),
            P(("fsdp", "tp"), None),
        ),
        out_specs=(
            P(("fsdp", "tp"), None),
            P(("fsdp", "tp"), None),
            P(("fsdp", "tp"), None),
            P(("fsdp", "tp"), None),
            P("fsdp", "tp"),
            P("fsdp", "tp"),
            P("fsdp", "tp"),
            P("tp", "fsdp"),
            P("fsdp", "tp"),
            P("tp", "fsdp"),
            P(("fsdp", "tp")),
            P(("fsdp", "tp")),
            P(("fsdp", "tp")),
            P(("fsdp", "tp")),
            P(("fsdp", "tp")),
            P(("fsdp", "tp")),
            P(("fsdp", "tp")),
            P(("fsdp", "tp")),
            P(("fsdp", "tp")),
            P(("fsdp", "tp")),
            P(("fsdp", "tp"), None),
            P(("fsdp", "tp"), None),
            P(("fsdp", "tp"), None),
        ),
        check_vma=False,
    )
```

```python
import functools
import math

import jax
import jax.numpy as jnp
from jax import lax
from jax.experimental import pallas as pl
from jax.experimental.pallas import tpu as pltpu
from jax.sharding import PartitionSpec as P

HD = 64
SEQ_LEN = 512


EPSILON = 1e-05
MASKED_SCORE = -1e30
ROPE_BASE = 10000.0


def rope_tables(places, head_width):
    half_width = head_width // 2
    inv_freq = jnp.exp(
        jnp.arange(half_width, dtype=jnp.float32) * (-2.0 * math.log(ROPE_BASE) / head_width)
    )
    angles = places.astype(jnp.float32)[:, None] * inv_freq[None, :]
    cos_table = jnp.cos(angles)
    sin_table = jnp.sin(angles)
    return (
        jnp.concatenate([cos_table, cos_table], axis=-1),
        jnp.concatenate([sin_table, sin_table], axis=-1),
    )


def product_tn(left_side, right_side):
    return lax.dot_general(
        left_side, right_side, (((0,), (0,)), ((), ())), preferred_element_type=jnp.float32
    )

ROUNDS = (
    {"x": (0, 0, 1), "z": (3, 0, 0), "y": (0, 1, 0)},
    {"x": (3, 0, 1), "y": (3, 1, 0), "z": (2, 0, 0)},
    {"z": (2, 1, 0), "x": (2, 0, 1), "y": (3, 1, 1)},
    {"y": (2, 1, 1), "x": (0, 1, 1), "z": (1, 0, 0)},
    {"x": (1, 0, 1), "y": (1, 1, 0), "z": (1, 1, 1)},
)
KEYS = tuple((z, y, x) for z in range(4) for y in range(2) for x in range(2))
OWN = (0, 0, 0)


def place(z, y, x):
    return (z * 2 + y) * 2 + x


def hop(link):
    def target(z, y, x):
        if link == "x":
            return place(z, y, 1 - x)
        if link == "y":
            return place(z, 1 - y, x)
        return place((z + 1) % 4, y, x)

    return [(place(*k), target(*k)) for k in KEYS]


HOPS = {link: hop(link) for link in "xyz"}
BACK = {link: [(b, a) for a, b in pairs] for link, pairs in HOPS.items()}


def sender_key(key, link):
    z, y, x = key
    if link == "x":
        return (z, y, 1 - x)
    if link == "y":
        return (z, 1 - y, x)
    return ((z + 1) % 4, y, x)


def gridded():
    return lax.axis_size("fsdp") == 16


def after(values, *others):
    return lax.optimization_barrier((values, others))[0]


class Gather:
    def __init__(self, shard):
        self.have = {OWN: shard}

    def step(self, number, *others):
        if not gridded():
            return ()
        step = ROUNDS[number]
        sends = {key: self.have[sender_key(key, link)] for link, key in step.items()}
        if others:
            sends = after(sends, *others)
        got = {key: lax.ppermute(sends[key], "fsdp", HOPS[link]) for link, key in step.items()}
        self.have.update(got)
        return list(got.values())

    def pieces(self):
        if not gridded():
            full = lax.all_gather(self.have[OWN], "fsdp", axis=0, tiled=True)
            rows = full.shape[0] // 16
            return [full[rows * i : rows * (i + 1)] for i in range(16)]
        return [self.have[key] for key in KEYS]


class Scatter:
    def __init__(self, pieces):
        self.held = dict(zip(KEYS, pieces))

    def step(self, number, *others):
        if not gridded():
            return ()
        step = ROUNDS[4 - number]
        sends = {key: self.held.pop(key) for key in step.values()}
        if others:
            sends = after(sends, *others)
        got = [
            (sender_key(key, link), lax.ppermute(sends[key], "fsdp", BACK[link]))
            for link, key in step.items()
        ]
        for key, part in got:
            self.held[key] = self.held[key] + part
        return [self.held[key] for key, _ in got]

    def rows(self):
        if not gridded():
            full = jnp.concatenate([self.held[key] for key in KEYS], axis=0)
            return lax.psum_scatter(full, "fsdp", scatter_dimension=0, tiled=True)
        return self.held[OWN]


def other_core(values):
    return lax.ppermute(values, "tp", [(0, 1), (1, 0)])


def reorder_kernel(inverse, place_ref, in_ref, out_ref):
    z, y, x = place_ref[0], place_ref[1], place_ref[2]
    turn = x == 1
    for block in range(8):
        zb, yb = block // 2, block % 2
        away = (zb + 4 - z) % 4 if inverse else (zb + z) % 4
        source = pl.multiple_of((away * 2 + (yb + y) % 2) * 128, 128)
        part = in_ref[:, pl.ds(source, 128)].astype(jnp.float32)
        part = jnp.where(turn, pltpu.roll(part, 64, 1), part)
        out_ref[:, block * 128 : block * 128 + 128] = part.astype(out_ref.dtype)


def grid_place():
    me = lax.axis_index("fsdp")
    return jnp.stack([me // 4, (me // 2) % 2, me % 2]).astype(jnp.int32)


def reorder(values, inverse):
    if not gridded():
        return values
    places = grid_place()
    return pl.pallas_call(
        functools.partial(reorder_kernel, inverse),
        out_shape=jax.ShapeDtypeStruct(values.shape, values.dtype),
        in_specs=[
            pl.BlockSpec(memory_space=pltpu.SMEM),
            pl.BlockSpec(memory_space=pltpu.VMEM),
        ],
        out_specs=pl.BlockSpec(memory_space=pltpu.VMEM),
    )(places, values)


def halves(values):
    first = lax.axis_index("tp") == 0
    other = other_core(values)
    return jnp.concatenate(
        [jnp.where(first, values, other), jnp.where(first, other, values)], axis=0
    )


def vmem_spec():
    return pl.BlockSpec(memory_space=pltpu.VMEM)


def any_spec():
    return pl.BlockSpec(memory_space=pl.ANY)


def call(body, outs, ins, specs, out_specs, scratch=(), grid=None, limit=60, flops=0, bytes_moved=0):
    extra = {} if grid is None else {"grid": grid}
    return pl.pallas_call(
        body,
        out_shape=outs,
        in_specs=specs,
        out_specs=out_specs,
        scratch_shapes=list(scratch),
        compiler_params=pltpu.CompilerParams(vmem_limit_bytes=limit * 1024 * 1024),
        cost_estimate=pl.CostEstimate(flops=flops, bytes_accessed=bytes_moved, transcendentals=0),
        **extra,
    )(*ins)


def shaped(shape, kind):
    return jax.ShapeDtypeStruct(shape, kind)


LOW, WIDE = jnp.bfloat16, jnp.float32


def dot(a, b):
    return jnp.dot(a, b, preferred_element_type=WIDE)


def dot_nt(a, b):
    return lax.dot_general(a, b, (((1,), (1,)), ((), ())), preferred_element_type=WIDE)


def dot_tn(a, b):
    return lax.dot_general(a, b, (((0,), (0,)), ((), ())), preferred_element_type=WIDE)


def fetch(pieces, columns, buffer, sems):
    rows = pieces[0].shape[0]
    copies = []
    for i, piece in enumerate(pieces):
        copy = pltpu.make_async_copy(
            piece.at[:, columns[0] : columns[1]], buffer.at[i * rows : (i + 1) * rows], sems.at[i]
        )
        copy.start()
        copies.append(copy)

    def ready(first, last):
        for copy in copies[first:last]:
            copy.wait()

    return ready


def pack_kernel(count, *refs):
    out_ref, at = refs[count], 0
    for ref in refs[:count]:
        size = ref.shape[1]
        out_ref[:, at : at + size] = ref[...].astype(LOW)
        at += size


def pack(arrays):
    rows = arrays[0].shape[0]
    total = sum(a.shape[1] for a in arrays)
    return call(
        functools.partial(pack_kernel, len(arrays)),
        shaped((rows, total), LOW),
        arrays,
        [vmem_spec() for _ in arrays],
        vmem_spec(),
        bytes_moved=rows * total * 6,
        limit=60,
    )


def flip(values):
    width = values.shape[1]
    lane = lax.broadcasted_iota(jnp.int32, values.shape, 1)
    return jnp.where(
        lane % HD < HD // 2, pltpu.roll(values, width - HD // 2, 1), pltpu.roll(values, HD // 2, 1)
    )


def tile_lanes(table, width):
    return jnp.concatenate([table] * (width // table.shape[1]), axis=1)


def qkv_kernel(x_ref, shift_ref, cos_ref, sin_ref, *refs):
    pieces, (q_ref, k_ref, v_ref, buffer, sems) = refs[:16], refs[16:]
    width = q_ref.shape[1]
    ready = fetch(pieces, (0, 3 * width), buffer, sems)
    ready(0, 16)
    chunk = min(256, width)
    cos_table, sin_table = tile_lanes(cos_ref[...], chunk), tile_lanes(sin_ref[...], chunk)
    for which, out_ref in enumerate((q_ref, k_ref, v_ref)):
        for at in range(0, width, chunk):
            first = which * width + at
            pre = dot(x_ref[...], buffer[:, first : first + chunk]) + shift_ref[:, first : first + chunk]
            if which < 2:
                pre = pre * cos_table + flip(pre) * sin_table
            if which == 0:
                pre = pre.astype(LOW).astype(WIDE) * (HD ** -0.5)
            out_ref[:, at : at + chunk] = pre.astype(LOW)


def project_qkv(x_all, shift, cos_table, sin_table, pieces, width):
    rows, depth = x_all.shape
    out = shaped((rows, width), LOW)
    return call(
        qkv_kernel,
        (out, out, out),
        (x_all, shift, cos_table, sin_table, *pieces),
        [vmem_spec()] * 4 + [any_spec()] * 16,
        (vmem_spec(),) * 3,
        [pltpu.VMEM((depth, 3 * width), LOW), pltpu.SemaphoreType.DMA((16,))],
        flops=2 * rows * depth * 3 * width,
        bytes_moved=2 * (3 * depth * width + rows * depth),
        limit=60,
    )


def attend_kernel(heads, q_ref, k_ref, v_ref, column_ref, row_ref, ctx_ref, prob_ref, mask_ref):
    rows = q_ref.shape[0]
    mask_ref[...] = jnp.where(column_ref[...] == row_ref[...], 0.0, MASKED_SCORE)
    flat = v_ref[...].astype(WIDE).T.astype(LOW)
    parts = []
    for head in range(heads):
        cols = slice(head * HD, head * HD + HD)
        scores = dot_nt(k_ref[:, cols], q_ref[:, cols]) + mask_ref[...]
        top = jnp.max(scores, axis=0, keepdims=True)
        raised = jnp.exp(scores - top)
        total = jnp.sum(raised, axis=0, keepdims=True)
        prob = (raised * (1.0 / total)).astype(LOW)
        prob_ref[head] = prob
        parts.append(dot(flat[cols], prob))
    ctx_ref[...] = jnp.concatenate(parts, axis=0).T.astype(LOW)


def attend(query, key, value, column, row, first, heads):
    rows = query.shape[0]
    width = heads * HD
    block = pl.BlockSpec((rows, width), lambda i: (0, first))
    whole = lambda shape: pl.BlockSpec(shape, lambda i: (0,) * len(shape))
    return call(
        functools.partial(attend_kernel, heads),
        (shaped((rows, width), LOW), shaped((heads, rows, rows), LOW)),
        (query, key, value, column, row),
        [block] * 3 + [whole((rows, 1)), whole((1, rows))],
        (whole((rows, width)), whole((heads, rows, rows))),
        [pltpu.VMEM((rows, rows), WIDE)],
        grid=(1,),
        flops=4 * heads * rows * rows * HD,
        bytes_moved=2 * heads * rows * rows,
        limit=60,
    )


def attend_back_kernel(heads, q_ref, k_ref, v_ref, g_ref, prob_ref, cos_ref, sin_ref, gq_ref, gk_ref, gv_ref, sums_ref):
    width = heads * HD
    key_flat = k_ref[...].astype(WIDE).T.astype(LOW)
    q_parts, k_parts, v_parts = [], [], []
    for head in range(heads):
        cols = slice(head * HD, head * HD + HD)
        prob = prob_ref[head]
        prob_wide = prob.astype(WIDE)
        grad = dot_nt(v_ref[:, cols], g_ref[:, cols])
        delta = jnp.sum(prob_wide * grad, axis=0, keepdims=True)
        raw = (prob_wide * (grad - delta)).astype(LOW)
        v_parts.append(dot(prob, g_ref[:, cols]))
        k_parts.append(dot(raw, q_ref[:, cols]))
        q_parts.append(dot(key_flat[cols], raw))
    cos_table, sin_table = tile_lanes(cos_ref[...], width), tile_lanes(sin_ref[...], width)
    gq = jnp.concatenate(q_parts, axis=0).T * (HD ** -0.5)
    gk = jnp.concatenate(k_parts, axis=1)
    gv = jnp.concatenate(v_parts, axis=1)
    gq = (gq * cos_table - flip(gq) * sin_table).astype(LOW)
    gk = (gk * cos_table - flip(gk) * sin_table).astype(LOW)
    gv = gv.astype(LOW)
    for i, (ref, value) in enumerate(((gq_ref, gq), (gk_ref, gk), (gv_ref, gv))):
        ref[...] = value
        sums_ref[i : i + 1, :] = jnp.sum(value.astype(WIDE), axis=0, keepdims=True)


def attend_back(query, key, value, grad_ctx, prob, cos_table, sin_table, first, heads):
    rows = query.shape[0]
    width = heads * HD
    block = pl.BlockSpec((rows, width), lambda i: (0, first))
    whole = lambda shape: pl.BlockSpec(shape, lambda i: (0,) * len(shape))
    out = shaped((rows, width), LOW)
    return call(
        functools.partial(attend_back_kernel, heads),
        (out, out, out, shaped((3, width), WIDE)),
        (query, key, value, grad_ctx, prob, cos_table, sin_table),
        [block] * 4 + [whole(prob.shape), whole(cos_table.shape), whole(sin_table.shape)],
        (whole((rows, width)),) * 3 + (whole((3, width)),),
        grid=(1,),
        flops=8 * heads * rows * rows * HD,
        bytes_moved=2 * heads * rows * rows,
        limit=60,
    )


def spread_kernel(count, first, width, *refs):
    lefts, pieces, (out_ref, buffer, sems) = refs[:count], refs[count : count + 16], refs[count + 16 :]
    ready = fetch(pieces, (first, first + width), buffer, sems)
    left = lefts[0][...] if count == 1 else jnp.concatenate([ref[...] for ref in lefts], axis=1)
    step = buffer.shape[0] // 4
    for i in range(4):
        ready(4 * i, 4 * i + 4)
        out_ref[:, i * step : i * step + step] = dot_nt(left, buffer[i * step : i * step + step]).astype(LOW)


def spread(lefts, pieces, first, width):
    rows = lefts[0].shape[0]
    depth = 16 * pieces[0].shape[0]
    return call(
        functools.partial(spread_kernel, len(lefts), first, width),
        shaped((rows, depth), LOW),
        (*lefts, *pieces),
        [vmem_spec()] * len(lefts) + [any_spec()] * 16,
        vmem_spec(),
        [pltpu.VMEM((depth, width), LOW), pltpu.SemaphoreType.DMA((16,))],
        flops=2 * rows * depth * width,
        bytes_moved=2 * (depth * width + rows * width + rows * depth),
        limit=60,
    )


def spec_rows(rows, width, turn=0, steps=4):
    if turn:
        return pl.BlockSpec((rows, width), lambda i: ((i + turn) % steps, 0))
    return pl.BlockSpec((rows, width), lambda i: (i, 0))


def spec_own(rows, width):
    return pl.BlockSpec((rows, width), lambda i: (jnp.minimum(i, 1), 0))


def spec_whole(shape):
    return pl.BlockSpec(shape, lambda i: (0,) * len(shape))


def row_stats(values):
    mean = jnp.mean(values, axis=1, keepdims=True)
    centered = values - mean
    inv = lax.rsqrt(jnp.mean(centered * centered, axis=1, keepdims=True) + EPSILON)
    return centered * inv, inv


def row_back(grad, unit, inv, gain):
    scaled = grad * gain
    return inv * (
        scaled
        - jnp.mean(scaled, axis=1, keepdims=True)
        - unit * jnp.mean(scaled * unit, axis=1, keepdims=True)
    )


def first_norm_kernel(x_ref, mine_ref, other_ref, vec_ref, unit_ref, inv_ref, low_ref):
    pre = x_ref[...].astype(WIDE) + (mine_ref[...].astype(WIDE) + other_ref[...].astype(WIDE)) + vec_ref[3:4, :]
    unit, inv = row_stats(pre)
    unit_ref[...] = unit
    inv_ref[...] = jnp.broadcast_to(inv, inv_ref.shape)
    low_ref[...] = (unit * vec_ref[5:6, :] + vec_ref[6:7, :]).astype(LOW)


def first_norm(x_all, mine, other, vectors):
    rows, width = x_all.shape
    step = rows // 4
    return call(
        first_norm_kernel,
        (shaped((rows, width), WIDE), shaped((rows, 128), WIDE), shaped((rows, width), LOW)),
        (x_all, mine, other, vectors),
        [spec_rows(step, width), spec_rows(step, width), spec_rows(step, width, 2), spec_whole(vectors.shape)],
        (spec_rows(step, width), spec_rows(step, 128), spec_rows(step, width)),
        grid=(4,),
        bytes_moved=12 * rows * width,
        limit=60,
    )


def up_kernel(first, mid_ref, shift_ref, *refs):
    pieces, (act_ref, slope_ref, buffer, sems) = refs[:16], refs[16:]
    width = act_ref.shape[1]
    ready = fetch(pieces, (first, first + width), buffer, sems)
    ready(0, 16)
    chunk = 256
    for at in range(0, width, chunk):
        u = dot(mid_ref[...], buffer[:, at : at + chunk]) + shift_ref[:, at : at + chunk]
        phi = 0.5 + 0.5 * lax.erf(u * (2.0 ** -0.5))
        act_ref[:, at : at + chunk] = (u * phi).astype(LOW)
        slope_ref[:, at : at + chunk] = (phi + u * (jnp.exp(-0.5 * u * u) * (2.0 * math.pi) ** -0.5)).astype(LOW)


def feed_up(mid_low, shift, pieces, first, width):
    rows, depth = mid_low.shape
    out = shaped((rows, width), LOW)
    return call(
        functools.partial(up_kernel, first),
        (out, out),
        (mid_low, shift, *pieces),
        [vmem_spec()] * 2 + [any_spec()] * 16,
        (vmem_spec(),) * 2,
        [pltpu.VMEM((depth, width), LOW), pltpu.SemaphoreType.DMA((16,))],
        flops=2 * rows * depth * width,
        bytes_moved=2 * (depth * width + rows * depth + 2 * rows * width),
        limit=60,
    )


def second_norm_kernel(first, unit1_ref, mine_ref, other_ref, vec_ref, cot_ref, *refs):
    pieces = refs[:16]
    wide_ref, mid_ref, narrow_ref, grad_ref, low_ref, top_ref, sums_ref, proj, sems = refs[16:]
    step = pl.program_id(0)
    cols = proj.shape[1]

    @pl.when(step == 0)
    def _():
        fetch(pieces, (first, first + cols), proj, sems)(0, 16)
        sums_ref[...] = jnp.zeros_like(sums_ref)

    pre = (
        unit1_ref[...] * vec_ref[5:6, :]
        + vec_ref[6:7, :]
        + (mine_ref[...].astype(WIDE) + other_ref[...].astype(WIDE))
        + vec_ref[4:5, :]
    )
    unit, inv = row_stats(pre)
    top = (unit * vec_ref[7:8, :] + vec_ref[8:9, :]).astype(LOW)
    top_ref[...] = top

    @pl.when(step < 2)
    def _():
        embed = dot(top, proj[...])
        wide_ref[...] = embed[:, : wide_ref.shape[1]]
        mid_ref[...] = embed[:, 128 : 128 + mid_ref.shape[1]]
        narrow_ref[...] = embed[:, 256 : 256 + narrow_ref.shape[1]]

    g_top = dot_nt(cot_ref[...], proj[...])
    g_sum = row_back(g_top, unit, inv, vec_ref[7:8, :])
    grad_ref[...] = g_sum
    low_ref[...] = g_sum.astype(LOW)
    sums_ref[0:1, :] += jnp.sum(g_sum, axis=0, keepdims=True)
    sums_ref[1:2, :] += jnp.sum(g_top * unit, axis=0, keepdims=True)
    sums_ref[2:3, :] += jnp.sum(g_top, axis=0, keepdims=True)


def second_norm(unit1, mine, other, vectors, cot_all, pieces, first, sizes):
    rows, width = unit1.shape
    step = rows // 4
    cols = cot_all.shape[1]
    return call(
        functools.partial(second_norm_kernel, first),
        tuple(shaped((rows // 2, n), WIDE) for n in sizes)
        + (shaped((rows, width), WIDE), shaped((rows, width), LOW), shaped((rows, width), LOW), shaped((8, width), WIDE)),
        (unit1, mine, other, vectors, cot_all, *pieces),
        [
            spec_rows(step, width),
            spec_rows(step, width),
            spec_rows(step, width, 2),
            spec_whole(vectors.shape),
            spec_rows(step, cols),
        ]
        + [any_spec()] * 16,
        tuple(spec_own(step, n) for n in sizes)
        + (spec_rows(step, width), spec_rows(step, width), spec_rows(step, width), spec_whole((8, width))),
        [pltpu.VMEM((width, cols), LOW), pltpu.SemaphoreType.DMA((16,))],
        grid=(4,),
        flops=4 * rows * width * cols,
        bytes_moved=16 * rows * width,
        limit=60,
    )


def hidden_back_kernel(first, g_ref, slope_ref, *refs):
    pieces, (out_ref, sums_ref, buffer, sems) = refs[:16], refs[16:]
    width = out_ref.shape[1]
    ready = fetch(pieces, (first, first + width), buffer, sems)
    ready(0, 16)
    chunk = 256
    for at in range(0, width, chunk):
        g = dot(g_ref[...], buffer[:, at : at + chunk]) * slope_ref[:, at : at + chunk].astype(WIDE)
        g = g.astype(LOW)
        out_ref[:, at : at + chunk] = g
        sums_ref[:, at : at + chunk] = jnp.sum(g.astype(WIDE), axis=0, keepdims=True)


def hidden_back(grad_low, slope, pieces, first):
    rows, depth = grad_low.shape
    width = slope.shape[1]
    return call(
        functools.partial(hidden_back_kernel, first),
        (shaped((rows, width), LOW), shaped((1, width), WIDE)),
        (grad_low, slope, *pieces),
        [vmem_spec()] * 2 + [any_spec()] * 16,
        (vmem_spec(),) * 2,
        [pltpu.VMEM((depth, width), LOW), pltpu.SemaphoreType.DMA((16,))],
        flops=2 * rows * depth * width,
        bytes_moved=2 * (depth * width + rows * depth + 2 * rows * width),
        limit=60,
    )


def context_back_kernel(first, g_ref, *refs):
    pieces, (out_ref, buffer, sems) = refs[:16], refs[16:]
    width = out_ref.shape[1]
    fetch(pieces, (first, first + width), buffer, sems)(0, 16)
    out_ref[...] = dot(g_ref[...], buffer[...]).astype(LOW)


def context_back(grad_low, pieces, first, width):
    rows, depth = grad_low.shape
    return call(
        functools.partial(context_back_kernel, first),
        shaped((rows, width), LOW),
        (grad_low, *pieces),
        [vmem_spec()] + [any_spec()] * 16,
        vmem_spec(),
        [pltpu.VMEM((depth, width), LOW), pltpu.SemaphoreType.DMA((16,))],
        flops=2 * rows * depth * width,
        bytes_moved=2 * (depth * width + rows * depth + rows * width),
        limit=60,
    )


def fold_kernel(pairs, extra, *refs):
    at = 0
    groups = []
    for n in pairs:
        groups.append((refs[at], refs[at + 1 : at + 1 + n]))
        at += 1 + n
    add_ref = None
    if extra:
        add_ref = refs[at]
        at += 1
    outs, (buffer, sems) = refs[at : at + 16], refs[at + 16 :]
    rows = outs[0].shape[0]
    copies = []
    for i in range(4):
        block = slice(4 * rows * i, 4 * rows * (i + 1))
        column = 0
        for left_ref, rights in groups:
            for right_ref in rights:
                size = right_ref.shape[1]
                for part in range(0, size, 512):
                    end = min(part + 512, size)
                    value = dot_tn(left_ref[:, block], right_ref[:, part:end])
                    if extra and right_ref is groups[-1][1][-1]:
                        value = value + add_ref[block].astype(WIDE)
                    buffer[block, column + part : column + end] = value.astype(LOW)
                column += size
        for k in range(4 * i, 4 * i + 4):
            copy = pltpu.make_async_copy(buffer.at[k * rows : (k + 1) * rows], outs[k], sems.at[k])
            copy.start()
            copies.append(copy)
    for copy in copies:
        copy.wait()


def fold(groups, extra=None):
    left = groups[0][0]
    rows, depth = left.shape
    ins = [a for l, rs in groups for a in (l, *rs)]
    width = sum(r.shape[1] for _, rs in groups for r in rs)
    total = width
    if extra is not None:
        ins.append(extra)
    piece = shaped((depth // 16, total), LOW)
    return call(
        functools.partial(fold_kernel, tuple(len(rs) for _, rs in groups), extra is not None),
        (piece,) * 16,
        ins,
        [vmem_spec()] * len(ins),
        (any_spec(),) * 16,
        [pltpu.VMEM((depth, total), LOW), pltpu.SemaphoreType.DMA((16,))],
        flops=2 * rows * depth * width,
        bytes_moved=2 * (depth * total + rows * width + rows * depth),
        limit=60,
    )


def middle_back_kernel(g_ref, mine_ref, other_ref, unit_ref, inv_ref, vec_ref, own_ref, low_ref, sums_ref):
    step = pl.program_id(0)

    @pl.when(step == 0)
    def _():
        sums_ref[...] = jnp.zeros_like(sums_ref)

    unit = unit_ref[...]
    g_mid = g_ref[...] + (mine_ref[...].astype(WIDE) + other_ref[...].astype(WIDE))
    g_pre = row_back(g_mid, unit, inv_ref[:, :1], vec_ref[5:6, :])

    @pl.when(step < 2)
    def _():
        own_ref[...] = g_pre

    low_ref[...] = g_pre.astype(LOW)
    sums_ref[0:1, :] += jnp.sum(g_pre, axis=0, keepdims=True)
    sums_ref[1:2, :] += jnp.sum(g_mid * unit, axis=0, keepdims=True)
    sums_ref[2:3, :] += jnp.sum(g_mid, axis=0, keepdims=True)


def middle_back(grad, mine, other, unit, inv, vectors):
    rows, width = grad.shape
    step = rows // 4
    return call(
        middle_back_kernel,
        (shaped((rows // 2, width), WIDE), shaped((rows, width), LOW), shaped((8, width), WIDE)),
        (grad, mine, other, unit, inv, vectors),
        [
            spec_rows(step, width),
            spec_rows(step, width),
            spec_rows(step, width, 2),
            spec_rows(step, width),
            spec_rows(step, 128),
            spec_whole(vectors.shape),
        ],
        (spec_own(step, width), spec_rows(step, width), spec_whole((8, width))),
        grid=(4,),
        bytes_moved=14 * rows * width,
        limit=60,
    )


def finish_kernel(place_ref, g_ref, mine_ref, other_ref, out_ref):
    z, y, x = place_ref[0], place_ref[1], place_ref[2]
    turn = x == 1
    for block in range(8):
        zb, yb = block // 2, block % 2
        source = pl.multiple_of((((zb + 4 - z) % 4) * 2 + (yb + y) % 2) * 128, 128)
        cols = pl.ds(source, 128)
        part = g_ref[:, cols] + mine_ref[:, cols].astype(WIDE) + other_ref[:, cols].astype(WIDE)
        out_ref[:, block * 128 : block * 128 + 128] = jnp.where(turn, pltpu.roll(part, 64, 1), part)


def finish(grad, mine, other):
    if not gridded():
        return grad + mine.astype(WIDE) + other.astype(WIDE)
    rows, width = grad.shape
    return call(
        finish_kernel,
        shaped((rows, width), WIDE),
        (grid_place(), grad, mine, other),
        [pl.BlockSpec(memory_space=pltpu.SMEM)] + [vmem_spec()] * 3,
        vmem_spec(),
        bytes_moved=12 * rows * width,
        limit=60,
    )


def small_kernel(*refs):
    vectors, heads, (out_ref, rows_ref) = refs[:10], refs[10:13], refs[13:]
    rows_ref[...] = jnp.zeros_like(rows_ref)
    for i, ref in enumerate(vectors):
        rows_ref[i : i + 1, : ref.shape[1]] = ref[...]
    out_ref[...] = jnp.zeros_like(out_ref)
    out_ref[:16, :128] = rows_ref[...].astype(LOW)
    for i, ref in enumerate(heads):
        out_ref[16 : 16 + ref.shape[0], 128 * i : 128 * i + ref.shape[1]] = ref[...].astype(LOW)


def small_pack(vectors, heads):
    piece = heads[0].shape[0]
    ins = [v.reshape(1, -1) for v in vectors] + list(heads)
    return call(
        small_kernel,
        shaped((16 + piece, 384), LOW),
        ins,
        [vmem_spec()] * len(ins),
        vmem_spec(),
        [pltpu.VMEM((16, 128), WIDE)],
        bytes_moved=100000,
        limit=60,
    )


def pack_rows_kernel(spot_ref, q_ref, k_ref, v_ref, mine_ref, other_ref, out_ref):
    first = spot_ref[3] == 0
    width = q_ref.shape[1]
    for i, ref in enumerate((q_ref, k_ref, v_ref)):
        out_ref[:, i * width : i * width + width] = ref[...].astype(LOW)
    piece = out_ref.shape[0] // 2
    mine, other = mine_ref[:16, :128].astype(WIDE), other_ref[:16, :128].astype(WIDE)
    zero, one = jnp.where(first, mine, other), jnp.where(first, other, mine)
    lane = lax.broadcasted_iota(jnp.int32, zero.shape, 1)
    row = lax.broadcasted_iota(jnp.int32, zero.shape, 0)
    both = jnp.where(lane < piece, zero, pltpu.roll(one, piece, 1))
    both = jnp.where(row == 9, zero, jnp.where(row == 10, pltpu.roll(one, 1, 0), both))
    out_ref[:16, 3 * width :] = both.astype(LOW)
    out_ref[16:, 3 * width :] = jnp.zeros((2 * piece - 16, 128), LOW)


def pack_rows(spot, weights, mine, other):
    rows, width = weights[0].shape
    return call(
        pack_rows_kernel,
        shaped((rows, 3 * width + 128), LOW),
        (spot, *weights, mine, other),
        [pl.BlockSpec(memory_space=pltpu.SMEM)] + [vmem_spec()] * 5,
        vmem_spec(),
        bytes_moved=18 * rows * width,
        limit=60,
    )


def pack_heads_kernel(spot_ref, weight_ref, mine_ref, other_ref, out_ref):
    first = spot_ref[3] == 0
    width = weight_ref.shape[1]
    piece = out_ref.shape[0] // 2
    out_ref[:, :width] = weight_ref[...].astype(LOW)
    mine, other = mine_ref[16:], other_ref[16:]
    out_ref[:piece, width:] = jnp.where(first, mine, other)
    out_ref[piece:, width:] = jnp.where(first, other, mine)


def pack_heads(spot, weight, mine, other):
    rows, width = weight.shape
    return call(
        pack_heads_kernel,
        shaped((rows, width + 384), LOW),
        (spot, weight, mine, other),
        [pl.BlockSpec(memory_space=pltpu.SMEM)] + [vmem_spec()] * 3,
        vmem_spec(),
        bytes_moved=6 * rows * width,
        limit=60,
    )


def vectors_kernel(first, spot_ref, *refs):
    pieces, (vec_ref, qkv_ref, up_ref, low_buffer, rows_ref, sems) = refs[:16], refs[16:]
    z, y, x, core = spot_ref[0], spot_ref[1], spot_ref[2], spot_ref[3]
    copies = []
    for i, piece in enumerate(pieces):
        copy = pltpu.make_async_copy(
            piece.at[0:16, first : first + 128], low_buffer.at[16 * i : 16 * i + 16], sems.at[i]
        )
        copy.start()
        copies.append(copy)
    for copy in copies:
        copy.wait()
    rows_ref[...] = low_buffer[...].astype(WIDE)
    lane = lax.broadcasted_iota(jnp.int32, (16, 128), 1)
    for j in range(8):
        even, odd = rows_ref[32 * j : 32 * j + 16], rows_ref[32 * j + 16 : 32 * j + 32]
        vec_ref[:, 128 * j : 128 * j + 128] = jnp.where(lane < 64, even, pltpu.roll(odd, 64, 1))
    turn = x == 1
    blocks = qkv_ref.shape[1] // 384
    for b in range(blocks):
        source = ((core * 2 + b // 2 + 4 - z) % 4) * 2 + (b % 2 + y) % 2
        part = vec_ref[:, pl.ds(pl.multiple_of(source * 128, 128), 128)]
        part = jnp.where(turn, pltpu.roll(part, 64, 1), part)
        for j in range(3):
            at = (j * blocks + b) * 128
            qkv_ref[:, at : at + 128] = part[j : j + 1]
    for j in range(8):
        key = (((core * 2 + j // 4 + 4 - z) % 4) * 2 + (j // 2 % 2 + y) % 2) * 2 + (j % 2 + x) % 2
        for t in range(2):
            at = j * 256 + t * 128
            up_ref[:, at : at + 128] = rows_ref[pl.ds(key * 16 + 9 + t, 1), :]


def read_vectors(spot, pieces, first, width, head_width, hidden):
    return call(
        functools.partial(vectors_kernel, first),
        (shaped((16, width), WIDE), shaped((1, 3 * head_width), WIDE), shaped((1, hidden), WIDE)),
        (spot, *pieces),
        [pl.BlockSpec(memory_space=pltpu.SMEM)] + [any_spec()] * 16,
        (vmem_spec(),) * 3,
        [pltpu.VMEM((256, 128), LOW), pltpu.VMEM((256, 128), WIDE), pltpu.SemaphoreType.DMA((16,))],
        bytes_moved=200000,
        limit=60,
    )


def sums_kernel(zero_ref, one_ref, up_ref, out_ref, rows_ref):
    rows_ref[...] = jnp.zeros_like(rows_ref)
    half = zero_ref.shape[1]
    rows_ref[0:3, :half] = zero_ref[...]
    rows_ref[0:3, half : 2 * half] = one_ref[...]
    rows_ref[3:4, :] = up_ref[...]
    out_ref[...] = rows_ref[...].astype(LOW)


def pack_sums(zero, one, up):
    width = up.shape[1]
    return call(
        sums_kernel,
        shaped((16, width), LOW),
        (zero, one, up),
        [vmem_spec()] * 3,
        vmem_spec(),
        [pltpu.VMEM((16, width), WIDE)],
        bytes_moved=100000,
        limit=60,
    )


def vector_grads_kernel(share, spot_ref, mine_ref, other_ref, mid_ref, top_ref, out_ref, plain, long, block):
    z, y, x, core = spot_ref[0], spot_ref[1], spot_ref[2], spot_ref[3]
    turn = x == 1
    half = plain.shape[1] // 2
    hidden = mine_ref.shape[1]
    mine, other = mine_ref[...].astype(WIDE), other_ref[...].astype(WIDE)
    for i in range(2):
        side = jnp.where(core == i, mine, other)
        plain[:, i * half : i * half + half] = side[:8, :half]
        long[:, i * hidden : i * hidden + hidden] = side[3:4]
    out_ref[...] = jnp.zeros_like(out_ref)
    for j in range(8):
        source = ((j // 2 + z) % 4) * 2 + (j % 2 + y) % 2
        part = plain[:, pl.ds(pl.multiple_of(source * 128, 128), 128)]
        part = jnp.where(turn, pltpu.roll(part, 64, 1), part)
        cols = slice(128 * j, 128 * j + 128)
        block[0:3, :] = part[0:3]
        block[3:4, :] = mid_ref[0:1, cols]
        block[4:5, :] = top_ref[0:1, cols]
        block[5:7, :] = mid_ref[1:3, cols]
        block[7:9, :] = top_ref[1:3, cols]
        block[9:16, :] = jnp.zeros((7, 128), WIDE)
        pair = block[...]
        for odd in range(2):
            owner = source * 2 + (odd + x) % 2
            block[...] = pltpu.roll(pair, 64, 1) if odd else pair
            for t in range(2):
                wide_row = long[:, pl.ds(pl.multiple_of(owner * 256 + t * 128, 128), 128)]
                block[9 + 2 * t : 10 + 2 * t, :] = wide_row
                block[10 + 2 * t : 11 + 2 * t, :] = pltpu.roll(wide_row, 64, 1)
            at = (2 * j + odd) * 64
            out_ref[at : at + 16, share - 64 : share] = jnp.where(core == 1, block[:, :64], 0.0).astype(LOW)


def spread_vector_grads(spot, mine, other, mid_sums, top_sums, share):
    width = mid_sums.shape[1]
    hidden = mine.shape[1]
    return call(
        functools.partial(vector_grads_kernel, share),
        shaped((width, share), LOW),
        (spot, mine, other, mid_sums, top_sums),
        [pl.BlockSpec(memory_space=pltpu.SMEM)] + [vmem_spec()] * 4,
        vmem_spec(),
        [pltpu.VMEM((8, width), WIDE), pltpu.VMEM((1, 2 * hidden), WIDE), pltpu.VMEM((16, 128), WIDE)],
        bytes_moved=400000,
        limit=60,
    )


def local(
    hidden_in,
    segment_ids,
    positions,
    query_weight,
    key_weight,
    value_weight,
    output_weight,
    up_weight,
    down_weight,
    query_bias,
    key_bias,
    value_bias,
    output_bias,
    up_bias,
    down_bias,
    attn_gain,
    attn_shift,
    ffn_gain,
    ffn_shift,
    proj_wide,
    proj_mid,
    proj_narrow,
    cot_wide,
    cot_mid,
    cot_narrow,
):
    tp_rank = lax.axis_index("tp")
    own_rows, width = hidden_in.shape
    head_width = query_weight.shape[1]
    heads_here = head_width // HD
    hidden_here = up_weight.shape[1]
    piece = query_bias.shape[0]
    low, wide = LOW, WIDE
    half = head_width // 2
    half_heads = heads_here // 2

    spot = jnp.concatenate([grid_place(), tp_rank[None].astype(jnp.int32)])
    first_core = tp_rank == 0

    up_group = Gather(pack([output_weight.T, up_weight]))
    up_steps = [up_group.step(0)]
    small = small_pack(
        (
            query_bias, key_bias, value_bias, output_bias, down_bias,
            attn_gain, attn_shift, ffn_gain, ffn_shift, up_bias,
        ),
        (proj_wide, proj_mid, proj_narrow),
    )
    small_other = other_core(small)
    qkv_weights = (query_weight, key_weight, value_weight)
    if gridded():
        qkv_group = Gather(pack_rows(spot, qkv_weights, small, small_other))
        down_group = Gather(pack_heads(spot, down_weight.T, small, small_other))
    else:
        small_zero = jnp.where(first_core, small, small_other)
        small_one = jnp.where(first_core, small_other, small)
        qkv_group = Gather(pack([*qkv_weights, jnp.zeros((2 * piece, 128), low)]))
        heads_pair = jnp.concatenate([small_zero[16:], small_one[16:]], axis=0)
        down_group = Gather(pack([down_weight.T, heads_pair]))
    own_qkv = qkv_group.have[OWN]
    qkv_steps = [qkv_group.step(0), qkv_group.step(1)]
    up_steps.append(up_group.step(1, own_qkv))
    qkv_steps.append(qkv_group.step(2, up_steps[0]))
    qkv_steps.append(qkv_group.step(3))
    up_steps.append(up_group.step(2))
    qkv_steps.append(qkv_group.step(4, up_steps[1]))
    up_steps += [up_group.step(3), up_group.step(4)]
    down_steps = [down_group.step(i) for i in range(5)]
    qkv_pieces = qkv_group.pieces()
    up_pieces = up_group.pieces()
    down_pieces = down_group.pieces()
    if gridded():
        vectors, qkv_shift, up_shift = read_vectors(
            spot, qkv_pieces, 3 * head_width, width, head_width, hidden_here
        )
    else:
        pair = jnp.stack([small_zero[:16, :128], small_one[:16, :128]])
        pair = lax.all_gather(pair[None], "fsdp", axis=0, tiled=True).astype(wide)
        vectors = pair[..., :piece].transpose(2, 0, 1, 3).reshape(16, width)
        qkv_shift = lax.dynamic_slice_in_dim(vectors[:3], tp_rank * head_width, head_width, 1).reshape(1, -1)
        up_shift = lax.dynamic_slice_in_dim(
            pair[:, :, 9, : 4 * piece].reshape(1, -1), tp_rank * hidden_here, hidden_here, 1
        )

    tags = jnp.stack([segment_ids, positions])
    tags = jnp.concatenate([tags, other_core(tags)], axis=1)
    x_all = reorder(jnp.concatenate([hidden_in, other_core(hidden_in)], axis=0), False)
    cot_own = jnp.concatenate(
        [cot_wide, jnp.pad(cot_mid, ((0, 0), (0, 128 - cot_mid.shape[1]))), jnp.pad(cot_narrow, ((0, 0), (0, 128 - cot_narrow.shape[1])))],
        axis=1,
    )
    cot_all = jnp.concatenate([cot_own, other_core(cot_own)], axis=0)
    column, row = tags[0].reshape(-1, 1), tags[0].reshape(1, -1)
    cos_table, sin_table = rope_tables(tags[1], HD)
    cos_table = jnp.concatenate([cos_table, cos_table], axis=1)
    sin_table = jnp.concatenate([-sin_table[:, : HD // 2], sin_table[:, HD // 2 :]] * 2, axis=1)

    query, key, value = project_qkv(after(x_all, up_steps[2]), qkv_shift, cos_table, sin_table, qkv_pieces, head_width)
    contexts, probs = zip(
        attend(after(query, up_steps[3]), key, value, column, row, 0, half_heads),
        attend(after(query, down_steps[0]), key, value, column, row, 1, half_heads),
    )
    attn_mine = spread(contexts, up_pieces, 0, head_width)
    unit_one, inv_one, mid_low = first_norm(
        after(x_all, down_steps[1]), attn_mine, other_core(attn_mine), vectors
    )
    act_low, slope = feed_up(after(mid_low, down_steps[2]), up_shift, up_pieces, head_width, hidden_here)
    ffn_mine = spread((act_low,), down_pieces, 0, hidden_here)
    embed_wide, embed_mid, embed_narrow, grad_top, grad_top_low, top_low, top_sums = second_norm(
        unit_one, ffn_mine, other_core(ffn_mine), vectors, cot_all, down_pieces, hidden_here,
        (proj_wide.shape[1], proj_mid.shape[1], proj_narrow.shape[1]),
    )

    share = 192
    cot_share = lax.dynamic_slice_in_dim(cot_all, tp_rank * share, share, 1)
    grad_hidden_low, up_sums = hidden_back(grad_top_low, slope, down_pieces, 0)
    ffn_scatter = Scatter(fold([(grad_top_low, [act_low]), (mid_low, [grad_hidden_low])]))
    ffn_steps = [ffn_scatter.step(i) for i in range(5)]
    mid_mine = spread((grad_hidden_low,), up_pieces, head_width, hidden_here)
    grad_own, grad_mid_low, mid_sums = middle_back(
        grad_top, mid_mine, other_core(mid_mine), unit_one, inv_one, vectors
    )
    grad_context = context_back(grad_mid_low, up_pieces, 0, head_width)
    backs = [
        attend_back(
            query, key, value, after(grad_context, ffn_steps[0]), probs[i], cos_table, sin_table, i, half_heads
        )
        for i in range(2)
    ]
    grads = [backs[i][j] for j in range(3) for i in range(2)]
    sums = pack_sums(backs[0][3], backs[1][3], up_sums)
    sums_other = other_core(sums)
    if gridded():
        extra = spread_vector_grads(spot, sums, sums_other, mid_sums, top_sums, share)
    else:
        extra = jnp.zeros((width, share), low)
    attn_scatter = Scatter(
        fold([(after(x_all, ffn_steps[1]), grads), (grad_mid_low, list(contexts)), (top_low, [cot_share])], extra)
    )
    x_mine = spread([after(grads[0], ffn_steps[2])] + grads[1:], qkv_pieces, 0, 3 * head_width)
    x_other = other_core(x_mine[own_rows:])
    grad_hidden = finish(grad_own, x_mine[:own_rows], x_other)
    attn_steps = [attn_scatter.step(i) for i in range(5)]
    ffn_part = ffn_scatter.rows()
    attn_part = attn_scatter.rows()

    small_part = attn_part[:, 4 * head_width :]
    small_away = other_core(small_part)
    joined = jnp.where(
        first_core,
        jnp.concatenate([small_part, small_away], axis=1),
        jnp.concatenate([small_away, small_part], axis=1),
    ).astype(wide)
    own_heads = lax.dynamic_slice_in_dim(joined, tp_rank * piece, piece, 0)
    if gridded():
        block = joined[:16, 2 * share - 64 :]
        own_vectors = lax.dynamic_slice_in_dim(block[:9], tp_rank * piece, piece, 1)
        own_up = lax.dynamic_slice_in_dim(block, 9 + 2 * tp_rank, 2, 0).reshape(-1)
    else:
        both = jnp.concatenate(
            [
                jnp.where(first_core, sums, sums_other)[:3, :head_width],
                jnp.where(first_core, sums_other, sums)[:3, :head_width],
            ],
            axis=1,
        ).astype(wide)
        table = jnp.concatenate(
            [both, mid_sums[:1], top_sums[:1], mid_sums[1:3], top_sums[1:3], jnp.zeros((7, width), wide)], axis=0
        )
        table = lax.psum_scatter(table, "fsdp", scatter_dimension=1, tiled=True)
        own_vectors = lax.dynamic_slice_in_dim(table, tp_rank * piece, piece, 1)
        long = lax.dynamic_update_slice_in_dim(
            jnp.zeros((2 * hidden_here,), wide), up_sums.reshape(-1), tp_rank * hidden_here, 0
        )
        own_up = lax.psum_scatter(long, ("fsdp", "tp"), scatter_dimension=0, tiled=True)
    attn_part = attn_part.astype(wide)
    return (
        embed_wide,
        embed_mid,
        embed_narrow,
        grad_hidden,
        attn_part[:, :head_width],
        attn_part[:, head_width : 2 * head_width],
        attn_part[:, 2 * head_width : 3 * head_width],
        attn_part[:, 3 * head_width : 4 * head_width].T,
        ffn_part[:, hidden_here:].astype(wide),
        ffn_part[:, :hidden_here].astype(wide).T,
        own_vectors[0],
        own_vectors[1],
        own_vectors[2],
        own_vectors[3],
        own_up,
        own_vectors[4],
        own_vectors[5],
        own_vectors[6],
        own_vectors[7],
        own_vectors[8],
        own_heads[:, : proj_wide.shape[1]],
        own_heads[:, 128 : 128 + proj_mid.shape[1]],
        own_heads[:, 256 : 256 + proj_narrow.shape[1]],
    )


def solution(mesh):
    return jax.shard_map(
        local,
        mesh=mesh,
        in_specs=(
            P(("fsdp", "tp"), None),
            P(("fsdp", "tp")),
            P(("fsdp", "tp")),
            P("fsdp", "tp"),
            P("fsdp", "tp"),
            P("fsdp", "tp"),
            P("tp", "fsdp"),
            P("fsdp", "tp"),
            P("tp", "fsdp"),
            P(("fsdp", "tp")),
            P(("fsdp", "tp")),
            P(("fsdp", "tp")),
            P(("fsdp", "tp")),
            P(("fsdp", "tp")),
            P(("fsdp", "tp")),
            P(("fsdp", "tp")),
            P(("fsdp", "tp")),
            P(("fsdp", "tp")),
            P(("fsdp", "tp")),
            P(("fsdp", "tp"), None),
            P(("fsdp", "tp"), None),
            P(("fsdp", "tp"), None),
            P(("fsdp", "tp"), None),
            P(("fsdp", "tp"), None),
            P(("fsdp", "tp"), None),
        ),
        out_specs=(
            P(("fsdp", "tp"), None),
            P(("fsdp", "tp"), None),
            P(("fsdp", "tp"), None),
            P(("fsdp", "tp"), None),
            P("fsdp", "tp"),
            P("fsdp", "tp"),
            P("fsdp", "tp"),
            P("tp", "fsdp"),
            P("fsdp", "tp"),
            P("tp", "fsdp"),
            P(("fsdp", "tp")),
            P(("fsdp", "tp")),
            P(("fsdp", "tp")),
            P(("fsdp", "tp")),
            P(("fsdp", "tp")),
            P(("fsdp", "tp")),
            P(("fsdp", "tp")),
            P(("fsdp", "tp")),
            P(("fsdp", "tp")),
            P(("fsdp", "tp")),
            P(("fsdp", "tp"), None),
            P(("fsdp", "tp"), None),
            P(("fsdp", "tp"), None),
        ),
        check_vma=False,
    )
```

```python
import functools
import math

import jax
import jax.numpy as jnp
from jax import lax
from jax.experimental import pallas as pl
from jax.experimental.pallas import tpu as pltpu
from jax.sharding import PartitionSpec as P

HD = 64
SEQ_LEN = 512


EPSILON = 1e-05
MASKED_SCORE = -1e30
ROPE_BASE = 10000.0


def rope_tables(places, head_width):
    half_width = head_width // 2
    inv_freq = jnp.exp(
        jnp.arange(half_width, dtype=jnp.float32) * (-2.0 * math.log(ROPE_BASE) / head_width)
    )
    angles = places.astype(jnp.float32)[:, None] * inv_freq[None, :]
    cos_table = jnp.cos(angles)
    sin_table = jnp.sin(angles)
    return (
        jnp.concatenate([cos_table, cos_table], axis=-1),
        jnp.concatenate([sin_table, sin_table], axis=-1),
    )


def product_tn(left_side, right_side):
    return lax.dot_general(
        left_side, right_side, (((0,), (0,)), ((), ())), preferred_element_type=jnp.float32
    )

GATHERED = (
    ("z", (3, 0, 0)), ("x", (0, 0, 1)), ("y", (0, 1, 0)),
    ("z", (2, 0, 0)), ("x", (3, 0, 1)), ("y", (3, 1, 0)),
    ("z", (1, 0, 0)), ("x", (2, 0, 1)), ("y", (3, 1, 1)),
    ("z", (2, 1, 0)), ("x", (0, 1, 1)), ("y", (2, 1, 1)),
    ("x", (1, 0, 1)), ("y", (1, 1, 0)), ("z", (1, 1, 1)),
)
SCATTERED = (
    ("z", (1, 1, 1)), ("x", (1, 0, 1)), ("y", (1, 1, 0)), ("x", (0, 1, 1)),
    ("z", (2, 1, 0)), ("y", (2, 1, 1)), ("z", (1, 0, 0)), ("y", (3, 1, 1)),
    ("x", (2, 0, 1)), ("y", (3, 1, 0)), ("x", (3, 0, 1)), ("z", (2, 0, 0)),
    ("x", (0, 0, 1)), ("y", (0, 1, 0)), ("z", (3, 0, 0)),
)
KEYS = tuple((z, y, x) for z in range(4) for y in range(2) for x in range(2))
OWN = (0, 0, 0)


def place(z, y, x):
    return (z * 2 + y) * 2 + x


def hop(link):
    def target(z, y, x):
        if link == "x":
            return place(z, y, 1 - x)
        if link == "y":
            return place(z, 1 - y, x)
        return place((z + 1) % 4, y, x)

    return [(place(*k), target(*k)) for k in KEYS]


HOPS = {link: hop(link) for link in "xyz"}
BACK = {link: [(b, a) for a, b in pairs] for link, pairs in HOPS.items()}


def sender_key(key, link):
    z, y, x = key
    if link == "x":
        return (z, y, 1 - x)
    if link == "y":
        return (z, 1 - y, x)
    return ((z + 1) % 4, y, x)


def gridded():
    return lax.axis_size("fsdp") == 16


def after(values, *others):
    return lax.optimization_barrier((values, others))[0] if others else values


class Gather:
    def __init__(self, shard):
        self.have = {OWN: shard}

    def start(self, number, *others):
        link, key = GATHERED[number]
        send = self.have[sender_key(key, link)]
        if others:
            send = after(send, *others)
        self.have[key] = lax.ppermute(send, "fsdp", HOPS[link])
        return self.have[key]

    def pieces(self):
        if not gridded():
            full = lax.all_gather(self.have[OWN], "fsdp", axis=0, tiled=True)
            rows = full.shape[0] // 16
            return [full[rows * i : rows * (i + 1)] for i in range(16)]
        return [self.have[key] for key in KEYS]


class Scatter:
    def __init__(self, pieces):
        self.held = dict(zip(KEYS, pieces))
        self.parts = {key: [] for key in KEYS}

    def total(self, key, *others):
        return sum(after(self.parts[key], *others), after(self.held[key], *others))

    def start(self, number, *others):
        link, key = SCATTERED[number]
        part = lax.ppermute(self.total(key, *others), "fsdp", BACK[link])
        self.parts[sender_key(key, link)].append(part)
        return part

    def rows(self):
        if not gridded():
            full = jnp.concatenate([self.held[key] for key in KEYS], axis=0)
            return lax.psum_scatter(full, "fsdp", scatter_dimension=0, tiled=True)
        return self.total(OWN)


class Queue:
    def __init__(self):
        self.landed = []

    def add(self, group, numbers, *others, places=0):
        if gridded():
            for number in numbers:
                tied = self.landed[-places : len(self.landed) - places + 1] if places else []
                self.landed.append(group.start(number, *others, *tied))

    def at(self, *indices):
        return [self.landed[i] for i in indices if gridded()]


def other_core(values):
    return lax.ppermute(values, "tp", [(0, 1), (1, 0)])


def reorder_kernel(inverse, place_ref, in_ref, out_ref):
    z, y, x = place_ref[0], place_ref[1], place_ref[2]
    turn = x == 1
    for block in range(8):
        zb, yb = block // 2, block % 2
        away = (zb + 4 - z) % 4 if inverse else (zb + z) % 4
        source = pl.multiple_of((away * 2 + (yb + y) % 2) * 128, 128)
        part = in_ref[:, pl.ds(source, 128)].astype(jnp.float32)
        part = jnp.where(turn, pltpu.roll(part, 64, 1), part)
        out_ref[:, block * 128 : block * 128 + 128] = part.astype(out_ref.dtype)


def grid_place():
    me = lax.axis_index("fsdp")
    return jnp.stack([me // 4, (me // 2) % 2, me % 2]).astype(jnp.int32)


def reorder(values, inverse):
    if not gridded():
        return values
    places = grid_place()
    return pl.pallas_call(
        functools.partial(reorder_kernel, inverse),
        out_shape=jax.ShapeDtypeStruct(values.shape, values.dtype),
        in_specs=[
            pl.BlockSpec(memory_space=pltpu.SMEM),
            pl.BlockSpec(memory_space=pltpu.VMEM),
        ],
        out_specs=pl.BlockSpec(memory_space=pltpu.VMEM),
    )(places, values)


def halves(values):
    first = lax.axis_index("tp") == 0
    other = other_core(values)
    return jnp.concatenate(
        [jnp.where(first, values, other), jnp.where(first, other, values)], axis=0
    )


def vmem_spec():
    return pl.BlockSpec(memory_space=pltpu.VMEM)


def any_spec():
    return pl.BlockSpec(memory_space=pl.ANY)


def call(body, outs, ins, specs, out_specs, scratch=(), grid=None, limit=60, flops=0, bytes_moved=0):
    extra = {} if grid is None else {"grid": grid}
    return pl.pallas_call(
        body,
        name=getattr(body, "func", body).__name__,
        out_shape=outs,
        in_specs=specs,
        out_specs=out_specs,
        scratch_shapes=list(scratch),
        compiler_params=pltpu.CompilerParams(vmem_limit_bytes=limit * 1024 * 1024),
        cost_estimate=pl.CostEstimate(flops=1000, bytes_accessed=1000, transcendentals=0),
        **extra,
    )(*ins)


def shaped(shape, kind):
    return jax.ShapeDtypeStruct(shape, kind)


LOW, WIDE = jnp.bfloat16, jnp.float32


def dot(a, b):
    return jnp.dot(a, b, preferred_element_type=WIDE)


def dot_nt(a, b):
    return lax.dot_general(a, b, (((1,), (1,)), ((), ())), preferred_element_type=WIDE)


def dot_tn(a, b):
    return lax.dot_general(a, b, (((0,), (0,)), ((), ())), preferred_element_type=WIDE)


def fetch(pieces, columns, buffer, sems):
    rows = pieces[0].shape[0]
    copies = []
    for i, piece in enumerate(pieces):
        copy = pltpu.make_async_copy(
            piece.at[:, columns[0] : columns[1]], buffer.at[i * rows : (i + 1) * rows], sems.at[i]
        )
        copy.start()
        copies.append(copy)

    def ready(first, last):
        for copy in copies[first:last]:
            copy.wait()

    return ready


def pack_kernel(count, *refs):
    out_ref, at = refs[count], 0
    for ref in refs[:count]:
        size = ref.shape[1]
        out_ref[:, at : at + size] = ref[...].astype(LOW)
        at += size


def pack(arrays):
    rows = arrays[0].shape[0]
    total = sum(a.shape[1] for a in arrays)
    return call(
        functools.partial(pack_kernel, len(arrays)),
        shaped((rows, total), LOW),
        arrays,
        [vmem_spec() for _ in arrays],
        vmem_spec(),
        bytes_moved=rows * total * 6,
        limit=60,
    )


def flip(values):
    width = values.shape[1]
    lane = lax.broadcasted_iota(jnp.int32, values.shape, 1)
    return jnp.where(
        lane % HD < HD // 2, pltpu.roll(values, width - HD // 2, 1), pltpu.roll(values, HD // 2, 1)
    )


def tile_lanes(table, width):
    return jnp.concatenate([table] * (width // table.shape[1]), axis=1)


def qkv_kernel(x_ref, shift_ref, cos_ref, sin_ref, *refs):
    pieces, (q_ref, k_ref, v_ref, buffer, sems) = refs[:16], refs[16:]
    width = q_ref.shape[1]
    ready = fetch(pieces, (0, 3 * width), buffer, sems)
    ready(0, 16)
    chunk = min(256, width)
    cos_table, sin_table = tile_lanes(cos_ref[...], chunk), tile_lanes(sin_ref[...], chunk)
    for which, out_ref in enumerate((q_ref, k_ref, v_ref)):
        for at in range(0, width, chunk):
            first = which * width + at
            pre = dot(x_ref[...], buffer[:, first : first + chunk]) + shift_ref[:, first : first + chunk]
            if which < 2:
                pre = pre * cos_table + flip(pre) * sin_table
            if which == 0:
                pre = pre.astype(LOW).astype(WIDE) * (HD ** -0.5)
            out_ref[:, at : at + chunk] = pre.astype(LOW)


def project_qkv(x_all, shift, cos_table, sin_table, pieces, width):
    rows, depth = x_all.shape
    out = shaped((rows, width), LOW)
    return call(
        qkv_kernel,
        (out, out, out),
        (x_all, shift, cos_table, sin_table, *pieces),
        [vmem_spec()] * 4 + [any_spec()] * 16,
        (vmem_spec(),) * 3,
        [pltpu.VMEM((depth, 3 * width), LOW), pltpu.SemaphoreType.DMA((16,))],
        flops=2 * rows * depth * 3 * width,
        bytes_moved=2 * (3 * depth * width + rows * depth),
        limit=60,
    )


def attend_kernel(heads, q_ref, k_ref, v_ref, column_ref, row_ref, ctx_ref, prob_ref, mask_ref):
    rows = q_ref.shape[0]
    mask_ref[...] = jnp.where(column_ref[...] == row_ref[...], 0.0, MASKED_SCORE)
    flat = v_ref[...].astype(WIDE).T.astype(LOW)
    parts = []
    for head in range(heads):
        cols = slice(head * HD, head * HD + HD)
        scores = dot_nt(k_ref[:, cols], q_ref[:, cols]) + mask_ref[...]
        top = jnp.max(scores, axis=0, keepdims=True)
        raised = jnp.exp(scores - top)
        total = jnp.sum(raised, axis=0, keepdims=True)
        prob = (raised * (1.0 / total)).astype(LOW)
        prob_ref[head] = prob
        parts.append(dot(flat[cols], prob))
    ctx_ref[...] = jnp.concatenate(parts, axis=0).T.astype(LOW)


def attend(query, key, value, column, row, first, heads):
    rows = query.shape[0]
    width = heads * HD
    block = pl.BlockSpec((rows, width), lambda i: (0, first))
    whole = lambda shape: pl.BlockSpec(shape, lambda i: (0,) * len(shape))
    return call(
        functools.partial(attend_kernel, heads),
        (shaped((rows, width), LOW), shaped((heads, rows, rows), LOW)),
        (query, key, value, column, row),
        [block] * 3 + [whole((rows, 1)), whole((1, rows))],
        (whole((rows, width)), whole((heads, rows, rows))),
        [pltpu.VMEM((rows, rows), WIDE)],
        grid=(1,),
        flops=4 * heads * rows * rows * HD,
        bytes_moved=2 * heads * rows * rows,
        limit=60,
    )


def attend_back_kernel(heads, q_ref, k_ref, v_ref, g_ref, prob_ref, cos_ref, sin_ref, gq_ref, gk_ref, gv_ref, sums_ref):
    width = heads * HD
    key_flat = k_ref[...].astype(WIDE).T.astype(LOW)
    q_parts, k_parts, v_parts = [], [], []
    for head in range(heads):
        cols = slice(head * HD, head * HD + HD)
        prob = prob_ref[head]
        prob_wide = prob.astype(WIDE)
        grad = dot_nt(v_ref[:, cols], g_ref[:, cols])
        delta = jnp.sum(prob_wide * grad, axis=0, keepdims=True)
        raw = (prob_wide * (grad - delta)).astype(LOW)
        v_parts.append(dot(prob, g_ref[:, cols]))
        k_parts.append(dot(raw, q_ref[:, cols]))
        q_parts.append(dot(key_flat[cols], raw))
    cos_table, sin_table = tile_lanes(cos_ref[...], width), tile_lanes(sin_ref[...], width)
    gq = jnp.concatenate(q_parts, axis=0).T * (HD ** -0.5)
    gk = jnp.concatenate(k_parts, axis=1)
    gv = jnp.concatenate(v_parts, axis=1)
    gq = (gq * cos_table - flip(gq) * sin_table).astype(LOW)
    gk = (gk * cos_table - flip(gk) * sin_table).astype(LOW)
    gv = gv.astype(LOW)
    for i, (ref, value) in enumerate(((gq_ref, gq), (gk_ref, gk), (gv_ref, gv))):
        ref[...] = value
        sums_ref[i : i + 1, :] = jnp.sum(value.astype(WIDE), axis=0, keepdims=True)


def attend_back(query, key, value, grad_ctx, prob, cos_table, sin_table, first, heads):
    rows = query.shape[0]
    width = heads * HD
    block = pl.BlockSpec((rows, width), lambda i: (0, first))
    whole = lambda shape: pl.BlockSpec(shape, lambda i: (0,) * len(shape))
    out = shaped((rows, width), LOW)
    return call(
        functools.partial(attend_back_kernel, heads),
        (out, out, out, shaped((3, width), WIDE)),
        (query, key, value, grad_ctx, prob, cos_table, sin_table),
        [block] * 4 + [whole(prob.shape), whole(cos_table.shape), whole(sin_table.shape)],
        (whole((rows, width)),) * 3 + (whole((3, width)),),
        grid=(1,),
        flops=8 * heads * rows * rows * HD,
        bytes_moved=2 * heads * rows * rows,
        limit=60,
    )


def spread_kernel(count, first, width, *refs):
    lefts, pieces, (out_ref, buffer, sems) = refs[:count], refs[count : count + 16], refs[count + 16 :]
    ready = fetch(pieces, (first, first + width), buffer, sems)
    left = lefts[0][...] if count == 1 else jnp.concatenate([ref[...] for ref in lefts], axis=1)
    step = buffer.shape[0] // 4
    for i in range(4):
        ready(4 * i, 4 * i + 4)
        out_ref[:, i * step : i * step + step] = dot_nt(left, buffer[i * step : i * step + step]).astype(LOW)


def spread(lefts, pieces, first, width):
    rows = lefts[0].shape[0]
    depth = 16 * pieces[0].shape[0]
    return call(
        functools.partial(spread_kernel, len(lefts), first, width),
        shaped((rows, depth), LOW),
        (*lefts, *pieces),
        [vmem_spec()] * len(lefts) + [any_spec()] * 16,
        vmem_spec(),
        [pltpu.VMEM((depth, width), LOW), pltpu.SemaphoreType.DMA((16,))],
        flops=2 * rows * depth * width,
        bytes_moved=2 * (depth * width + rows * width + rows * depth),
        limit=60,
    )


def spec_rows(rows, width, turn=0, steps=4):
    if turn:
        return pl.BlockSpec((rows, width), lambda i: ((i + turn) % steps, 0))
    return pl.BlockSpec((rows, width), lambda i: (i, 0))


def spec_own(rows, width):
    return pl.BlockSpec((rows, width), lambda i: (jnp.minimum(i, 1), 0))


def spec_whole(shape):
    return pl.BlockSpec(shape, lambda i: (0,) * len(shape))


def row_stats(values):
    mean = jnp.mean(values, axis=1, keepdims=True)
    centered = values - mean
    inv = lax.rsqrt(jnp.mean(centered * centered, axis=1, keepdims=True) + EPSILON)
    return centered * inv, inv


def row_back(grad, unit, inv, gain):
    scaled = grad * gain
    return inv * (
        scaled
        - jnp.mean(scaled, axis=1, keepdims=True)
        - unit * jnp.mean(scaled * unit, axis=1, keepdims=True)
    )


def first_norm_kernel(x_ref, mine_ref, other_ref, vec_ref, unit_ref, inv_ref, low_ref):
    pre = x_ref[...].astype(WIDE) + (mine_ref[...].astype(WIDE) + other_ref[...].astype(WIDE)) + vec_ref[3:4, :]
    unit, inv = row_stats(pre)
    unit_ref[...] = unit
    inv_ref[...] = jnp.broadcast_to(inv, inv_ref.shape)
    low_ref[...] = (unit * vec_ref[5:6, :] + vec_ref[6:7, :]).astype(LOW)


def first_norm(x_all, mine, other, vectors):
    rows, width = x_all.shape
    step = rows // 4
    return call(
        first_norm_kernel,
        (shaped((rows, width), WIDE), shaped((rows, 128), WIDE), shaped((rows, width), LOW)),
        (x_all, mine, other, vectors),
        [spec_rows(step, width), spec_rows(step, width), spec_rows(step, width, 2), spec_whole(vectors.shape)],
        (spec_rows(step, width), spec_rows(step, 128), spec_rows(step, width)),
        grid=(4,),
        bytes_moved=12 * rows * width,
        limit=60,
    )


def up_kernel(first, mid_ref, shift_ref, *refs):
    pieces, (act_ref, slope_ref, buffer, sems) = refs[:16], refs[16:]
    width = act_ref.shape[1]
    ready = fetch(pieces, (first, first + width), buffer, sems)
    ready(0, 16)
    chunk = 256
    for at in range(0, width, chunk):
        u = dot(mid_ref[...], buffer[:, at : at + chunk]) + shift_ref[:, at : at + chunk]
        phi = 0.5 + 0.5 * lax.erf(u * (2.0 ** -0.5))
        act_ref[:, at : at + chunk] = (u * phi).astype(LOW)
        slope_ref[:, at : at + chunk] = (phi + u * (jnp.exp(-0.5 * u * u) * (2.0 * math.pi) ** -0.5)).astype(LOW)


def feed_up(mid_low, shift, pieces, first, width):
    rows, depth = mid_low.shape
    out = shaped((rows, width), LOW)
    return call(
        functools.partial(up_kernel, first),
        (out, out),
        (mid_low, shift, *pieces),
        [vmem_spec()] * 2 + [any_spec()] * 16,
        (vmem_spec(),) * 2,
        [pltpu.VMEM((depth, width), LOW), pltpu.SemaphoreType.DMA((16,))],
        flops=2 * rows * depth * width,
        bytes_moved=2 * (depth * width + rows * depth + 2 * rows * width),
        limit=60,
    )


def second_norm_kernel(first, unit1_ref, mine_ref, other_ref, vec_ref, cot_ref, *refs):
    pieces = refs[:16]
    wide_ref, mid_ref, narrow_ref, grad_ref, low_ref, top_ref, sums_ref, proj, sems = refs[16:]
    step = pl.program_id(0)
    cols = proj.shape[1]

    @pl.when(step == 0)
    def _():
        fetch(pieces, (first, first + cols), proj, sems)(0, 16)
        sums_ref[...] = jnp.zeros_like(sums_ref)

    pre = (
        unit1_ref[...] * vec_ref[5:6, :]
        + vec_ref[6:7, :]
        + (mine_ref[...].astype(WIDE) + other_ref[...].astype(WIDE))
        + vec_ref[4:5, :]
    )
    unit, inv = row_stats(pre)
    top = (unit * vec_ref[7:8, :] + vec_ref[8:9, :]).astype(LOW)
    top_ref[...] = top

    @pl.when(step < 2)
    def _():
        embed = dot(top, proj[...])
        wide_ref[...] = embed[:, : wide_ref.shape[1]]
        mid_ref[...] = embed[:, 128 : 128 + mid_ref.shape[1]]
        narrow_ref[...] = embed[:, 256 : 256 + narrow_ref.shape[1]]

    g_top = dot_nt(cot_ref[...], proj[...])
    g_sum = row_back(g_top, unit, inv, vec_ref[7:8, :])
    grad_ref[...] = g_sum
    low_ref[...] = g_sum.astype(LOW)
    sums_ref[0:1, :] += jnp.sum(g_sum, axis=0, keepdims=True)
    sums_ref[1:2, :] += jnp.sum(g_top * unit, axis=0, keepdims=True)
    sums_ref[2:3, :] += jnp.sum(g_top, axis=0, keepdims=True)


def second_norm(unit1, mine, other, vectors, cot_all, pieces, first, sizes):
    rows, width = unit1.shape
    step = rows // 4
    cols = cot_all.shape[1]
    return call(
        functools.partial(second_norm_kernel, first),
        tuple(shaped((rows // 2, n), WIDE) for n in sizes)
        + (shaped((rows, width), WIDE), shaped((rows, width), LOW), shaped((rows, width), LOW), shaped((8, width), WIDE)),
        (unit1, mine, other, vectors, cot_all, *pieces),
        [
            spec_rows(step, width),
            spec_rows(step, width),
            spec_rows(step, width, 2),
            spec_whole(vectors.shape),
            spec_rows(step, cols),
        ]
        + [any_spec()] * 16,
        tuple(spec_own(step, n) for n in sizes)
        + (spec_rows(step, width), spec_rows(step, width), spec_rows(step, width), spec_whole((8, width))),
        [pltpu.VMEM((width, cols), LOW), pltpu.SemaphoreType.DMA((16,))],
        grid=(4,),
        flops=4 * rows * width * cols,
        bytes_moved=16 * rows * width,
        limit=60,
    )


def hidden_back_kernel(first, g_ref, slope_ref, *refs):
    pieces, (out_ref, sums_ref, buffer, sems) = refs[:16], refs[16:]
    width = out_ref.shape[1]
    ready = fetch(pieces, (first, first + width), buffer, sems)
    ready(0, 16)
    chunk = 256
    for at in range(0, width, chunk):
        g = dot(g_ref[...], buffer[:, at : at + chunk]) * slope_ref[:, at : at + chunk].astype(WIDE)
        g = g.astype(LOW)
        out_ref[:, at : at + chunk] = g
        sums_ref[:, at : at + chunk] = jnp.sum(g.astype(WIDE), axis=0, keepdims=True)


def hidden_back(grad_low, slope, pieces, first):
    rows, depth = grad_low.shape
    width = slope.shape[1]
    return call(
        functools.partial(hidden_back_kernel, first),
        (shaped((rows, width), LOW), shaped((1, width), WIDE)),
        (grad_low, slope, *pieces),
        [vmem_spec()] * 2 + [any_spec()] * 16,
        (vmem_spec(),) * 2,
        [pltpu.VMEM((depth, width), LOW), pltpu.SemaphoreType.DMA((16,))],
        flops=2 * rows * depth * width,
        bytes_moved=2 * (depth * width + rows * depth + 2 * rows * width),
        limit=60,
    )


def context_back_kernel(first, g_ref, *refs):
    pieces, (out_ref, buffer, sems) = refs[:16], refs[16:]
    width = out_ref.shape[1]
    fetch(pieces, (first, first + width), buffer, sems)(0, 16)
    out_ref[...] = dot(g_ref[...], buffer[...]).astype(LOW)


def context_back(grad_low, pieces, first, width):
    rows, depth = grad_low.shape
    return call(
        functools.partial(context_back_kernel, first),
        shaped((rows, width), LOW),
        (grad_low, *pieces),
        [vmem_spec()] + [any_spec()] * 16,
        vmem_spec(),
        [pltpu.VMEM((depth, width), LOW), pltpu.SemaphoreType.DMA((16,))],
        flops=2 * rows * depth * width,
        bytes_moved=2 * (depth * width + rows * depth + rows * width),
        limit=60,
    )


def fold_kernel(pairs, extra, *refs):
    at = 0
    groups = []
    for n in pairs:
        groups.append((refs[at], refs[at + 1 : at + 1 + n]))
        at += 1 + n
    add_ref = None
    if extra:
        add_ref = refs[at]
        at += 1
    outs, (buffer, sems) = refs[at : at + 16], refs[at + 16 :]
    rows = outs[0].shape[0]
    copies = []
    for i in range(4):
        block = slice(4 * rows * i, 4 * rows * (i + 1))
        column = 0
        for left_ref, rights in groups:
            for right_ref in rights:
                size = right_ref.shape[1]
                for part in range(0, size, 512):
                    end = min(part + 512, size)
                    value = dot_tn(left_ref[:, block], right_ref[:, part:end])
                    if extra and right_ref is groups[-1][1][-1]:
                        value = value + add_ref[block].astype(WIDE)
                    buffer[block, column + part : column + end] = value.astype(LOW)
                column += size
        for k in range(4 * i, 4 * i + 4):
            copy = pltpu.make_async_copy(buffer.at[k * rows : (k + 1) * rows], outs[k], sems.at[k])
            copy.start()
            copies.append(copy)
    for copy in copies:
        copy.wait()


def fold(groups, extra=None):
    left = groups[0][0]
    rows, depth = left.shape
    ins = [a for l, rs in groups for a in (l, *rs)]
    width = sum(r.shape[1] for _, rs in groups for r in rs)
    total = width
    if extra is not None:
        ins.append(extra)
    piece = shaped((depth // 16, total), LOW)
    return call(
        functools.partial(fold_kernel, tuple(len(rs) for _, rs in groups), extra is not None),
        (piece,) * 16,
        ins,
        [vmem_spec()] * len(ins),
        (any_spec(),) * 16,
        [pltpu.VMEM((depth, total), LOW), pltpu.SemaphoreType.DMA((16,))],
        flops=2 * rows * depth * width,
        bytes_moved=2 * (depth * total + rows * width + rows * depth),
        limit=60,
    )


def middle_back_kernel(g_ref, mine_ref, other_ref, unit_ref, inv_ref, vec_ref, own_ref, low_ref, sums_ref):
    step = pl.program_id(0)

    @pl.when(step == 0)
    def _():
        sums_ref[...] = jnp.zeros_like(sums_ref)

    unit = unit_ref[...]
    g_mid = g_ref[...] + (mine_ref[...].astype(WIDE) + other_ref[...].astype(WIDE))
    g_pre = row_back(g_mid, unit, inv_ref[:, :1], vec_ref[5:6, :])

    @pl.when(step < 2)
    def _():
        own_ref[...] = g_pre

    low_ref[...] = g_pre.astype(LOW)
    sums_ref[0:1, :] += jnp.sum(g_pre, axis=0, keepdims=True)
    sums_ref[1:2, :] += jnp.sum(g_mid * unit, axis=0, keepdims=True)
    sums_ref[2:3, :] += jnp.sum(g_mid, axis=0, keepdims=True)


def middle_back(grad, mine, other, unit, inv, vectors):
    rows, width = grad.shape
    step = rows // 4
    return call(
        middle_back_kernel,
        (shaped((rows // 2, width), WIDE), shaped((rows, width), LOW), shaped((8, width), WIDE)),
        (grad, mine, other, unit, inv, vectors),
        [
            spec_rows(step, width),
            spec_rows(step, width),
            spec_rows(step, width, 2),
            spec_rows(step, width),
            spec_rows(step, 128),
            spec_whole(vectors.shape),
        ],
        (spec_own(step, width), spec_rows(step, width), spec_whole((8, width))),
        grid=(4,),
        bytes_moved=14 * rows * width,
        limit=60,
    )


def finish_kernel(place_ref, g_ref, mine_ref, other_ref, out_ref):
    z, y, x = place_ref[0], place_ref[1], place_ref[2]
    turn = x == 1
    for block in range(8):
        zb, yb = block // 2, block % 2
        source = pl.multiple_of((((zb + 4 - z) % 4) * 2 + (yb + y) % 2) * 128, 128)
        cols = pl.ds(source, 128)
        part = g_ref[:, cols] + mine_ref[:, cols].astype(WIDE) + other_ref[:, cols].astype(WIDE)
        out_ref[:, block * 128 : block * 128 + 128] = jnp.where(turn, pltpu.roll(part, 64, 1), part)


def finish(grad, mine, other):
    if not gridded():
        return grad + mine.astype(WIDE) + other.astype(WIDE)
    rows, width = grad.shape
    return call(
        finish_kernel,
        shaped((rows, width), WIDE),
        (grid_place(), grad, mine, other),
        [pl.BlockSpec(memory_space=pltpu.SMEM)] + [vmem_spec()] * 3,
        vmem_spec(),
        bytes_moved=12 * rows * width,
        limit=60,
    )


def small_kernel(*refs):
    vectors, heads, (out_ref, rows_ref) = refs[:10], refs[10:13], refs[13:]
    rows_ref[...] = jnp.zeros_like(rows_ref)
    for i, ref in enumerate(vectors):
        rows_ref[i : i + 1, : ref.shape[1]] = ref[...]
    out_ref[...] = jnp.zeros_like(out_ref)
    out_ref[:16, :128] = rows_ref[...].astype(LOW)
    for i, ref in enumerate(heads):
        out_ref[16 : 16 + ref.shape[0], 128 * i : 128 * i + ref.shape[1]] = ref[...].astype(LOW)


def small_pack(vectors, heads):
    piece = heads[0].shape[0]
    ins = [v.reshape(1, -1) for v in vectors] + list(heads)
    return call(
        small_kernel,
        shaped((16 + piece, 384), LOW),
        ins,
        [vmem_spec()] * len(ins),
        vmem_spec(),
        [pltpu.VMEM((16, 128), WIDE)],
        bytes_moved=100000,
        limit=60,
    )


def pack_rows_kernel(spot_ref, q_ref, k_ref, v_ref, o_ref, mine_ref, other_ref, out_ref):
    first = spot_ref[3] == 0
    width = q_ref.shape[1]
    for i, ref in enumerate((q_ref, k_ref, v_ref, o_ref)):
        out_ref[:, i * width : i * width + width] = ref[...].astype(LOW)
    piece = out_ref.shape[0] // 2
    mine, other = mine_ref[:16, :128].astype(WIDE), other_ref[:16, :128].astype(WIDE)
    zero, one = jnp.where(first, mine, other), jnp.where(first, other, mine)
    lane = lax.broadcasted_iota(jnp.int32, zero.shape, 1)
    row = lax.broadcasted_iota(jnp.int32, zero.shape, 0)
    both = jnp.where(lane < piece, zero, pltpu.roll(one, piece, 1))
    both = jnp.where(row == 9, zero, jnp.where(row == 10, pltpu.roll(one, 1, 0), both))
    out_ref[:16, 4 * width :] = both.astype(LOW)
    out_ref[16:, 4 * width :] = jnp.zeros((2 * piece - 16, 128), LOW)


def pack_rows(spot, weights, mine, other):
    rows, width = weights[0].shape
    return call(
        pack_rows_kernel,
        shaped((rows, 4 * width + 128), LOW),
        (spot, *weights, mine, other),
        [pl.BlockSpec(memory_space=pltpu.SMEM)] + [vmem_spec()] * 6,
        vmem_spec(),
        bytes_moved=18 * rows * width,
        limit=60,
    )


def pack_heads_kernel(spot_ref, up_ref, down_ref, mine_ref, other_ref, out_ref):
    first = spot_ref[3] == 0
    width = 2 * up_ref.shape[1]
    piece = out_ref.shape[0] // 2
    out_ref[:, : width // 2] = up_ref[...].astype(LOW)
    out_ref[:, width // 2 : width] = down_ref[...].astype(LOW)
    mine, other = mine_ref[16:], other_ref[16:]
    out_ref[:piece, width:] = jnp.where(first, mine, other)
    out_ref[piece:, width:] = jnp.where(first, other, mine)


def pack_heads(spot, up, down, mine, other):
    rows, width = up.shape
    return call(
        pack_heads_kernel,
        shaped((rows, 2 * width + 384), LOW),
        (spot, up, down, mine, other),
        [pl.BlockSpec(memory_space=pltpu.SMEM)] + [vmem_spec()] * 4,
        vmem_spec(),
        bytes_moved=6 * rows * width,
        limit=60,
    )


def vectors_kernel(first, spot_ref, *refs):
    pieces, (vec_ref, qkv_ref, up_ref, low_buffer, rows_ref, sems) = refs[:16], refs[16:]
    z, y, x, core = spot_ref[0], spot_ref[1], spot_ref[2], spot_ref[3]
    copies = []
    for i, piece in enumerate(pieces):
        copy = pltpu.make_async_copy(
            piece.at[0:16, first : first + 128], low_buffer.at[16 * i : 16 * i + 16], sems.at[i]
        )
        copy.start()
        copies.append(copy)
    for copy in copies:
        copy.wait()
    rows_ref[...] = low_buffer[...].astype(WIDE)
    lane = lax.broadcasted_iota(jnp.int32, (16, 128), 1)
    for j in range(8):
        even, odd = rows_ref[32 * j : 32 * j + 16], rows_ref[32 * j + 16 : 32 * j + 32]
        vec_ref[:, 128 * j : 128 * j + 128] = jnp.where(lane < 64, even, pltpu.roll(odd, 64, 1))
    turn = x == 1
    blocks = qkv_ref.shape[1] // 384
    for b in range(blocks):
        source = ((core * 2 + b // 2 + 4 - z) % 4) * 2 + (b % 2 + y) % 2
        part = vec_ref[:, pl.ds(pl.multiple_of(source * 128, 128), 128)]
        part = jnp.where(turn, pltpu.roll(part, 64, 1), part)
        for j in range(3):
            at = (j * blocks + b) * 128
            qkv_ref[:, at : at + 128] = part[j : j + 1]
    for j in range(8):
        key = (((core * 2 + j // 4 + 4 - z) % 4) * 2 + (j // 2 % 2 + y) % 2) * 2 + (j % 2 + x) % 2
        for t in range(2):
            at = j * 256 + t * 128
            up_ref[:, at : at + 128] = rows_ref[pl.ds(key * 16 + 9 + t, 1), :]


def read_vectors(spot, pieces, first, width, head_width, hidden):
    return call(
        functools.partial(vectors_kernel, first),
        (shaped((16, width), WIDE), shaped((1, 3 * head_width), WIDE), shaped((1, hidden), WIDE)),
        (spot, *pieces),
        [pl.BlockSpec(memory_space=pltpu.SMEM)] + [any_spec()] * 16,
        (vmem_spec(),) * 3,
        [pltpu.VMEM((256, 128), LOW), pltpu.VMEM((256, 128), WIDE), pltpu.SemaphoreType.DMA((16,))],
        bytes_moved=200000,
        limit=60,
    )


def sums_kernel(zero_ref, one_ref, up_ref, out_ref, rows_ref):
    rows_ref[...] = jnp.zeros_like(rows_ref)
    half = zero_ref.shape[1]
    rows_ref[0:3, :half] = zero_ref[...]
    rows_ref[0:3, half : 2 * half] = one_ref[...]
    rows_ref[3:4, :] = up_ref[...]
    out_ref[...] = rows_ref[...].astype(LOW)


def pack_sums(zero, one, up):
    width = up.shape[1]
    return call(
        sums_kernel,
        shaped((16, width), LOW),
        (zero, one, up),
        [vmem_spec()] * 3,
        vmem_spec(),
        [pltpu.VMEM((16, width), WIDE)],
        bytes_moved=100000,
        limit=60,
    )


def vector_grads_kernel(share, spot_ref, mine_ref, other_ref, mid_ref, top_ref, out_ref, plain, long, block):
    z, y, x, core = spot_ref[0], spot_ref[1], spot_ref[2], spot_ref[3]
    turn = x == 1
    half = plain.shape[1] // 2
    hidden = mine_ref.shape[1]
    mine, other = mine_ref[...].astype(WIDE), other_ref[...].astype(WIDE)
    for i in range(2):
        side = jnp.where(core == i, mine, other)
        plain[:, i * half : i * half + half] = side[:8, :half]
        long[:, i * hidden : i * hidden + hidden] = side[3:4]
    out_ref[...] = jnp.zeros_like(out_ref)
    for j in range(8):
        source = ((j // 2 + z) % 4) * 2 + (j % 2 + y) % 2
        part = plain[:, pl.ds(pl.multiple_of(source * 128, 128), 128)]
        part = jnp.where(turn, pltpu.roll(part, 64, 1), part)
        cols = slice(128 * j, 128 * j + 128)
        block[0:3, :] = part[0:3]
        block[3:4, :] = mid_ref[0:1, cols]
        block[4:5, :] = top_ref[0:1, cols]
        block[5:7, :] = mid_ref[1:3, cols]
        block[7:9, :] = top_ref[1:3, cols]
        block[9:16, :] = jnp.zeros((7, 128), WIDE)
        pair = block[...]
        for odd in range(2):
            owner = source * 2 + (odd + x) % 2
            block[...] = pltpu.roll(pair, 64, 1) if odd else pair
            for t in range(2):
                wide_row = long[:, pl.ds(pl.multiple_of(owner * 256 + t * 128, 128), 128)]
                block[9 + 2 * t : 10 + 2 * t, :] = wide_row
                block[10 + 2 * t : 11 + 2 * t, :] = pltpu.roll(wide_row, 64, 1)
            at = (2 * j + odd) * 64
            out_ref[at : at + 16, share - 64 : share] = jnp.where(core == 1, block[:, :64], 0.0).astype(LOW)


def spread_vector_grads(spot, mine, other, mid_sums, top_sums, share):
    width = mid_sums.shape[1]
    hidden = mine.shape[1]
    return call(
        functools.partial(vector_grads_kernel, share),
        shaped((width, share), LOW),
        (spot, mine, other, mid_sums, top_sums),
        [pl.BlockSpec(memory_space=pltpu.SMEM)] + [vmem_spec()] * 4,
        vmem_spec(),
        [pltpu.VMEM((8, width), WIDE), pltpu.VMEM((1, 2 * hidden), WIDE), pltpu.VMEM((16, 128), WIDE)],
        bytes_moved=400000,
        limit=60,
    )


def local(
    hidden_in,
    segment_ids,
    positions,
    query_weight,
    key_weight,
    value_weight,
    output_weight,
    up_weight,
    down_weight,
    query_bias,
    key_bias,
    value_bias,
    output_bias,
    up_bias,
    down_bias,
    attn_gain,
    attn_shift,
    ffn_gain,
    ffn_shift,
    proj_wide,
    proj_mid,
    proj_narrow,
    cot_wide,
    cot_mid,
    cot_narrow,
):
    tp_rank = lax.axis_index("tp")
    own_rows, width = hidden_in.shape
    head_width = query_weight.shape[1]
    heads_here = head_width // HD
    hidden_here = up_weight.shape[1]
    piece = query_bias.shape[0]
    low, wide = LOW, WIDE
    half = head_width // 2
    half_heads = heads_here // 2

    spot = jnp.concatenate([grid_place(), tp_rank[None].astype(jnp.int32)])
    first_core = tp_rank == 0

    small = small_pack(
        (
            query_bias, key_bias, value_bias, output_bias, down_bias,
            attn_gain, attn_shift, ffn_gain, ffn_shift, up_bias,
        ),
        (proj_wide, proj_mid, proj_narrow),
    )
    small_other = other_core(small)
    attn_weights = (query_weight, key_weight, value_weight, output_weight.T)
    if gridded():
        attn_group = Gather(pack_rows(spot, attn_weights, small, small_other))
        ffn_group = Gather(pack_heads(spot, up_weight, down_weight.T, small, small_other))
    else:
        small_zero = jnp.where(first_core, small, small_other)
        small_one = jnp.where(first_core, small_other, small)
        attn_group = Gather(pack([*attn_weights, jnp.zeros((2 * piece, 128), low)]))
        heads_pair = jnp.concatenate([small_zero[16:], small_one[16:]], axis=0)
        ffn_group = Gather(pack([up_weight, down_weight.T, heads_pair]))
    queue = Queue()
    queue.add(attn_group, range(3))
    queue.add(attn_group, range(3, 6), *queue.at(0, 1, 2))

    tags = after(jnp.stack([segment_ids, positions]), *queue.at(1))
    tags = jnp.concatenate([tags, other_core(tags)], axis=1)
    hidden_other = other_core(after(hidden_in, *queue.at(0)))
    x_all = reorder(jnp.concatenate([hidden_in, hidden_other], axis=0), False)
    cot_own = jnp.concatenate(
        [cot_wide, jnp.pad(cot_mid, ((0, 0), (0, 128 - cot_mid.shape[1]))), jnp.pad(cot_narrow, ((0, 0), (0, 128 - cot_narrow.shape[1])))],
        axis=1,
    )
    cot_all = jnp.concatenate([cot_own, other_core(after(cot_own, *queue.at(3)))], axis=0)
    column, row = tags[0].reshape(-1, 1), tags[0].reshape(1, -1)
    cos_table, sin_table = rope_tables(tags[1], HD)
    cos_table = jnp.concatenate([cos_table, cos_table], axis=1)
    sin_table = jnp.concatenate([-sin_table[:, : HD // 2], sin_table[:, HD // 2 :]] * 2, axis=1)

    queue.add(attn_group, range(6, 9), *queue.at(3, 4, 5))
    queue.add(attn_group, range(9, 12), x_all, cot_all, cos_table, sin_table, *queue.at(6, 7, 8))
    queue.add(attn_group, range(12, 15), *queue.at(9, 10, 11))
    queue.add(ffn_group, range(3), *queue.at(12, 13, 14))
    attn_pieces = attn_group.pieces()
    if gridded():
        vectors, qkv_shift, up_shift = read_vectors(
            spot, attn_pieces, 4 * head_width, width, head_width, hidden_here
        )
    else:
        pair = jnp.stack([small_zero[:16, :128], small_one[:16, :128]])
        pair = lax.all_gather(pair[None], "fsdp", axis=0, tiled=True).astype(wide)
        vectors = pair[..., :piece].transpose(2, 0, 1, 3).reshape(16, width)
        qkv_shift = lax.dynamic_slice_in_dim(vectors[:3], tp_rank * head_width, head_width, 1).reshape(1, -1)
        up_shift = lax.dynamic_slice_in_dim(
            pair[:, :, 9, : 4 * piece].reshape(1, -1), tp_rank * hidden_here, hidden_here, 1
        )

    query, key, value = project_qkv(x_all, qkv_shift, cos_table, sin_table, attn_pieces, head_width)
    first_half = attend(query, key, value, column, row, 0, half_heads)
    queue.add(ffn_group, range(3, 6), first_half[0], *queue.at(15, 16, 17))
    second_half = attend(after(query, first_half[0], *queue.at(15, 16, 17)), key, value, column, row, 1, half_heads)
    contexts, probs = zip(first_half, second_half)
    attn_mine = spread(contexts, attn_pieces, 3 * head_width, head_width)
    unit_one, inv_one, mid_low = first_norm(
        x_all, attn_mine, other_core(after(attn_mine, *queue.at(18, 19, 20))), vectors
    )
    queue.add(ffn_group, range(6, 9), attn_mine, *queue.at(18, 19, 20))
    queue.add(ffn_group, range(9, 15), places=4)
    ffn_pieces = ffn_group.pieces()
    act_low, slope = feed_up(mid_low, up_shift, ffn_pieces, 0, hidden_here)
    ffn_mine = spread((act_low,), ffn_pieces, hidden_here, hidden_here)
    embed_wide, embed_mid, embed_narrow, grad_top, grad_top_low, top_low, top_sums = second_norm(
        unit_one, ffn_mine, other_core(ffn_mine), vectors, cot_all, ffn_pieces, 2 * hidden_here,
        (proj_wide.shape[1], proj_mid.shape[1], proj_narrow.shape[1]),
    )

    share = 192
    cot_share = lax.dynamic_slice_in_dim(cot_all, tp_rank * share, share, 1)
    grad_hidden_low, up_sums = hidden_back(grad_top_low, slope, ffn_pieces, hidden_here)
    mid_mine = spread((grad_hidden_low,), ffn_pieces, 0, hidden_here)
    mid_other = other_core(mid_mine)
    ffn_scatter = Scatter(fold([(after(grad_top_low, mid_mine), [act_low]), (mid_low, [grad_hidden_low])]))
    back = Queue()
    back.add(ffn_scatter, range(4))
    grad_own, grad_mid_low, mid_sums = middle_back(
        grad_top, mid_mine, mid_other, unit_one, inv_one, vectors
    )
    grad_context = context_back(grad_mid_low, attn_pieces, 3 * head_width, head_width)
    back.add(ffn_scatter, (4, 5), grad_context)
    backs = []
    for i in range(2):
        ready = [backs[0][0]] if i else back.at(0, 1, 2)
        backs.append(
            attend_back(query, key, value, after(grad_context, *ready), probs[i], cos_table, sin_table, i, half_heads)
        )
        back.add(ffn_scatter, (8, 9) if i else (6, 7), backs[i][0])
    grads = [backs[i][j] for j in range(3) for i in range(2)]
    sums = pack_sums(backs[0][3], backs[1][3], up_sums)
    sums_other = other_core(sums)
    if gridded():
        extra = spread_vector_grads(spot, sums, sums_other, mid_sums, top_sums, share)
    else:
        extra = jnp.zeros((width, share), low)
    attn_scatter = Scatter(
        fold([(after(x_all, *back.at(3, 4, 5, 6)), grads), (grad_mid_low, list(contexts)), (top_low, [cot_share])], extra)
    )
    back.add(attn_scatter, (0, 1, 2))
    back.add(ffn_scatter, (10,), attn_scatter.held[OWN])
    x_mine = spread([after(grads[0], attn_scatter.held[OWN], *back.at(7, 8))] + grads[1:], attn_pieces, 0, 3 * head_width)
    back.add(ffn_scatter, (11, 12), x_mine)
    back.add(attn_scatter, (3, 4), x_mine)
    x_other = other_core(after(x_mine[own_rows:], *back.at(10, 11, 12)))
    grad_hidden = finish(grad_own, x_mine[:own_rows], x_other)
    for group, number in (
        (attn_scatter, 5), (attn_scatter, 6), (ffn_scatter, 13), (attn_scatter, 7), (attn_scatter, 8), (ffn_scatter, 14),
    ):
        back.add(group, (number,), places=5)
    back.add(attn_scatter, range(9, 15), places=5)
    ffn_part = ffn_scatter.rows()
    attn_part = attn_scatter.rows()

    small_part = attn_part[:, 4 * head_width :]
    small_away = other_core(small_part)
    joined = jnp.where(
        first_core,
        jnp.concatenate([small_part, small_away], axis=1),
        jnp.concatenate([small_away, small_part], axis=1),
    ).astype(wide)
    own_heads = lax.dynamic_slice_in_dim(joined, tp_rank * piece, piece, 0)
    if gridded():
        block = joined[:16, 2 * share - 64 :]
        own_vectors = lax.dynamic_slice_in_dim(block[:9], tp_rank * piece, piece, 1)
        own_up = lax.dynamic_slice_in_dim(block, 9 + 2 * tp_rank, 2, 0).reshape(-1)
    else:
        both = jnp.concatenate(
            [
                jnp.where(first_core, sums, sums_other)[:3, :head_width],
                jnp.where(first_core, sums_other, sums)[:3, :head_width],
            ],
            axis=1,
        ).astype(wide)
        table = jnp.concatenate(
            [both, mid_sums[:1], top_sums[:1], mid_sums[1:3], top_sums[1:3], jnp.zeros((7, width), wide)], axis=0
        )
        table = lax.psum_scatter(table, "fsdp", scatter_dimension=1, tiled=True)
        own_vectors = lax.dynamic_slice_in_dim(table, tp_rank * piece, piece, 1)
        long = lax.dynamic_update_slice_in_dim(
            jnp.zeros((2 * hidden_here,), wide), up_sums.reshape(-1), tp_rank * hidden_here, 0
        )
        own_up = lax.psum_scatter(long, ("fsdp", "tp"), scatter_dimension=0, tiled=True)
    attn_part = attn_part.astype(wide)
    return (
        embed_wide,
        embed_mid,
        embed_narrow,
        grad_hidden,
        attn_part[:, :head_width],
        attn_part[:, head_width : 2 * head_width],
        attn_part[:, 2 * head_width : 3 * head_width],
        attn_part[:, 3 * head_width : 4 * head_width].T,
        ffn_part[:, hidden_here:].astype(wide),
        ffn_part[:, :hidden_here].astype(wide).T,
        own_vectors[0],
        own_vectors[1],
        own_vectors[2],
        own_vectors[3],
        own_up,
        own_vectors[4],
        own_vectors[5],
        own_vectors[6],
        own_vectors[7],
        own_vectors[8],
        own_heads[:, : proj_wide.shape[1]],
        own_heads[:, 128 : 128 + proj_mid.shape[1]],
        own_heads[:, 256 : 256 + proj_narrow.shape[1]],
    )


def solution(mesh):
    return jax.shard_map(
        local,
        mesh=mesh,
        in_specs=(
            P(("fsdp", "tp"), None),
            P(("fsdp", "tp")),
            P(("fsdp", "tp")),
            P("fsdp", "tp"),
            P("fsdp", "tp"),
            P("fsdp", "tp"),
            P("tp", "fsdp"),
            P("fsdp", "tp"),
            P("tp", "fsdp"),
            P(("fsdp", "tp")),
            P(("fsdp", "tp")),
            P(("fsdp", "tp")),
            P(("fsdp", "tp")),
            P(("fsdp", "tp")),
            P(("fsdp", "tp")),
            P(("fsdp", "tp")),
            P(("fsdp", "tp")),
            P(("fsdp", "tp")),
            P(("fsdp", "tp")),
            P(("fsdp", "tp"), None),
            P(("fsdp", "tp"), None),
            P(("fsdp", "tp"), None),
            P(("fsdp", "tp"), None),
            P(("fsdp", "tp"), None),
            P(("fsdp", "tp"), None),
        ),
        out_specs=(
            P(("fsdp", "tp"), None),
            P(("fsdp", "tp"), None),
            P(("fsdp", "tp"), None),
            P(("fsdp", "tp"), None),
            P("fsdp", "tp"),
            P("fsdp", "tp"),
            P("fsdp", "tp"),
            P("tp", "fsdp"),
            P("fsdp", "tp"),
            P("tp", "fsdp"),
            P(("fsdp", "tp")),
            P(("fsdp", "tp")),
            P(("fsdp", "tp")),
            P(("fsdp", "tp")),
            P(("fsdp", "tp")),
            P(("fsdp", "tp")),
            P(("fsdp", "tp")),
            P(("fsdp", "tp")),
            P(("fsdp", "tp")),
            P(("fsdp", "tp")),
            P(("fsdp", "tp"), None),
            P(("fsdp", "tp"), None),
            P(("fsdp", "tp"), None),
        ),
        check_vma=False,
    )
```

```python
import functools
import math

import jax
import jax.numpy as jnp
from jax import lax
from jax.experimental import pallas as pl
from jax.experimental.pallas import tpu as pltpu
from jax.sharding import PartitionSpec as P

HD = 64
SEQ_LEN = 512


EPSILON = 1e-05
MASKED_SCORE = -1e30
ROPE_BASE = 10000.0


def rope_tables(places, head_width):
    half_width = head_width // 2
    inv_freq = jnp.exp(
        jnp.arange(half_width, dtype=jnp.float32) * (-2.0 * math.log(ROPE_BASE) / head_width)
    )
    angles = places.astype(jnp.float32)[:, None] * inv_freq[None, :]
    cos_table = jnp.cos(angles)
    sin_table = jnp.sin(angles)
    return (
        jnp.concatenate([cos_table, cos_table], axis=-1),
        jnp.concatenate([sin_table, sin_table], axis=-1),
    )


def product_tn(left_side, right_side):
    return lax.dot_general(
        left_side, right_side, (((0,), (0,)), ((), ())), preferred_element_type=jnp.float32
    )

GATHERED = (
    ("z", (3, 0, 0)), ("x", (0, 0, 1)), ("y", (0, 1, 0)),
    ("z", (2, 0, 0)), ("x", (3, 0, 1)), ("y", (3, 1, 0)),
    ("z", (1, 0, 0)), ("x", (2, 0, 1)), ("y", (3, 1, 1)),
    ("z", (2, 1, 0)), ("x", (0, 1, 1)), ("y", (2, 1, 1)),
    ("x", (1, 0, 1)), ("y", (1, 1, 0)), ("z", (1, 1, 1)),
)
SCATTERED = (
    ("z", (1, 1, 1)), ("x", (1, 0, 1)), ("y", (1, 1, 0)), ("x", (0, 1, 1)),
    ("z", (2, 1, 0)), ("y", (2, 1, 1)), ("z", (1, 0, 0)), ("y", (3, 1, 1)),
    ("x", (2, 0, 1)), ("y", (3, 1, 0)), ("x", (3, 0, 1)), ("z", (2, 0, 0)),
    ("x", (0, 0, 1)), ("y", (0, 1, 0)), ("z", (3, 0, 0)),
)
KEYS = tuple((z, y, x) for z in range(4) for y in range(2) for x in range(2))
OWN = (0, 0, 0)


def place(z, y, x):
    return (z * 2 + y) * 2 + x


def hop(link):
    def target(z, y, x):
        if link == "x":
            return place(z, y, 1 - x)
        if link == "y":
            return place(z, 1 - y, x)
        return place((z + 1) % 4, y, x)

    return [(place(*k), target(*k)) for k in KEYS]


HOPS = {link: hop(link) for link in "xyz"}
BACK = {link: [(b, a) for a, b in pairs] for link, pairs in HOPS.items()}


def sender_key(key, link):
    z, y, x = key
    if link == "x":
        return (z, y, 1 - x)
    if link == "y":
        return (z, 1 - y, x)
    return ((z + 1) % 4, y, x)


def gridded():
    return lax.axis_size("fsdp") == 16


def after(values, *others):
    return lax.optimization_barrier((values, others))[0] if others else values


class Gather:
    def __init__(self, shard):
        self.have = {OWN: shard}

    def start(self, number, *others):
        link, key = GATHERED[number]
        send = self.have[sender_key(key, link)]
        if others:
            send = after(send, *others)
        self.have[key] = lax.ppermute(send, "fsdp", HOPS[link])
        return self.have[key]

    def pieces(self):
        if not gridded():
            full = lax.all_gather(self.have[OWN], "fsdp", axis=0, tiled=True)
            rows = full.shape[0] // 16
            return [full[rows * i : rows * (i + 1)] for i in range(16)]
        return [self.have[key] for key in KEYS]


class Scatter:
    def __init__(self, pieces):
        self.held = dict(zip(KEYS, pieces))
        self.parts = {key: [] for key in KEYS}

    def total(self, key, *others):
        return sum(after(self.parts[key], *others), after(self.held[key], *others))

    def start(self, number, *others):
        link, key = SCATTERED[number]
        part = lax.ppermute(self.total(key, *others), "fsdp", BACK[link])
        self.parts[sender_key(key, link)].append(part)
        return part

    def rows(self):
        if not gridded():
            full = jnp.concatenate([self.held[key] for key in KEYS], axis=0)
            return lax.psum_scatter(full, "fsdp", scatter_dimension=0, tiled=True)
        return self.total(OWN)


class Queue:
    def __init__(self):
        self.landed = []

    def add(self, group, numbers, *others, places=0):
        if gridded():
            for number in numbers:
                tied = self.landed[-places : len(self.landed) - places + 1] if places else []
                self.landed.append(group.start(number, *others, *tied))

    def at(self, *indices):
        return [self.landed[i] for i in indices if gridded()]


def other_core(values):
    return lax.ppermute(values, "tp", [(0, 1), (1, 0)])


def reorder_kernel(inverse, place_ref, in_ref, out_ref):
    z, y, x = place_ref[0], place_ref[1], place_ref[2]
    turn = x == 1
    for block in range(8):
        zb, yb = block // 2, block % 2
        away = (zb + 4 - z) % 4 if inverse else (zb + z) % 4
        source = pl.multiple_of((away * 2 + (yb + y) % 2) * 128, 128)
        part = in_ref[:, pl.ds(source, 128)].astype(jnp.float32)
        part = jnp.where(turn, pltpu.roll(part, 64, 1), part)
        out_ref[:, block * 128 : block * 128 + 128] = part.astype(out_ref.dtype)


def grid_place():
    me = lax.axis_index("fsdp")
    return jnp.stack([me // 4, (me // 2) % 2, me % 2]).astype(jnp.int32)


def reorder(values, inverse):
    if not gridded():
        return values
    places = grid_place()
    return pl.pallas_call(
        functools.partial(reorder_kernel, inverse),
        out_shape=jax.ShapeDtypeStruct(values.shape, values.dtype),
        in_specs=[
            pl.BlockSpec(memory_space=pltpu.SMEM),
            pl.BlockSpec(memory_space=pltpu.VMEM),
        ],
        out_specs=pl.BlockSpec(memory_space=pltpu.VMEM),
    )(places, values)


def halves(values):
    first = lax.axis_index("tp") == 0
    other = other_core(values)
    return jnp.concatenate(
        [jnp.where(first, values, other), jnp.where(first, other, values)], axis=0
    )


def vmem_spec():
    return pl.BlockSpec(memory_space=pltpu.VMEM)


def any_spec():
    return pl.BlockSpec(memory_space=pl.ANY)


def call(body, outs, ins, specs, out_specs, scratch=(), grid=None, limit=60, flops=0, bytes_moved=0):
    extra = {} if grid is None else {"grid": grid}
    return pl.pallas_call(
        body,
        name=getattr(body, "func", body).__name__,
        out_shape=outs,
        in_specs=specs,
        out_specs=out_specs,
        scratch_shapes=list(scratch),
        compiler_params=pltpu.CompilerParams(vmem_limit_bytes=limit * 1024 * 1024),
        cost_estimate=pl.CostEstimate(flops=1000, bytes_accessed=1000, transcendentals=0),
        **extra,
    )(*ins)


def shaped(shape, kind):
    return jax.ShapeDtypeStruct(shape, kind)


LOW, WIDE = jnp.bfloat16, jnp.float32


def dot(a, b):
    return jnp.dot(a, b, preferred_element_type=WIDE)


def dot_nt(a, b):
    return lax.dot_general(a, b, (((1,), (1,)), ((), ())), preferred_element_type=WIDE)


def dot_tn(a, b):
    return lax.dot_general(a, b, (((0,), (0,)), ((), ())), preferred_element_type=WIDE)


def fetch(pieces, columns, buffer, sems):
    rows = pieces[0].shape[0]
    copies = []
    for i, piece in enumerate(pieces):
        copy = pltpu.make_async_copy(
            piece.at[:, columns[0] : columns[1]], buffer.at[i * rows : (i + 1) * rows], sems.at[i]
        )
        copy.start()
        copies.append(copy)

    def ready(first, last):
        for copy in copies[first:last]:
            copy.wait()

    return ready


def pack_kernel(count, *refs):
    out_ref, at = refs[count], 0
    for ref in refs[:count]:
        size = ref.shape[1]
        out_ref[:, at : at + size] = ref[...].astype(LOW)
        at += size


def pack(arrays):
    rows = arrays[0].shape[0]
    total = sum(a.shape[1] for a in arrays)
    return call(
        functools.partial(pack_kernel, len(arrays)),
        shaped((rows, total), LOW),
        arrays,
        [vmem_spec() for _ in arrays],
        vmem_spec(),
        bytes_moved=rows * total * 6,
        limit=60,
    )


def flip(values):
    width = values.shape[1]
    lane = lax.broadcasted_iota(jnp.int32, values.shape, 1)
    return jnp.where(
        lane % HD < HD // 2, pltpu.roll(values, width - HD // 2, 1), pltpu.roll(values, HD // 2, 1)
    )


def tile_lanes(table, width):
    return jnp.concatenate([table] * (width // table.shape[1]), axis=1)


def qkv_kernel(x_ref, shift_ref, cos_ref, sin_ref, *refs):
    pieces, (q_ref, k_ref, v_ref, buffer, sems) = refs[:16], refs[16:]
    width = q_ref.shape[1]
    ready = fetch(pieces, (0, 3 * width), buffer, sems)
    ready(0, 16)
    chunk = min(256, width)
    cos_table, sin_table = tile_lanes(cos_ref[...], chunk), tile_lanes(sin_ref[...], chunk)
    for which, out_ref in enumerate((q_ref, k_ref, v_ref)):
        for at in range(0, width, chunk):
            first = which * width + at
            pre = dot(x_ref[...], buffer[:, first : first + chunk]) + shift_ref[:, first : first + chunk]
            if which < 2:
                pre = pre * cos_table + flip(pre) * sin_table
            if which == 0:
                pre = pre.astype(LOW).astype(WIDE) * (HD ** -0.5)
            out_ref[:, at : at + chunk] = pre.astype(LOW)


def project_qkv(x_all, shift, cos_table, sin_table, pieces, width):
    rows, depth = x_all.shape
    out = shaped((rows, width), LOW)
    return call(
        qkv_kernel,
        (out, out, out),
        (x_all, shift, cos_table, sin_table, *pieces),
        [vmem_spec()] * 4 + [any_spec()] * 16,
        (vmem_spec(),) * 3,
        [pltpu.VMEM((depth, 3 * width), LOW), pltpu.SemaphoreType.DMA((16,))],
        flops=2 * rows * depth * 3 * width,
        bytes_moved=2 * (3 * depth * width + rows * depth),
        limit=60,
    )


def attend_kernel(heads, q_ref, k_ref, v_ref, column_ref, row_ref, ctx_ref, prob_ref, mask_ref):
    rows = q_ref.shape[0]
    mask_ref[...] = jnp.where(column_ref[...] == row_ref[...], 0.0, MASKED_SCORE)
    flat = v_ref[...].astype(WIDE).T.astype(LOW)
    parts = []
    for head in range(heads):
        cols = slice(head * HD, head * HD + HD)
        scores = dot_nt(k_ref[:, cols], q_ref[:, cols]) + mask_ref[...]
        top = jnp.max(scores, axis=0, keepdims=True)
        raised = jnp.exp(scores - top)
        total = jnp.sum(raised, axis=0, keepdims=True)
        prob = (raised * (1.0 / total)).astype(LOW)
        prob_ref[head] = prob
        parts.append(dot(flat[cols], prob))
    ctx_ref[...] = jnp.concatenate(parts, axis=0).T.astype(LOW)


def attend(query, key, value, column, row, first, heads):
    rows = query.shape[0]
    width = heads * HD
    block = pl.BlockSpec((rows, width), lambda i: (0, first))
    whole = lambda shape: pl.BlockSpec(shape, lambda i: (0,) * len(shape))
    return call(
        functools.partial(attend_kernel, heads),
        (shaped((rows, width), LOW), shaped((heads, rows, rows), LOW)),
        (query, key, value, column, row),
        [block] * 3 + [whole((rows, 1)), whole((1, rows))],
        (whole((rows, width)), whole((heads, rows, rows))),
        [pltpu.VMEM((rows, rows), WIDE)],
        grid=(1,),
        flops=4 * heads * rows * rows * HD,
        bytes_moved=2 * heads * rows * rows,
        limit=60,
    )


def attend_back_kernel(heads, q_ref, k_ref, v_ref, g_ref, prob_ref, cos_ref, sin_ref, gq_ref, gk_ref, gv_ref, sums_ref):
    width = heads * HD
    key_flat = k_ref[...].astype(WIDE).T.astype(LOW)
    q_parts, k_parts, v_parts = [], [], []
    for head in range(heads):
        cols = slice(head * HD, head * HD + HD)
        prob = prob_ref[head]
        prob_wide = prob.astype(WIDE)
        grad = dot_nt(v_ref[:, cols], g_ref[:, cols])
        delta = jnp.sum(prob_wide * grad, axis=0, keepdims=True)
        raw = (prob_wide * (grad - delta)).astype(LOW)
        v_parts.append(dot(prob, g_ref[:, cols]))
        k_parts.append(dot(raw, q_ref[:, cols]))
        q_parts.append(dot(key_flat[cols], raw))
    cos_table, sin_table = tile_lanes(cos_ref[...], width), tile_lanes(sin_ref[...], width)
    gq = jnp.concatenate(q_parts, axis=0).T * (HD ** -0.5)
    gk = jnp.concatenate(k_parts, axis=1)
    gv = jnp.concatenate(v_parts, axis=1)
    gq = (gq * cos_table - flip(gq) * sin_table).astype(LOW)
    gk = (gk * cos_table - flip(gk) * sin_table).astype(LOW)
    gv = gv.astype(LOW)
    for i, (ref, value) in enumerate(((gq_ref, gq), (gk_ref, gk), (gv_ref, gv))):
        ref[...] = value
        sums_ref[i : i + 1, :] = jnp.sum(value.astype(WIDE), axis=0, keepdims=True)


def attend_back(query, key, value, grad_ctx, prob, cos_table, sin_table, first, heads):
    rows = query.shape[0]
    width = heads * HD
    block = pl.BlockSpec((rows, width), lambda i: (0, first))
    whole = lambda shape: pl.BlockSpec(shape, lambda i: (0,) * len(shape))
    out = shaped((rows, width), LOW)
    return call(
        functools.partial(attend_back_kernel, heads),
        (out, out, out, shaped((3, width), WIDE)),
        (query, key, value, grad_ctx, prob, cos_table, sin_table),
        [block] * 4 + [whole(prob.shape), whole(cos_table.shape), whole(sin_table.shape)],
        (whole((rows, width)),) * 3 + (whole((3, width)),),
        grid=(1,),
        flops=8 * heads * rows * rows * HD,
        bytes_moved=2 * heads * rows * rows,
        limit=60,
    )


def spread_kernel(count, parts, first, width, *refs):
    lefts, pieces, refs = refs[:count], refs[count : count + 16], refs[count + 16 :]
    outs, (buffer, sems) = refs[:parts], refs[parts:]
    ready = fetch(pieces, (first, first + width), buffer, sems)
    left = lefts[0][...] if count == 1 else jnp.concatenate([ref[...] for ref in lefts], axis=1)
    step = buffer.shape[0] // 2
    for i in range(2):
        ready(8 * i, 8 * i + 8)
        value = dot_nt(left, buffer[i * step : i * step + step]).astype(LOW)
        for k, out_ref in enumerate(outs):
            out_ref[:, i * step : i * step + step] = value[k * out_ref.shape[0] : (k + 1) * out_ref.shape[0]]


def spread(lefts, pieces, first, width, parts=1):
    rows = lefts[0].shape[0]
    depth = 16 * pieces[0].shape[0]
    return call(
        functools.partial(spread_kernel, len(lefts), parts, first, width),
        (shaped((rows // parts, depth), LOW),) * parts,
        (*lefts, *pieces),
        [vmem_spec()] * len(lefts) + [any_spec()] * 16,
        (vmem_spec(),) * parts,
        [pltpu.VMEM((depth, width), LOW), pltpu.SemaphoreType.DMA((16,))],
        flops=2 * rows * depth * width,
        bytes_moved=2 * (depth * width + rows * width + rows * depth),
        limit=60,
    )


def spec_rows(rows, width, turn=0, steps=4):
    if turn:
        return pl.BlockSpec((rows, width), lambda i: ((i + turn) % steps, 0))
    return pl.BlockSpec((rows, width), lambda i: (i, 0))


def spec_own(rows, width):
    return pl.BlockSpec((rows, width), lambda i: (jnp.minimum(i, 1), 0))


def spec_whole(shape):
    return pl.BlockSpec(shape, lambda i: (0,) * len(shape))


def row_stats(values):
    mean = jnp.mean(values, axis=1, keepdims=True)
    centered = values - mean
    inv = lax.rsqrt(jnp.mean(centered * centered, axis=1, keepdims=True) + EPSILON)
    return centered * inv, inv


def row_back(grad, unit, inv, gain):
    scaled = grad * gain
    return inv * (
        scaled
        - jnp.mean(scaled, axis=1, keepdims=True)
        - unit * jnp.mean(scaled * unit, axis=1, keepdims=True)
    )


def first_norm_kernel(x_ref, mine_ref, other_ref, vec_ref, unit_ref, inv_ref, low_ref):
    pre = x_ref[...].astype(WIDE) + (mine_ref[...].astype(WIDE) + other_ref[...].astype(WIDE)) + vec_ref[3:4, :]
    unit, inv = row_stats(pre)
    unit_ref[...] = unit
    inv_ref[...] = jnp.broadcast_to(inv, inv_ref.shape)
    low_ref[...] = (unit * vec_ref[5:6, :] + vec_ref[6:7, :]).astype(LOW)


def first_norm(x_all, mine, other, vectors):
    rows, width = x_all.shape
    step = rows // 4
    return call(
        first_norm_kernel,
        (shaped((rows, width), WIDE), shaped((rows, 128), WIDE), shaped((rows, width), LOW)),
        (x_all, mine, other, vectors),
        [spec_rows(step, width), spec_rows(step, width), spec_rows(step, width, 2), spec_whole(vectors.shape)],
        (spec_rows(step, width), spec_rows(step, 128), spec_rows(step, width)),
        grid=(4,),
        bytes_moved=12 * rows * width,
        limit=60,
    )


def feed_kernel(first, second, mid_ref, shift_ref, *refs):
    pieces, (act_ref, slope_ref, out_ref, buffer, below, sems, more_sems) = refs[:16], refs[16:]
    width = act_ref.shape[1]
    ready = fetch(pieces, (first, first + width), buffer, sems)
    later = fetch(pieces, (second, second + width), below, more_sems)
    ready(0, 16)
    chunk = 256
    for at in range(0, width, chunk):
        u = dot(mid_ref[...], buffer[:, at : at + chunk]) + shift_ref[:, at : at + chunk]
        phi = 0.5 + 0.5 * lax.erf(u * (2.0 ** -0.5))
        act_ref[:, at : at + chunk] = (u * phi).astype(LOW)
        slope_ref[:, at : at + chunk] = (phi + u * (jnp.exp(-0.5 * u * u) * (2.0 * math.pi) ** -0.5)).astype(LOW)
    step = below.shape[0] // 2
    for i in range(2):
        later(8 * i, 8 * i + 8)
        out_ref[:, i * step : i * step + step] = dot_nt(act_ref[...], below[i * step : i * step + step]).astype(LOW)


def feed(mid_low, shift, pieces, first, second, width):
    rows, depth = mid_low.shape
    out = shaped((rows, width), LOW)
    return call(
        functools.partial(feed_kernel, first, second),
        (out, out, shaped((rows, depth), LOW)),
        (mid_low, shift, *pieces),
        [vmem_spec()] * 2 + [any_spec()] * 16,
        (vmem_spec(),) * 3,
        [pltpu.VMEM((depth, width), LOW)] * 2 + [pltpu.SemaphoreType.DMA((16,))] * 2,
        limit=60,
    )


def second_norm_kernel(first, unit1_ref, mine_ref, other_ref, vec_ref, cot_ref, *refs):
    pieces = refs[:16]
    wide_ref, mid_ref, narrow_ref, grad_ref, low_ref, top_ref, sums_ref, proj, sems = refs[16:]
    step = pl.program_id(0)
    cols = proj.shape[1]

    @pl.when(step == 0)
    def _():
        fetch(pieces, (first, first + cols), proj, sems)(0, 16)
        sums_ref[...] = jnp.zeros_like(sums_ref)

    pre = (
        unit1_ref[...] * vec_ref[5:6, :]
        + vec_ref[6:7, :]
        + (mine_ref[...].astype(WIDE) + other_ref[...].astype(WIDE))
        + vec_ref[4:5, :]
    )
    unit, inv = row_stats(pre)
    top = (unit * vec_ref[7:8, :] + vec_ref[8:9, :]).astype(LOW)
    top_ref[...] = top

    @pl.when(step < 2)
    def _():
        embed = dot(top, proj[...])
        wide_ref[...] = embed[:, : wide_ref.shape[1]]
        mid_ref[...] = embed[:, 128 : 128 + mid_ref.shape[1]]
        narrow_ref[...] = embed[:, 256 : 256 + narrow_ref.shape[1]]

    g_top = dot_nt(cot_ref[...], proj[...])
    g_sum = row_back(g_top, unit, inv, vec_ref[7:8, :])
    grad_ref[...] = g_sum
    low_ref[...] = g_sum.astype(LOW)
    sums_ref[0:1, :] += jnp.sum(g_sum, axis=0, keepdims=True)
    sums_ref[1:2, :] += jnp.sum(g_top * unit, axis=0, keepdims=True)
    sums_ref[2:3, :] += jnp.sum(g_top, axis=0, keepdims=True)


def second_norm(unit1, mine, other, vectors, cot_all, pieces, first, sizes):
    rows, width = unit1.shape
    step = rows // 4
    cols = cot_all.shape[1]
    return call(
        functools.partial(second_norm_kernel, first),
        tuple(shaped((rows // 2, n), WIDE) for n in sizes)
        + (shaped((rows, width), WIDE), shaped((rows, width), LOW), shaped((rows, width), LOW), shaped((8, width), WIDE)),
        (unit1, mine, other, vectors, cot_all, *pieces),
        [
            spec_rows(step, width),
            spec_rows(step, width),
            spec_rows(step, width, 2),
            spec_whole(vectors.shape),
            spec_rows(step, cols),
        ]
        + [any_spec()] * 16,
        tuple(spec_own(step, n) for n in sizes)
        + (spec_rows(step, width), spec_rows(step, width), spec_rows(step, width), spec_whole((8, width))),
        [pltpu.VMEM((width, cols), LOW), pltpu.SemaphoreType.DMA((16,))],
        grid=(4,),
        flops=4 * rows * width * cols,
        bytes_moved=16 * rows * width,
        limit=60,
    )


def feed_back_kernel(first, second, g_ref, slope_ref, *refs):
    pieces, (grad_ref, sums_ref, out_ref, below, buffer, sems, more_sems) = refs[:16], refs[16:]
    width = grad_ref.shape[1]
    ready = fetch(pieces, (second, second + width), below, sems)
    later = fetch(pieces, (first, first + width), buffer, more_sems)
    ready(0, 16)
    chunk = 256
    for at in range(0, width, chunk):
        g = dot(g_ref[...], below[:, at : at + chunk]) * slope_ref[:, at : at + chunk].astype(WIDE)
        g = g.astype(LOW)
        grad_ref[:, at : at + chunk] = g
        sums_ref[:, at : at + chunk] = jnp.sum(g.astype(WIDE), axis=0, keepdims=True)
    step = buffer.shape[0] // 2
    for i in range(2):
        later(8 * i, 8 * i + 8)
        out_ref[:, i * step : i * step + step] = dot_nt(grad_ref[...], buffer[i * step : i * step + step]).astype(LOW)


def feed_back(grad_low, slope, pieces, first, second):
    rows, depth = grad_low.shape
    width = slope.shape[1]
    return call(
        functools.partial(feed_back_kernel, first, second),
        (shaped((rows, width), LOW), shaped((1, width), WIDE), shaped((rows, depth), LOW)),
        (grad_low, slope, *pieces),
        [vmem_spec()] * 2 + [any_spec()] * 16,
        (vmem_spec(),) * 3,
        [pltpu.VMEM((depth, width), LOW)] * 2 + [pltpu.SemaphoreType.DMA((16,))] * 2,
        limit=60,
    )


def fold_kernel(pairs, extra, *refs):
    at = 0
    groups = []
    for n in pairs:
        groups.append((refs[at], refs[at + 1 : at + 1 + n]))
        at += 1 + n
    add_ref = None
    if extra:
        add_ref = refs[at]
        at += 1
    outs, (buffer, sems) = refs[at : at + 16], refs[at + 16 :]
    rows = outs[0].shape[0]
    copies = []
    for i in range(4):
        block = slice(4 * rows * i, 4 * rows * (i + 1))
        column = 0
        for left_ref, rights in groups:
            for right_ref in rights:
                size = right_ref.shape[1]
                for part in range(0, size, 512):
                    end = min(part + 512, size)
                    value = dot_tn(left_ref[:, block], right_ref[:, part:end])
                    if extra and right_ref is groups[-1][1][-1]:
                        value = value + add_ref[block].astype(WIDE)
                    buffer[block, column + part : column + end] = value.astype(LOW)
                column += size
        for k in range(4 * i, 4 * i + 4):
            copy = pltpu.make_async_copy(buffer.at[k * rows : (k + 1) * rows], outs[k], sems.at[k])
            copy.start()
            copies.append(copy)
    for copy in copies:
        copy.wait()


def fold(groups, extra=None):
    left = groups[0][0]
    rows, depth = left.shape
    ins = [a for l, rs in groups for a in (l, *rs)]
    width = sum(r.shape[1] for _, rs in groups for r in rs)
    total = width
    if extra is not None:
        ins.append(extra)
    piece = shaped((depth // 16, total), LOW)
    return call(
        functools.partial(fold_kernel, tuple(len(rs) for _, rs in groups), extra is not None),
        (piece,) * 16,
        ins,
        [vmem_spec()] * len(ins),
        (any_spec(),) * 16,
        [pltpu.VMEM((depth, total), LOW), pltpu.SemaphoreType.DMA((16,))],
        flops=2 * rows * depth * width,
        bytes_moved=2 * (depth * total + rows * width + rows * depth),
        limit=60,
    )


def middle_back_kernel(first, g_ref, mine_ref, other_ref, unit_ref, inv_ref, vec_ref, *refs):
    pieces, (own_ref, low_ref, ctx_ref, sums_ref, buffer, sems) = refs[:16], refs[16:]
    step = pl.program_id(0)
    rows, width = pieces[0].shape[0], ctx_ref.shape[1]
    copies = [
        pltpu.make_async_copy(
            piece.at[:, first : first + width], buffer.at[i * rows : (i + 1) * rows], sems.at[i]
        )
        for i, piece in enumerate(pieces)
    ]

    @pl.when(step == 0)
    def _():
        for copy in copies:
            copy.start()
        sums_ref[...] = jnp.zeros_like(sums_ref)

    unit = unit_ref[...]
    g_mid = g_ref[...] + (mine_ref[...].astype(WIDE) + other_ref[...].astype(WIDE))
    g_pre = row_back(g_mid, unit, inv_ref[:, :1], vec_ref[5:6, :])

    @pl.when(step < 2)
    def _():
        own_ref[...] = g_pre

    low = g_pre.astype(LOW)
    low_ref[...] = low
    sums_ref[0:1, :] += jnp.sum(g_pre, axis=0, keepdims=True)
    sums_ref[1:2, :] += jnp.sum(g_mid * unit, axis=0, keepdims=True)
    sums_ref[2:3, :] += jnp.sum(g_mid, axis=0, keepdims=True)

    @pl.when(step == 0)
    def _():
        for copy in copies:
            copy.wait()

    ctx_ref[...] = dot(low, buffer[...]).astype(LOW)


def middle_back(grad, mine, other, unit, inv, vectors, pieces, first, out_width):
    rows, width = grad.shape
    step = rows // 4
    return call(
        functools.partial(middle_back_kernel, first),
        (
            shaped((rows // 2, width), WIDE), shaped((rows, width), LOW), shaped((rows, out_width), LOW),
            shaped((8, width), WIDE),
        ),
        (grad, mine, other, unit, inv, vectors, *pieces),
        [
            spec_rows(step, width),
            spec_rows(step, width),
            spec_rows(step, width, 2),
            spec_rows(step, width),
            spec_rows(step, 128),
            spec_whole(vectors.shape),
        ]
        + [any_spec()] * 16,
        (spec_own(step, width), spec_rows(step, width), spec_rows(step, out_width), spec_whole((8, width))),
        [pltpu.VMEM((width, out_width), LOW), pltpu.SemaphoreType.DMA((16,))],
        grid=(4,),
        limit=60,
    )


def finish_kernel(place_ref, g_ref, mine_ref, other_ref, out_ref):
    z, y, x = place_ref[0], place_ref[1], place_ref[2]
    turn = x == 1
    for block in range(8):
        zb, yb = block // 2, block % 2
        source = pl.multiple_of((((zb + 4 - z) % 4) * 2 + (yb + y) % 2) * 128, 128)
        cols = pl.ds(source, 128)
        part = g_ref[:, cols] + mine_ref[:, cols].astype(WIDE) + other_ref[:, cols].astype(WIDE)
        out_ref[:, block * 128 : block * 128 + 128] = jnp.where(turn, pltpu.roll(part, 64, 1), part)


def finish(grad, mine, other):
    if not gridded():
        return grad + mine.astype(WIDE) + other.astype(WIDE)
    rows, width = grad.shape
    return call(
        finish_kernel,
        shaped((rows, width), WIDE),
        (grid_place(), grad, mine, other),
        [pl.BlockSpec(memory_space=pltpu.SMEM)] + [vmem_spec()] * 3,
        vmem_spec(),
        bytes_moved=12 * rows * width,
        limit=60,
    )


def small_kernel(*refs):
    vectors, heads, (out_ref, rows_ref) = refs[:10], refs[10:13], refs[13:]
    rows_ref[...] = jnp.zeros_like(rows_ref)
    for i, ref in enumerate(vectors):
        rows_ref[i : i + 1, : ref.shape[1]] = ref[...]
    out_ref[...] = jnp.zeros_like(out_ref)
    out_ref[:16, :128] = rows_ref[...].astype(LOW)
    for i, ref in enumerate(heads):
        out_ref[16 : 16 + ref.shape[0], 128 * i : 128 * i + ref.shape[1]] = ref[...].astype(LOW)


def small_pack(vectors, heads):
    piece = heads[0].shape[0]
    ins = [v.reshape(1, -1) for v in vectors] + list(heads)
    return call(
        small_kernel,
        shaped((16 + piece, 384), LOW),
        ins,
        [vmem_spec()] * len(ins),
        vmem_spec(),
        [pltpu.VMEM((16, 128), WIDE)],
        bytes_moved=100000,
        limit=60,
    )


def pack_rows_kernel(spot_ref, q_ref, k_ref, v_ref, o_ref, mine_ref, other_ref, out_ref):
    first = spot_ref[3] == 0
    width = q_ref.shape[1]
    for i, ref in enumerate((q_ref, k_ref, v_ref, o_ref)):
        out_ref[:, i * width : i * width + width] = ref[...].astype(LOW)
    piece = out_ref.shape[0] // 2
    mine, other = mine_ref[:16, :128].astype(WIDE), other_ref[:16, :128].astype(WIDE)
    zero, one = jnp.where(first, mine, other), jnp.where(first, other, mine)
    lane = lax.broadcasted_iota(jnp.int32, zero.shape, 1)
    row = lax.broadcasted_iota(jnp.int32, zero.shape, 0)
    both = jnp.where(lane < piece, zero, pltpu.roll(one, piece, 1))
    both = jnp.where(row == 9, zero, jnp.where(row == 10, pltpu.roll(one, 1, 0), both))
    out_ref[:16, 4 * width :] = both.astype(LOW)
    out_ref[16:, 4 * width :] = jnp.zeros((2 * piece - 16, 128), LOW)


def pack_rows(spot, weights, mine, other):
    rows, width = weights[0].shape
    return call(
        pack_rows_kernel,
        shaped((rows, 4 * width + 128), LOW),
        (spot, *weights, mine, other),
        [pl.BlockSpec(memory_space=pltpu.SMEM)] + [vmem_spec()] * 6,
        vmem_spec(),
        bytes_moved=18 * rows * width,
        limit=60,
    )


def pack_heads_kernel(spot_ref, up_ref, down_ref, mine_ref, other_ref, out_ref):
    first = spot_ref[3] == 0
    width = 2 * up_ref.shape[1]
    piece = out_ref.shape[0] // 2
    out_ref[:, : width // 2] = up_ref[...].astype(LOW)
    out_ref[:, width // 2 : width] = down_ref[...].astype(LOW)
    mine, other = mine_ref[16:], other_ref[16:]
    out_ref[:piece, width:] = jnp.where(first, mine, other)
    out_ref[piece:, width:] = jnp.where(first, other, mine)


def pack_heads(spot, up, down, mine, other):
    rows, width = up.shape
    return call(
        pack_heads_kernel,
        shaped((rows, 2 * width + 384), LOW),
        (spot, up, down, mine, other),
        [pl.BlockSpec(memory_space=pltpu.SMEM)] + [vmem_spec()] * 4,
        vmem_spec(),
        bytes_moved=6 * rows * width,
        limit=60,
    )


def vectors_kernel(first, spot_ref, *refs):
    pieces, (vec_ref, qkv_ref, up_ref, low_buffer, rows_ref, sems) = refs[:16], refs[16:]
    z, y, x, core = spot_ref[0], spot_ref[1], spot_ref[2], spot_ref[3]
    copies = []
    for i, piece in enumerate(pieces):
        copy = pltpu.make_async_copy(
            piece.at[0:16, first : first + 128], low_buffer.at[16 * i : 16 * i + 16], sems.at[i]
        )
        copy.start()
        copies.append(copy)
    for copy in copies:
        copy.wait()
    rows_ref[...] = low_buffer[...].astype(WIDE)
    lane = lax.broadcasted_iota(jnp.int32, (16, 128), 1)
    for j in range(8):
        even, odd = rows_ref[32 * j : 32 * j + 16], rows_ref[32 * j + 16 : 32 * j + 32]
        vec_ref[:, 128 * j : 128 * j + 128] = jnp.where(lane < 64, even, pltpu.roll(odd, 64, 1))
    turn = x == 1
    blocks = qkv_ref.shape[1] // 384
    for b in range(blocks):
        source = ((core * 2 + b // 2 + 4 - z) % 4) * 2 + (b % 2 + y) % 2
        part = vec_ref[:, pl.ds(pl.multiple_of(source * 128, 128), 128)]
        part = jnp.where(turn, pltpu.roll(part, 64, 1), part)
        for j in range(3):
            at = (j * blocks + b) * 128
            qkv_ref[:, at : at + 128] = part[j : j + 1]
    for j in range(8):
        key = (((core * 2 + j // 4 + 4 - z) % 4) * 2 + (j // 2 % 2 + y) % 2) * 2 + (j % 2 + x) % 2
        for t in range(2):
            at = j * 256 + t * 128
            up_ref[:, at : at + 128] = rows_ref[pl.ds(key * 16 + 9 + t, 1), :]


def read_vectors(spot, pieces, first, width, head_width, hidden):
    return call(
        functools.partial(vectors_kernel, first),
        (shaped((16, width), WIDE), shaped((1, 3 * head_width), WIDE), shaped((1, hidden), WIDE)),
        (spot, *pieces),
        [pl.BlockSpec(memory_space=pltpu.SMEM)] + [any_spec()] * 16,
        (vmem_spec(),) * 3,
        [pltpu.VMEM((256, 128), LOW), pltpu.VMEM((256, 128), WIDE), pltpu.SemaphoreType.DMA((16,))],
        bytes_moved=200000,
        limit=60,
    )


def sums_kernel(zero_ref, one_ref, up_ref, out_ref, rows_ref):
    rows_ref[...] = jnp.zeros_like(rows_ref)
    half = zero_ref.shape[1]
    rows_ref[0:3, :half] = zero_ref[...]
    rows_ref[0:3, half : 2 * half] = one_ref[...]
    rows_ref[3:4, :] = up_ref[...]
    out_ref[...] = rows_ref[...].astype(LOW)


def pack_sums(zero, one, up):
    width = up.shape[1]
    return call(
        sums_kernel,
        shaped((16, width), LOW),
        (zero, one, up),
        [vmem_spec()] * 3,
        vmem_spec(),
        [pltpu.VMEM((16, width), WIDE)],
        bytes_moved=100000,
        limit=60,
    )


def vector_grads_kernel(share, spot_ref, mine_ref, other_ref, mid_ref, top_ref, out_ref, plain, long, block):
    z, y, x, core = spot_ref[0], spot_ref[1], spot_ref[2], spot_ref[3]
    turn = x == 1
    half = plain.shape[1] // 2
    hidden = mine_ref.shape[1]
    mine, other = mine_ref[...].astype(WIDE), other_ref[...].astype(WIDE)
    for i in range(2):
        side = jnp.where(core == i, mine, other)
        plain[:, i * half : i * half + half] = side[:8, :half]
        long[:, i * hidden : i * hidden + hidden] = side[3:4]
    out_ref[...] = jnp.zeros_like(out_ref)
    for j in range(8):
        source = ((j // 2 + z) % 4) * 2 + (j % 2 + y) % 2
        part = plain[:, pl.ds(pl.multiple_of(source * 128, 128), 128)]
        part = jnp.where(turn, pltpu.roll(part, 64, 1), part)
        cols = slice(128 * j, 128 * j + 128)
        block[0:3, :] = part[0:3]
        block[3:4, :] = mid_ref[0:1, cols]
        block[4:5, :] = top_ref[0:1, cols]
        block[5:7, :] = mid_ref[1:3, cols]
        block[7:9, :] = top_ref[1:3, cols]
        block[9:16, :] = jnp.zeros((7, 128), WIDE)
        pair = block[...]
        for odd in range(2):
            owner = source * 2 + (odd + x) % 2
            block[...] = pltpu.roll(pair, 64, 1) if odd else pair
            for t in range(2):
                wide_row = long[:, pl.ds(pl.multiple_of(owner * 256 + t * 128, 128), 128)]
                block[9 + 2 * t : 10 + 2 * t, :] = wide_row
                block[10 + 2 * t : 11 + 2 * t, :] = pltpu.roll(wide_row, 64, 1)
            at = (2 * j + odd) * 64
            out_ref[at : at + 16, share - 64 : share] = jnp.where(core == 1, block[:, :64], 0.0).astype(LOW)


def spread_vector_grads(spot, mine, other, mid_sums, top_sums, share):
    width = mid_sums.shape[1]
    hidden = mine.shape[1]
    return call(
        functools.partial(vector_grads_kernel, share),
        shaped((width, share), LOW),
        (spot, mine, other, mid_sums, top_sums),
        [pl.BlockSpec(memory_space=pltpu.SMEM)] + [vmem_spec()] * 4,
        vmem_spec(),
        [pltpu.VMEM((8, width), WIDE), pltpu.VMEM((1, 2 * hidden), WIDE), pltpu.VMEM((16, 128), WIDE)],
        bytes_moved=400000,
        limit=60,
    )


def local(
    hidden_in,
    segment_ids,
    positions,
    query_weight,
    key_weight,
    value_weight,
    output_weight,
    up_weight,
    down_weight,
    query_bias,
    key_bias,
    value_bias,
    output_bias,
    up_bias,
    down_bias,
    attn_gain,
    attn_shift,
    ffn_gain,
    ffn_shift,
    proj_wide,
    proj_mid,
    proj_narrow,
    cot_wide,
    cot_mid,
    cot_narrow,
):
    tp_rank = lax.axis_index("tp")
    own_rows, width = hidden_in.shape
    head_width = query_weight.shape[1]
    heads_here = head_width // HD
    hidden_here = up_weight.shape[1]
    piece = query_bias.shape[0]
    low, wide = LOW, WIDE
    half = head_width // 2
    half_heads = heads_here // 2

    spot = jnp.concatenate([grid_place(), tp_rank[None].astype(jnp.int32)])
    first_core = tp_rank == 0

    small = small_pack(
        (
            query_bias, key_bias, value_bias, output_bias, down_bias,
            attn_gain, attn_shift, ffn_gain, ffn_shift, up_bias,
        ),
        (proj_wide, proj_mid, proj_narrow),
    )
    small_other = other_core(small)
    attn_weights = (query_weight, key_weight, value_weight, output_weight.T)
    if gridded():
        attn_group = Gather(pack_rows(spot, attn_weights, small, small_other))
        ffn_group = Gather(pack_heads(spot, up_weight, down_weight.T, small, small_other))
    else:
        small_zero = jnp.where(first_core, small, small_other)
        small_one = jnp.where(first_core, small_other, small)
        attn_group = Gather(pack([*attn_weights, jnp.zeros((2 * piece, 128), low)]))
        heads_pair = jnp.concatenate([small_zero[16:], small_one[16:]], axis=0)
        ffn_group = Gather(pack([up_weight, down_weight.T, heads_pair]))
    queue = Queue()
    queue.add(attn_group, range(3))
    queue.add(attn_group, range(3, 6), *queue.at(0, 1, 2))

    tags = after(jnp.stack([segment_ids, positions]), *queue.at(1))
    tags = jnp.concatenate([tags, other_core(tags)], axis=1)
    hidden_other = other_core(after(hidden_in, *queue.at(0)))
    x_all = reorder(jnp.concatenate([hidden_in, hidden_other], axis=0), False)
    cot_own = jnp.concatenate(
        [cot_wide, jnp.pad(cot_mid, ((0, 0), (0, 128 - cot_mid.shape[1]))), jnp.pad(cot_narrow, ((0, 0), (0, 128 - cot_narrow.shape[1])))],
        axis=1,
    )
    cot_all = jnp.concatenate([cot_own, other_core(after(cot_own, *queue.at(3)))], axis=0)
    column, row = tags[0].reshape(-1, 1), tags[0].reshape(1, -1)
    cos_table, sin_table = rope_tables(tags[1], HD)
    cos_table = jnp.concatenate([cos_table, cos_table], axis=1)
    sin_table = jnp.concatenate([-sin_table[:, : HD // 2], sin_table[:, HD // 2 :]] * 2, axis=1)

    queue.add(attn_group, range(6, 9), places=4)
    queue.add(attn_group, range(9, 12), x_all, cot_all, cos_table, sin_table, places=4)
    queue.add(attn_group, range(12, 15), places=4)
    queue.add(ffn_group, range(3), *queue.at(12, 13, 14))
    attn_pieces = attn_group.pieces()
    if gridded():
        vectors, qkv_shift, up_shift = read_vectors(
            spot, attn_pieces, 4 * head_width, width, head_width, hidden_here
        )
    else:
        pair = jnp.stack([small_zero[:16, :128], small_one[:16, :128]])
        pair = lax.all_gather(pair[None], "fsdp", axis=0, tiled=True).astype(wide)
        vectors = pair[..., :piece].transpose(2, 0, 1, 3).reshape(16, width)
        qkv_shift = lax.dynamic_slice_in_dim(vectors[:3], tp_rank * head_width, head_width, 1).reshape(1, -1)
        up_shift = lax.dynamic_slice_in_dim(
            pair[:, :, 9, : 4 * piece].reshape(1, -1), tp_rank * hidden_here, hidden_here, 1
        )

    query, key, value = project_qkv(x_all, qkv_shift, cos_table, sin_table, attn_pieces, head_width)
    first_half = attend(query, key, value, column, row, 0, half_heads)
    queue.add(ffn_group, range(3, 6), first_half[0], *queue.at(15, 16, 17))
    second_half = attend(after(query, first_half[0], *queue.at(15, 16, 17)), key, value, column, row, 1, half_heads)
    contexts, probs = zip(first_half, second_half)
    (attn_mine,) = spread(contexts, attn_pieces, 3 * head_width, head_width)
    unit_one, inv_one, mid_low = first_norm(
        x_all, attn_mine, other_core(after(attn_mine, *queue.at(18, 19, 20))), vectors
    )
    queue.add(ffn_group, range(6, 9), attn_mine, *queue.at(18, 19, 20))
    queue.add(ffn_group, range(9, 15), places=4)
    ffn_pieces = ffn_group.pieces()
    act_low, slope, ffn_mine = feed(mid_low, up_shift, ffn_pieces, 0, hidden_here, hidden_here)
    embed_wide, embed_mid, embed_narrow, grad_top, grad_top_low, top_low, top_sums = second_norm(
        unit_one, ffn_mine, other_core(ffn_mine), vectors, cot_all, ffn_pieces, 2 * hidden_here,
        (proj_wide.shape[1], proj_mid.shape[1], proj_narrow.shape[1]),
    )

    share = 192
    cot_share = lax.dynamic_slice_in_dim(cot_all, tp_rank * share, share, 1)
    grad_hidden_low, up_sums, mid_mine = feed_back(grad_top_low, slope, ffn_pieces, 0, hidden_here)
    mid_other = other_core(mid_mine)
    ffn_scatter = Scatter(fold([(after(grad_top_low, mid_mine), [act_low]), (mid_low, [grad_hidden_low])]))
    back = Queue()
    back.add(ffn_scatter, (0, 1, 2, 4, 3))
    grad_own, grad_mid_low, grad_context, mid_sums = middle_back(
        grad_top, mid_mine, mid_other, unit_one, inv_one, vectors, attn_pieces, 3 * head_width, head_width
    )
    back.add(ffn_scatter, (5,), grad_context)
    backs = []
    for i in range(2):
        ready = [backs[0][0]] if i else back.at(0, 1, 2)
        backs.append(
            attend_back(query, key, value, after(grad_context, *ready), probs[i], cos_table, sin_table, i, half_heads)
        )
        back.add(ffn_scatter, (8, 9) if i else (6, 7), backs[i][0])
    grads = [backs[i][j] for j in range(3) for i in range(2)]
    sums = pack_sums(backs[0][3], backs[1][3], up_sums)
    sums_other = other_core(sums)
    if gridded():
        extra = spread_vector_grads(spot, sums, sums_other, mid_sums, top_sums, share)
    else:
        extra = jnp.zeros((width, share), low)
    attn_scatter = Scatter(
        fold([(after(x_all, *back.at(3, 4, 5)), grads), (grad_mid_low, list(contexts)), (top_low, [cot_share])], extra)
    )
    back.add(attn_scatter, (0, 1, 2))
    back.add(ffn_scatter, (10,), attn_scatter.held[OWN])
    x_mine, x_sent = spread([after(grads[0], attn_scatter.held[OWN], *back.at(7, 8))] + grads[1:], attn_pieces, 0, 3 * head_width, 2)
    back.add(ffn_scatter, (11, 12), x_mine)
    back.add(attn_scatter, (3, 4), x_mine)
    x_other = other_core(x_sent)
    grad_hidden = finish(grad_own, x_mine, x_other)
    for group, number in (
        (attn_scatter, 5), (attn_scatter, 6), (ffn_scatter, 13), (attn_scatter, 7), (attn_scatter, 8), (ffn_scatter, 14),
    ):
        back.add(group, (number,), places=5)
    back.add(attn_scatter, range(9, 15), places=5)
    ffn_part = ffn_scatter.rows()
    attn_part = attn_scatter.rows()

    small_part = attn_part[:, 4 * head_width :]
    small_away = other_core(small_part)
    joined = jnp.where(
        first_core,
        jnp.concatenate([small_part, small_away], axis=1),
        jnp.concatenate([small_away, small_part], axis=1),
    ).astype(wide)
    own_heads = lax.dynamic_slice_in_dim(joined, tp_rank * piece, piece, 0)
    if gridded():
        block = joined[:16, 2 * share - 64 :]
        own_vectors = lax.dynamic_slice_in_dim(block[:9], tp_rank * piece, piece, 1)
        own_up = lax.dynamic_slice_in_dim(block, 9 + 2 * tp_rank, 2, 0).reshape(-1)
    else:
        both = jnp.concatenate(
            [
                jnp.where(first_core, sums, sums_other)[:3, :head_width],
                jnp.where(first_core, sums_other, sums)[:3, :head_width],
            ],
            axis=1,
        ).astype(wide)
        table = jnp.concatenate(
            [both, mid_sums[:1], top_sums[:1], mid_sums[1:3], top_sums[1:3], jnp.zeros((7, width), wide)], axis=0
        )
        table = lax.psum_scatter(table, "fsdp", scatter_dimension=1, tiled=True)
        own_vectors = lax.dynamic_slice_in_dim(table, tp_rank * piece, piece, 1)
        long = lax.dynamic_update_slice_in_dim(
            jnp.zeros((2 * hidden_here,), wide), up_sums.reshape(-1), tp_rank * hidden_here, 0
        )
        own_up = lax.psum_scatter(long, ("fsdp", "tp"), scatter_dimension=0, tiled=True)
    attn_part = attn_part.astype(wide)
    return (
        embed_wide,
        embed_mid,
        embed_narrow,
        grad_hidden,
        attn_part[:, :head_width],
        attn_part[:, head_width : 2 * head_width],
        attn_part[:, 2 * head_width : 3 * head_width],
        attn_part[:, 3 * head_width : 4 * head_width].T,
        ffn_part[:, hidden_here:].astype(wide),
        ffn_part[:, :hidden_here].astype(wide).T,
        own_vectors[0],
        own_vectors[1],
        own_vectors[2],
        own_vectors[3],
        own_up,
        own_vectors[4],
        own_vectors[5],
        own_vectors[6],
        own_vectors[7],
        own_vectors[8],
        own_heads[:, : proj_wide.shape[1]],
        own_heads[:, 128 : 128 + proj_mid.shape[1]],
        own_heads[:, 256 : 256 + proj_narrow.shape[1]],
    )


def solution(mesh):
    return jax.shard_map(
        local,
        mesh=mesh,
        in_specs=(
            P(("fsdp", "tp"), None),
            P(("fsdp", "tp")),
            P(("fsdp", "tp")),
            P("fsdp", "tp"),
            P("fsdp", "tp"),
            P("fsdp", "tp"),
            P("tp", "fsdp"),
            P("fsdp", "tp"),
            P("tp", "fsdp"),
            P(("fsdp", "tp")),
            P(("fsdp", "tp")),
            P(("fsdp", "tp")),
            P(("fsdp", "tp")),
            P(("fsdp", "tp")),
            P(("fsdp", "tp")),
            P(("fsdp", "tp")),
            P(("fsdp", "tp")),
            P(("fsdp", "tp")),
            P(("fsdp", "tp")),
            P(("fsdp", "tp"), None),
            P(("fsdp", "tp"), None),
            P(("fsdp", "tp"), None),
            P(("fsdp", "tp"), None),
            P(("fsdp", "tp"), None),
            P(("fsdp", "tp"), None),
        ),
        out_specs=(
            P(("fsdp", "tp"), None),
            P(("fsdp", "tp"), None),
            P(("fsdp", "tp"), None),
            P(("fsdp", "tp"), None),
            P("fsdp", "tp"),
            P("fsdp", "tp"),
            P("fsdp", "tp"),
            P("tp", "fsdp"),
            P("fsdp", "tp"),
            P("tp", "fsdp"),
            P(("fsdp", "tp")),
            P(("fsdp", "tp")),
            P(("fsdp", "tp")),
            P(("fsdp", "tp")),
            P(("fsdp", "tp")),
            P(("fsdp", "tp")),
            P(("fsdp", "tp")),
            P(("fsdp", "tp")),
            P(("fsdp", "tp")),
            P(("fsdp", "tp")),
            P(("fsdp", "tp"), None),
            P(("fsdp", "tp"), None),
            P(("fsdp", "tp"), None),
        ),
        check_vma=False,
    )
```

```python
import functools
import math

import jax
import jax.numpy as jnp
from jax import lax
from jax.experimental import pallas as pl
from jax.experimental.pallas import tpu as pltpu
from jax.sharding import PartitionSpec as P

HD = 64
SEQ_LEN = 512


EPSILON = 1e-05
MASKED_SCORE = -1e30
ROPE_BASE = 10000.0


def rope_tables(places, head_width):
    half_width = head_width // 2
    inv_freq = jnp.exp(
        jnp.arange(half_width, dtype=jnp.float32) * (-2.0 * math.log(ROPE_BASE) / head_width)
    )
    angles = places.astype(jnp.float32)[:, None] * inv_freq[None, :]
    cos_table = jnp.cos(angles)
    sin_table = jnp.sin(angles)
    return (
        jnp.concatenate([cos_table, cos_table], axis=-1),
        jnp.concatenate([sin_table, sin_table], axis=-1),
    )


def product_tn(left_side, right_side):
    return lax.dot_general(
        left_side, right_side, (((0,), (0,)), ((), ())), preferred_element_type=jnp.float32
    )

GATHERED = (
    ("z", (3, 0, 0)), ("x", (0, 0, 1)), ("y", (0, 1, 0)),
    ("z", (2, 0, 0)), ("x", (3, 0, 1)), ("y", (3, 1, 0)),
    ("z", (1, 0, 0)), ("x", (2, 0, 1)), ("y", (3, 1, 1)),
    ("z", (2, 1, 0)), ("x", (0, 1, 1)), ("y", (2, 1, 1)),
    ("x", (1, 0, 1)), ("y", (1, 1, 0)), ("z", (1, 1, 1)),
)
SCATTERED = (
    ("z", (1, 1, 1)), ("x", (1, 0, 1)), ("y", (1, 1, 0)), ("x", (0, 1, 1)),
    ("z", (2, 1, 0)), ("y", (2, 1, 1)), ("z", (1, 0, 0)), ("y", (3, 1, 1)),
    ("x", (2, 0, 1)), ("y", (3, 1, 0)), ("x", (3, 0, 1)), ("z", (2, 0, 0)),
    ("x", (0, 0, 1)), ("y", (0, 1, 0)), ("z", (3, 0, 0)),
)
KEYS = tuple((z, y, x) for z in range(4) for y in range(2) for x in range(2))
OWN = (0, 0, 0)


def place(z, y, x):
    return (z * 2 + y) * 2 + x


def hop(link):
    def target(z, y, x):
        if link == "x":
            return place(z, y, 1 - x)
        if link == "y":
            return place(z, 1 - y, x)
        return place((z + 1) % 4, y, x)

    return [(place(*k), target(*k)) for k in KEYS]


HOPS = {link: hop(link) for link in "xyz"}
BACK = {link: [(b, a) for a, b in pairs] for link, pairs in HOPS.items()}


def sender_key(key, link):
    z, y, x = key
    if link == "x":
        return (z, y, 1 - x)
    if link == "y":
        return (z, 1 - y, x)
    return ((z + 1) % 4, y, x)


def gridded():
    return lax.axis_size("fsdp") == 16


def after(values, *others):
    return lax.optimization_barrier((values, others))[0] if others else values


class Gather:
    def __init__(self, shard):
        self.have = {OWN: shard}

    def start(self, number, *others):
        link, key = GATHERED[number]
        send = self.have[sender_key(key, link)]
        if others:
            send = after(send, *others)
        self.have[key] = lax.ppermute(send, "fsdp", HOPS[link])
        return self.have[key]

    def pieces(self):
        if not gridded():
            full = lax.all_gather(self.have[OWN], "fsdp", axis=0, tiled=True)
            rows = full.shape[0] // 16
            return [full[rows * i : rows * (i + 1)] for i in range(16)]
        return [self.have[key] for key in KEYS]


class Scatter:
    def __init__(self, pieces):
        self.held = dict(zip(KEYS, pieces))
        self.parts = {key: [] for key in KEYS}

    def total(self, key, *others):
        return sum(after(self.parts[key], *others), after(self.held[key], *others))

    def start(self, number, *others):
        link, key = SCATTERED[number]
        part = lax.ppermute(self.total(key, *others), "fsdp", BACK[link])
        self.parts[sender_key(key, link)].append(part)
        return part

    def rows(self):
        if not gridded():
            full = jnp.concatenate([self.held[key] for key in KEYS], axis=0)
            return lax.psum_scatter(full, "fsdp", scatter_dimension=0, tiled=True)
        return self.total(OWN)


class Queue:
    def __init__(self):
        self.landed = []

    def add(self, group, numbers, *others, places=0):
        if gridded():
            for number in numbers:
                tied = self.landed[-places : len(self.landed) - places + 1] if places else []
                self.landed.append(group.start(number, *others, *tied))

    def at(self, *indices):
        return [self.landed[i] for i in indices if gridded()]


def other_core(values):
    return lax.ppermute(values, "tp", [(0, 1), (1, 0)])


def reorder_kernel(inverse, place_ref, in_ref, out_ref):
    z, y, x = place_ref[0], place_ref[1], place_ref[2]
    turn = x == 1
    for block in range(8):
        zb, yb = block // 2, block % 2
        away = (zb + 4 - z) % 4 if inverse else (zb + z) % 4
        source = pl.multiple_of((away * 2 + (yb + y) % 2) * 128, 128)
        part = in_ref[:, pl.ds(source, 128)].astype(jnp.float32)
        part = jnp.where(turn, pltpu.roll(part, 64, 1), part)
        out_ref[:, block * 128 : block * 128 + 128] = part.astype(out_ref.dtype)


def grid_place():
    me = lax.axis_index("fsdp")
    return jnp.stack([me // 4, (me // 2) % 2, me % 2]).astype(jnp.int32)


def reorder(values, inverse):
    if not gridded():
        return values
    places = grid_place()
    return pl.pallas_call(
        functools.partial(reorder_kernel, inverse),
        out_shape=jax.ShapeDtypeStruct(values.shape, values.dtype),
        in_specs=[
            pl.BlockSpec(memory_space=pltpu.SMEM),
            pl.BlockSpec(memory_space=pltpu.VMEM),
        ],
        out_specs=pl.BlockSpec(memory_space=pltpu.VMEM),
    )(places, values)


def halves(values):
    first = lax.axis_index("tp") == 0
    other = other_core(values)
    return jnp.concatenate(
        [jnp.where(first, values, other), jnp.where(first, other, values)], axis=0
    )


def vmem_spec():
    return pl.BlockSpec(memory_space=pltpu.VMEM)


def any_spec():
    return pl.BlockSpec(memory_space=pl.ANY)


def call(body, outs, ins, specs, out_specs, scratch=(), grid=None, limit=60, flops=0, bytes_moved=0):
    extra = {} if grid is None else {"grid": grid}
    return pl.pallas_call(
        body,
        name=getattr(body, "func", body).__name__,
        out_shape=outs,
        in_specs=specs,
        out_specs=out_specs,
        scratch_shapes=list(scratch),
        compiler_params=pltpu.CompilerParams(vmem_limit_bytes=limit * 1024 * 1024),
        cost_estimate=pl.CostEstimate(flops=1000, bytes_accessed=1000, transcendentals=0),
        **extra,
    )(*ins)


def shaped(shape, kind):
    return jax.ShapeDtypeStruct(shape, kind)


LOW, WIDE = jnp.bfloat16, jnp.float32


def dot(a, b):
    return jnp.dot(a, b, preferred_element_type=WIDE)


def dot_nt(a, b):
    return lax.dot_general(a, b, (((1,), (1,)), ((), ())), preferred_element_type=WIDE)


def dot_tn(a, b):
    return lax.dot_general(a, b, (((0,), (0,)), ((), ())), preferred_element_type=WIDE)


def fetch(pieces, columns, buffer, sems):
    rows = pieces[0].shape[0]
    copies = []
    for i, piece in enumerate(pieces):
        copy = pltpu.make_async_copy(
            piece.at[:, columns[0] : columns[1]], buffer.at[i * rows : (i + 1) * rows], sems.at[i]
        )
        copy.start()
        copies.append(copy)

    def ready(first, last):
        for copy in copies[first:last]:
            copy.wait()

    return ready


def pack_kernel(count, *refs):
    out_ref, at = refs[count], 0
    for ref in refs[:count]:
        size = ref.shape[1]
        out_ref[:, at : at + size] = ref[...].astype(LOW)
        at += size


def pack(arrays):
    rows = arrays[0].shape[0]
    total = sum(a.shape[1] for a in arrays)
    return call(
        functools.partial(pack_kernel, len(arrays)),
        shaped((rows, total), LOW),
        arrays,
        [vmem_spec() for _ in arrays],
        vmem_spec(),
        bytes_moved=rows * total * 6,
        limit=60,
    )


def flip(values):
    width = values.shape[1]
    lane = lax.broadcasted_iota(jnp.int32, values.shape, 1)
    return jnp.where(
        lane % HD < HD // 2, pltpu.roll(values, width - HD // 2, 1), pltpu.roll(values, HD // 2, 1)
    )


def tile_lanes(table, width):
    return jnp.concatenate([table] * (width // table.shape[1]), axis=1)


def qkv_kernel(x_ref, shift_ref, cos_ref, sin_ref, *refs):
    pieces, (q_ref, k_ref, v_ref, buffer, sems) = refs[:16], refs[16:]
    width = q_ref.shape[1]
    ready = fetch(pieces, (0, 3 * width), buffer, sems)
    ready(0, 16)
    chunk = min(256, width)
    cos_table, sin_table = tile_lanes(cos_ref[...], chunk), tile_lanes(sin_ref[...], chunk)
    for which, out_ref in enumerate((q_ref, k_ref, v_ref)):
        for at in range(0, width, chunk):
            first = which * width + at
            pre = dot(x_ref[...], buffer[:, first : first + chunk]) + shift_ref[:, first : first + chunk]
            if which < 2:
                pre = pre * cos_table + flip(pre) * sin_table
            if which == 0:
                pre = pre.astype(LOW).astype(WIDE) * (HD ** -0.5)
            out_ref[:, at : at + chunk] = pre.astype(LOW)


def project_qkv(x_all, shift, cos_table, sin_table, pieces, width):
    rows, depth = x_all.shape
    out = shaped((rows, width), LOW)
    return call(
        qkv_kernel,
        (out, out, out),
        (x_all, shift, cos_table, sin_table, *pieces),
        [vmem_spec()] * 4 + [any_spec()] * 16,
        (vmem_spec(),) * 3,
        [pltpu.VMEM((depth, 3 * width), LOW), pltpu.SemaphoreType.DMA((16,))],
        flops=2 * rows * depth * 3 * width,
        bytes_moved=2 * (3 * depth * width + rows * depth),
        limit=60,
    )


def attend_kernel(heads, q_ref, k_ref, v_ref, column_ref, row_ref, ctx_ref, prob_ref, mask_ref):
    mask_ref[...] = jnp.where(column_ref[...] == row_ref[...], 0.0, MASKED_SCORE)

    def pair(i, _):
        wide = pl.ds(pl.multiple_of(i * 2 * HD, 2 * HD), 2 * HD)
        q, k = q_ref[:, wide], k_ref[:, wide]
        flat = v_ref[:, wide].astype(WIDE).T.astype(LOW)
        parts = []
        for j in range(2):
            cols = slice(j * HD, j * HD + HD)
            scores = dot_nt(k[:, cols], q[:, cols]) + mask_ref[...]
            top = jnp.max(scores, axis=0, keepdims=True)
            raised = jnp.exp(scores - top)
            total = jnp.sum(raised, axis=0, keepdims=True)
            prob = (raised * (1.0 / total)).astype(LOW)
            prob_ref[2 * i + j] = prob
            parts.append(dot(flat[cols], prob))
        ctx_ref[:, wide] = jnp.concatenate(parts, axis=0).T.astype(LOW)
        return 0

    lax.fori_loop(0, heads // 2, pair, 0)


def attend(query, key, value, column, row, first, heads):
    rows = query.shape[0]
    width = heads * HD
    block = pl.BlockSpec((rows, width), lambda i: (0, first))
    whole = lambda shape: pl.BlockSpec(shape, lambda i: (0,) * len(shape))
    return call(
        functools.partial(attend_kernel, heads),
        (shaped((rows, width), LOW), shaped((heads, rows, rows), LOW)),
        (query, key, value, column, row),
        [block] * 3 + [whole((rows, 1)), whole((1, rows))],
        (whole((rows, width)), whole((heads, rows, rows))),
        [pltpu.VMEM((rows, rows), WIDE)],
        grid=(1,),
        flops=4 * heads * rows * rows * HD,
        bytes_moved=2 * heads * rows * rows,
        limit=60,
    )


def attend_back_kernel(heads, q_ref, k_ref, v_ref, g_ref, prob_ref, cos_ref, sin_ref, gq_ref, gk_ref, gv_ref, sums_ref):
    cos_table, sin_table = cos_ref[...], sin_ref[...]

    def pair(i, _):
        wide = pl.ds(pl.multiple_of(i * 2 * HD, 2 * HD), 2 * HD)
        q, k, v, g = q_ref[:, wide], k_ref[:, wide], v_ref[:, wide], g_ref[:, wide]
        key_flat = k.astype(WIDE).T.astype(LOW)
        q_parts, k_parts, v_parts = [], [], []
        for j in range(2):
            cols = slice(j * HD, j * HD + HD)
            prob = prob_ref[2 * i + j]
            prob_wide = prob.astype(WIDE)
            grad = dot_nt(v[:, cols], g[:, cols])
            delta = jnp.sum(prob_wide * grad, axis=0, keepdims=True)
            raw = (prob_wide * (grad - delta)).astype(LOW)
            v_parts.append(dot(prob, g[:, cols]))
            k_parts.append(dot(raw, q[:, cols]))
            q_parts.append(dot(key_flat[cols], raw))
        gq = jnp.concatenate(q_parts, axis=0).T * (HD ** -0.5)
        gk = jnp.concatenate(k_parts, axis=1)
        gv = jnp.concatenate(v_parts, axis=1)
        gq = (gq * cos_table - flip(gq) * sin_table).astype(LOW)
        gk = (gk * cos_table - flip(gk) * sin_table).astype(LOW)
        gv = gv.astype(LOW)
        for n, (ref, value) in enumerate(((gq_ref, gq), (gk_ref, gk), (gv_ref, gv))):
            ref[:, wide] = value
            sums_ref[n : n + 1, wide] = jnp.sum(value.astype(WIDE), axis=0, keepdims=True)
        return 0

    lax.fori_loop(0, heads // 2, pair, 0)


def attend_back(query, key, value, grad_ctx, prob, cos_table, sin_table, first, heads):
    rows = query.shape[0]
    width = heads * HD
    block = pl.BlockSpec((rows, width), lambda i: (0, first))
    whole = lambda shape: pl.BlockSpec(shape, lambda i: (0,) * len(shape))
    out = shaped((rows, width), LOW)
    return call(
        functools.partial(attend_back_kernel, heads),
        (out, out, out, shaped((3, width), WIDE)),
        (query, key, value, grad_ctx, prob, cos_table, sin_table),
        [block] * 4 + [whole(prob.shape), whole(cos_table.shape), whole(sin_table.shape)],
        (whole((rows, width)),) * 3 + (whole((3, width)),),
        grid=(1,),
        flops=8 * heads * rows * rows * HD,
        bytes_moved=2 * heads * rows * rows,
        limit=60,
    )


def spread_kernel(count, parts, first, width, *refs):
    lefts, pieces, refs = refs[:count], refs[count : count + 16], refs[count + 16 :]
    outs, (buffer, sems) = refs[:parts], refs[parts:]
    ready = fetch(pieces, (first, first + width), buffer, sems)
    left = lefts[0][...] if count == 1 else jnp.concatenate([ref[...] for ref in lefts], axis=1)
    step = buffer.shape[0] // 2
    for i in range(2):
        ready(8 * i, 8 * i + 8)
        value = dot_nt(left, buffer[i * step : i * step + step]).astype(LOW)
        for k, out_ref in enumerate(outs):
            out_ref[:, i * step : i * step + step] = value[k * out_ref.shape[0] : (k + 1) * out_ref.shape[0]]


def spread(lefts, pieces, first, width, parts=1):
    rows = lefts[0].shape[0]
    depth = 16 * pieces[0].shape[0]
    return call(
        functools.partial(spread_kernel, len(lefts), parts, first, width),
        (shaped((rows // parts, depth), LOW),) * parts,
        (*lefts, *pieces),
        [vmem_spec()] * len(lefts) + [any_spec()] * 16,
        (vmem_spec(),) * parts,
        [pltpu.VMEM((depth, width), LOW), pltpu.SemaphoreType.DMA((16,))],
        flops=2 * rows * depth * width,
        bytes_moved=2 * (depth * width + rows * width + rows * depth),
        limit=60,
    )


def spec_rows(rows, width, turn=0, steps=4):
    if turn:
        return pl.BlockSpec((rows, width), lambda i: ((i + turn) % steps, 0))
    return pl.BlockSpec((rows, width), lambda i: (i, 0))


def spec_own(rows, width):
    return pl.BlockSpec((rows, width), lambda i: (jnp.minimum(i, 1), 0))


def spec_whole(shape):
    return pl.BlockSpec(shape, lambda i: (0,) * len(shape))


def row_stats(values):
    mean = jnp.mean(values, axis=1, keepdims=True)
    centered = values - mean
    inv = lax.rsqrt(jnp.mean(centered * centered, axis=1, keepdims=True) + EPSILON)
    return centered * inv, inv


def row_back(grad, unit, inv, gain):
    scaled = grad * gain
    return inv * (
        scaled
        - jnp.mean(scaled, axis=1, keepdims=True)
        - unit * jnp.mean(scaled * unit, axis=1, keepdims=True)
    )


def first_norm_kernel(x_ref, mine_ref, other_ref, vec_ref, unit_ref, inv_ref, low_ref):
    pre = x_ref[...].astype(WIDE) + (mine_ref[...].astype(WIDE) + other_ref[...].astype(WIDE)) + vec_ref[3:4, :]
    unit, inv = row_stats(pre)
    unit_ref[...] = unit
    inv_ref[...] = jnp.broadcast_to(inv, inv_ref.shape)
    low_ref[...] = (unit * vec_ref[5:6, :] + vec_ref[6:7, :]).astype(LOW)


def first_norm(x_all, mine, other, vectors):
    rows, width = x_all.shape
    step = rows // 4
    return call(
        first_norm_kernel,
        (shaped((rows, width), WIDE), shaped((rows, 128), WIDE), shaped((rows, width), LOW)),
        (x_all, mine, other, vectors),
        [spec_rows(step, width), spec_rows(step, width), spec_rows(step, width, 2), spec_whole(vectors.shape)],
        (spec_rows(step, width), spec_rows(step, 128), spec_rows(step, width)),
        grid=(4,),
        bytes_moved=12 * rows * width,
        limit=60,
    )


def feed_kernel(first, second, mid_ref, shift_ref, *refs):
    pieces, (act_ref, slope_ref, out_ref, buffer, below, sems, more_sems) = refs[:16], refs[16:]
    width = act_ref.shape[1]
    ready = fetch(pieces, (first, first + width), buffer, sems)
    later = fetch(pieces, (second, second + width), below, more_sems)
    ready(0, 16)

    for at in range(0, width, 256):
        cols = slice(at, at + 256)
        u = dot(mid_ref[...], buffer[:, cols]) + shift_ref[:, cols]
        phi = 0.5 + 0.5 * lax.erf(u * (2.0 ** -0.5))
        act_ref[:, cols] = (u * phi).astype(LOW)
        slope_ref[:, cols] = (phi + u * (jnp.exp(-0.5 * u * u) * (2.0 * math.pi) ** -0.5)).astype(LOW)
    step = below.shape[0] // 2
    for i in range(2):
        later(8 * i, 8 * i + 8)
        out_ref[:, i * step : i * step + step] = dot_nt(act_ref[...], below[i * step : i * step + step]).astype(LOW)


def feed(mid_low, shift, pieces, first, second, width):
    rows, depth = mid_low.shape
    out = shaped((rows, width), LOW)
    return call(
        functools.partial(feed_kernel, first, second),
        (out, out, shaped((rows, depth), LOW)),
        (mid_low, shift, *pieces),
        [vmem_spec()] * 2 + [any_spec()] * 16,
        (vmem_spec(),) * 3,
        [pltpu.VMEM((depth, width), LOW)] * 2 + [pltpu.SemaphoreType.DMA((16,))] * 2,
        limit=60,
    )


def second_norm_kernel(first, unit1_ref, mine_ref, other_ref, vec_ref, cot_ref, *refs):
    pieces = refs[:16]
    wide_ref, mid_ref, narrow_ref, grad_ref, low_ref, top_ref, sums_ref, proj, sems = refs[16:]
    step = pl.program_id(0)
    cols = proj.shape[1]

    @pl.when(step == 0)
    def _():
        fetch(pieces, (first, first + cols), proj, sems)(0, 16)
        sums_ref[...] = jnp.zeros_like(sums_ref)

    pre = (
        unit1_ref[...] * vec_ref[5:6, :]
        + vec_ref[6:7, :]
        + (mine_ref[...].astype(WIDE) + other_ref[...].astype(WIDE))
        + vec_ref[4:5, :]
    )
    unit, inv = row_stats(pre)
    top = (unit * vec_ref[7:8, :] + vec_ref[8:9, :]).astype(LOW)
    top_ref[...] = top

    @pl.when(step < 2)
    def _():
        wide_ref[...] = dot(top, proj[:, : wide_ref.shape[1]])
        flat = lax.dot_general(proj[:, 128:], top, (((0,), (1,)), ((), ())), preferred_element_type=WIDE)
        mid_ref[...] = flat[: mid_ref.shape[0]]
        narrow_ref[...] = flat[128 : 128 + narrow_ref.shape[0]]

    g_top = dot_nt(cot_ref[...], proj[...])
    g_sum = row_back(g_top, unit, inv, vec_ref[7:8, :])
    grad_ref[...] = g_sum
    low_ref[...] = g_sum.astype(LOW)
    sums_ref[0:1, :] += jnp.sum(g_sum, axis=0, keepdims=True)
    sums_ref[1:2, :] += jnp.sum(g_top * unit, axis=0, keepdims=True)
    sums_ref[2:3, :] += jnp.sum(g_top, axis=0, keepdims=True)


def second_norm(unit1, mine, other, vectors, cot_all, pieces, first, sizes):
    rows, width = unit1.shape
    step = rows // 4
    cols = cot_all.shape[1]
    return call(
        functools.partial(second_norm_kernel, first),
        (shaped((rows // 2, sizes[0]), WIDE), *(shaped((n, rows // 2), WIDE) for n in sizes[1:]))
        + (shaped((rows, width), WIDE), shaped((rows, width), LOW), shaped((rows, width), LOW), shaped((8, width), WIDE)),
        (unit1, mine, other, vectors, cot_all, *pieces),
        [
            spec_rows(step, width),
            spec_rows(step, width),
            spec_rows(step, width, 2),
            spec_whole(vectors.shape),
            spec_rows(step, cols),
        ]
        + [any_spec()] * 16,
        (spec_own(step, sizes[0]), *(pl.BlockSpec((n, step), lambda i: (0, jnp.minimum(i, 1))) for n in sizes[1:]))
        + (spec_rows(step, width), spec_rows(step, width), spec_rows(step, width), spec_whole((8, width))),
        [pltpu.VMEM((width, cols), LOW), pltpu.SemaphoreType.DMA((16,))],
        grid=(4,),
        flops=4 * rows * width * cols,
        bytes_moved=16 * rows * width,
        limit=60,
    )


def feed_back_kernel(first, second, g_ref, slope_ref, *refs):
    pieces, (grad_ref, sums_ref, out_ref, below, buffer, sems, more_sems) = refs[:16], refs[16:]
    width = grad_ref.shape[1]
    ready = fetch(pieces, (second, second + width), below, sems)
    later = fetch(pieces, (first, first + width), buffer, more_sems)
    ready(0, 16)

    def strip(n, _):
        for k in range(2):
            cols = pl.ds(pl.multiple_of(n * 512 + k * 256, 256), 256)
            g = (dot(g_ref[...], below[:, cols]) * slope_ref[:, cols].astype(WIDE)).astype(LOW)
            grad_ref[:, cols] = g
            sums_ref[:, cols] = jnp.sum(g.astype(WIDE), axis=0, keepdims=True)
        return 0

    lax.fori_loop(0, width // 512, strip, 0)
    step = buffer.shape[0] // 2
    for i in range(2):
        later(8 * i, 8 * i + 8)
        out_ref[:, i * step : i * step + step] = dot_nt(grad_ref[...], buffer[i * step : i * step + step]).astype(LOW)


def feed_back(grad_low, slope, pieces, first, second):
    rows, depth = grad_low.shape
    width = slope.shape[1]
    return call(
        functools.partial(feed_back_kernel, first, second),
        (shaped((rows, width), LOW), shaped((1, width), WIDE), shaped((rows, depth), LOW)),
        (grad_low, slope, *pieces),
        [vmem_spec()] * 2 + [any_spec()] * 16,
        (vmem_spec(),) * 3,
        [pltpu.VMEM((depth, width), LOW)] * 2 + [pltpu.SemaphoreType.DMA((16,))] * 2,
        limit=60,
    )


def fold_kernel(pairs, extra, *refs):
    at = 0
    groups = []
    for n in pairs:
        groups.append((refs[at], refs[at + 1 : at + 1 + n]))
        at += 1 + n
    add_ref = None
    if extra:
        add_ref = refs[at]
        at += 1
    outs, (buffer, sems) = refs[at : at + 16], refs[at + 16 :]
    rows = outs[0].shape[0]
    copies = [
        pltpu.make_async_copy(buffer.at[k * rows : (k + 1) * rows], out, sems.at[k]) for k, out in enumerate(outs)
    ]

    def quarter(i, _):
        block = pl.ds(pl.multiple_of(4 * rows * i, 4 * rows), 4 * rows)
        column = 0
        for left_ref, rights in groups:
            for right_ref in rights:
                size = right_ref.shape[1]
                for part in range(0, size, 512):
                    end = min(part + 512, size)
                    value = dot_tn(left_ref[:, block], right_ref[:, part:end])
                    if extra and right_ref is groups[-1][1][-1]:
                        value = value + add_ref[block].astype(WIDE)
                    buffer[block, column + part : column + end] = value.astype(LOW)
                column += size
        for j in range(4):

            @pl.when(i == j)
            def _():
                for copy in copies[4 * j : 4 * j + 4]:
                    copy.start()

        return 0

    lax.fori_loop(0, 4, quarter, 0)
    for copy in copies:
        copy.wait()


def fold(groups, extra=None):
    left = groups[0][0]
    rows, depth = left.shape
    ins = [a for l, rs in groups for a in (l, *rs)]
    width = sum(r.shape[1] for _, rs in groups for r in rs)
    total = width
    if extra is not None:
        ins.append(extra)
    piece = shaped((depth // 16, total), LOW)
    return call(
        functools.partial(fold_kernel, tuple(len(rs) for _, rs in groups), extra is not None),
        (piece,) * 16,
        ins,
        [vmem_spec()] * len(ins),
        (any_spec(),) * 16,
        [pltpu.VMEM((depth, total), LOW), pltpu.SemaphoreType.DMA((16,))],
        flops=2 * rows * depth * width,
        bytes_moved=2 * (depth * total + rows * width + rows * depth),
        limit=60,
    )


def middle_back_kernel(first, g_ref, mine_ref, other_ref, unit_ref, inv_ref, vec_ref, *refs):
    pieces, (own_ref, low_ref, ctx_ref, sums_ref, buffer, sems) = refs[:16], refs[16:]
    step = pl.program_id(0)
    rows, width = pieces[0].shape[0], ctx_ref.shape[1]
    copies = [
        pltpu.make_async_copy(
            piece.at[:, first : first + width], buffer.at[i * rows : (i + 1) * rows], sems.at[i]
        )
        for i, piece in enumerate(pieces)
    ]

    @pl.when(step == 0)
    def _():
        for copy in copies:
            copy.start()
        sums_ref[...] = jnp.zeros_like(sums_ref)

    unit = unit_ref[...]
    g_mid = g_ref[...] + (mine_ref[...].astype(WIDE) + other_ref[...].astype(WIDE))
    g_pre = row_back(g_mid, unit, inv_ref[:, :1], vec_ref[5:6, :])

    @pl.when(step < 2)
    def _():
        own_ref[...] = g_pre

    low = g_pre.astype(LOW)
    low_ref[...] = low
    sums_ref[0:1, :] += jnp.sum(g_pre, axis=0, keepdims=True)
    sums_ref[1:2, :] += jnp.sum(g_mid * unit, axis=0, keepdims=True)
    sums_ref[2:3, :] += jnp.sum(g_mid, axis=0, keepdims=True)

    @pl.when(step == 0)
    def _():
        for copy in copies:
            copy.wait()

    ctx_ref[...] = dot(low, buffer[...]).astype(LOW)


def middle_back(grad, mine, other, unit, inv, vectors, pieces, first, out_width):
    rows, width = grad.shape
    step = rows // 4
    return call(
        functools.partial(middle_back_kernel, first),
        (
            shaped((rows // 2, width), WIDE), shaped((rows, width), LOW), shaped((rows, out_width), LOW),
            shaped((8, width), WIDE),
        ),
        (grad, mine, other, unit, inv, vectors, *pieces),
        [
            spec_rows(step, width),
            spec_rows(step, width),
            spec_rows(step, width, 2),
            spec_rows(step, width),
            spec_rows(step, 128),
            spec_whole(vectors.shape),
        ]
        + [any_spec()] * 16,
        (spec_own(step, width), spec_rows(step, width), spec_rows(step, out_width), spec_whole((8, width))),
        [pltpu.VMEM((width, out_width), LOW), pltpu.SemaphoreType.DMA((16,))],
        grid=(4,),
        limit=60,
    )


def finish_kernel(place_ref, g_ref, mine_ref, other_ref, out_ref):
    z, y, x = place_ref[0], place_ref[1], place_ref[2]
    turn = x == 1
    for block in range(8):
        zb, yb = block // 2, block % 2
        source = pl.multiple_of((((zb + 4 - z) % 4) * 2 + (yb + y) % 2) * 128, 128)
        cols = pl.ds(source, 128)
        part = g_ref[:, cols] + mine_ref[:, cols].astype(WIDE) + other_ref[:, cols].astype(WIDE)
        out_ref[:, block * 128 : block * 128 + 128] = jnp.where(turn, pltpu.roll(part, 64, 1), part)


def finish(grad, mine, other):
    if not gridded():
        return grad + mine.astype(WIDE) + other.astype(WIDE)
    rows, width = grad.shape
    return call(
        finish_kernel,
        shaped((rows, width), WIDE),
        (grid_place(), grad, mine, other),
        [pl.BlockSpec(memory_space=pltpu.SMEM)] + [vmem_spec()] * 3,
        vmem_spec(),
        bytes_moved=12 * rows * width,
        limit=60,
    )


def small_kernel(*refs):
    vectors, heads, (out_ref, rows_ref) = refs[:10], refs[10:13], refs[13:]
    rows_ref[...] = jnp.zeros_like(rows_ref)
    for i, ref in enumerate(vectors):
        rows_ref[i : i + 1, : ref.shape[1]] = ref[...]
    out_ref[...] = jnp.zeros_like(out_ref)
    out_ref[:16, :128] = rows_ref[...].astype(LOW)
    for i, ref in enumerate(heads):
        out_ref[16 : 16 + ref.shape[0], 128 * i : 128 * i + ref.shape[1]] = ref[...].astype(LOW)


def small_pack(vectors, heads):
    piece = heads[0].shape[0]
    ins = [v.reshape(1, -1) for v in vectors] + list(heads)
    return call(
        small_kernel,
        shaped((16 + piece, 384), LOW),
        ins,
        [vmem_spec()] * len(ins),
        vmem_spec(),
        [pltpu.VMEM((16, 128), WIDE)],
        bytes_moved=100000,
        limit=60,
    )


def pack_rows_kernel(spot_ref, q_ref, k_ref, v_ref, o_ref, mine_ref, other_ref, out_ref):
    first = spot_ref[3] == 0
    width = q_ref.shape[1]
    for i, ref in enumerate((q_ref, k_ref, v_ref, o_ref)):
        out_ref[:, i * width : i * width + width] = ref[...].astype(LOW)
    piece = out_ref.shape[0] // 2
    mine, other = mine_ref[:16, :128].astype(WIDE), other_ref[:16, :128].astype(WIDE)
    zero, one = jnp.where(first, mine, other), jnp.where(first, other, mine)
    lane = lax.broadcasted_iota(jnp.int32, zero.shape, 1)
    row = lax.broadcasted_iota(jnp.int32, zero.shape, 0)
    both = jnp.where(lane < piece, zero, pltpu.roll(one, piece, 1))
    both = jnp.where(row == 9, zero, jnp.where(row == 10, pltpu.roll(one, 1, 0), both))
    out_ref[:16, 4 * width :] = both.astype(LOW)
    out_ref[16:, 4 * width :] = jnp.zeros((2 * piece - 16, 128), LOW)


def pack_rows(spot, weights, mine, other):
    rows, width = weights[0].shape
    return call(
        pack_rows_kernel,
        shaped((rows, 4 * width + 128), LOW),
        (spot, *weights, mine, other),
        [pl.BlockSpec(memory_space=pltpu.SMEM)] + [vmem_spec()] * 6,
        vmem_spec(),
        bytes_moved=18 * rows * width,
        limit=60,
    )


def pack_heads_kernel(spot_ref, up_ref, down_ref, mine_ref, other_ref, out_ref):
    first = spot_ref[3] == 0
    width = 2 * up_ref.shape[1]
    piece = out_ref.shape[0] // 2
    out_ref[:, : width // 2] = up_ref[...].astype(LOW)
    out_ref[:, width // 2 : width] = down_ref[...].astype(LOW)
    mine, other = mine_ref[16:], other_ref[16:]
    out_ref[:piece, width:] = jnp.where(first, mine, other)
    out_ref[piece:, width:] = jnp.where(first, other, mine)


def pack_heads(spot, up, down, mine, other):
    rows, width = up.shape
    return call(
        pack_heads_kernel,
        shaped((rows, 2 * width + 384), LOW),
        (spot, up, down, mine, other),
        [pl.BlockSpec(memory_space=pltpu.SMEM)] + [vmem_spec()] * 4,
        vmem_spec(),
        bytes_moved=6 * rows * width,
        limit=60,
    )


def vectors_kernel(first, spot_ref, *refs):
    pieces, (vec_ref, qkv_ref, up_ref, low_buffer, rows_ref, sems) = refs[:16], refs[16:]
    z, y, x, core = spot_ref[0], spot_ref[1], spot_ref[2], spot_ref[3]
    copies = []
    for i, piece in enumerate(pieces):
        copy = pltpu.make_async_copy(
            piece.at[0:16, first : first + 128], low_buffer.at[16 * i : 16 * i + 16], sems.at[i]
        )
        copy.start()
        copies.append(copy)
    for copy in copies:
        copy.wait()
    rows_ref[...] = low_buffer[...].astype(WIDE)
    lane = lax.broadcasted_iota(jnp.int32, (16, 128), 1)
    for j in range(8):
        even, odd = rows_ref[32 * j : 32 * j + 16], rows_ref[32 * j + 16 : 32 * j + 32]
        vec_ref[:, 128 * j : 128 * j + 128] = jnp.where(lane < 64, even, pltpu.roll(odd, 64, 1))
    turn = x == 1
    blocks = qkv_ref.shape[1] // 384
    for b in range(blocks):
        source = ((core * 2 + b // 2 + 4 - z) % 4) * 2 + (b % 2 + y) % 2
        part = vec_ref[:, pl.ds(pl.multiple_of(source * 128, 128), 128)]
        part = jnp.where(turn, pltpu.roll(part, 64, 1), part)
        for j in range(3):
            at = (j * blocks + b) * 128
            qkv_ref[:, at : at + 128] = part[j : j + 1]
    for j in range(8):
        key = (((core * 2 + j // 4 + 4 - z) % 4) * 2 + (j // 2 % 2 + y) % 2) * 2 + (j % 2 + x) % 2
        for t in range(2):
            at = j * 256 + t * 128
            up_ref[:, at : at + 128] = rows_ref[pl.ds(key * 16 + 9 + t, 1), :]


def read_vectors(spot, pieces, first, width, head_width, hidden):
    return call(
        functools.partial(vectors_kernel, first),
        (shaped((16, width), WIDE), shaped((1, 3 * head_width), WIDE), shaped((1, hidden), WIDE)),
        (spot, *pieces),
        [pl.BlockSpec(memory_space=pltpu.SMEM)] + [any_spec()] * 16,
        (vmem_spec(),) * 3,
        [pltpu.VMEM((256, 128), LOW), pltpu.VMEM((256, 128), WIDE), pltpu.SemaphoreType.DMA((16,))],
        bytes_moved=200000,
        limit=60,
    )


def sums_kernel(zero_ref, one_ref, up_ref, out_ref, rows_ref):
    rows_ref[...] = jnp.zeros_like(rows_ref)
    half = zero_ref.shape[1]
    rows_ref[0:3, :half] = zero_ref[...]
    rows_ref[0:3, half : 2 * half] = one_ref[...]
    rows_ref[3:4, :] = up_ref[...]
    out_ref[...] = rows_ref[...].astype(LOW)


def pack_sums(zero, one, up):
    width = up.shape[1]
    return call(
        sums_kernel,
        shaped((16, width), LOW),
        (zero, one, up),
        [vmem_spec()] * 3,
        vmem_spec(),
        [pltpu.VMEM((16, width), WIDE)],
        bytes_moved=100000,
        limit=60,
    )


def vector_grads_kernel(share, spot_ref, mine_ref, other_ref, mid_ref, top_ref, out_ref, plain, long, block):
    z, y, x, core = spot_ref[0], spot_ref[1], spot_ref[2], spot_ref[3]
    turn = x == 1
    half = plain.shape[1] // 2
    hidden = mine_ref.shape[1]
    mine, other = mine_ref[...].astype(WIDE), other_ref[...].astype(WIDE)
    for i in range(2):
        side = jnp.where(core == i, mine, other)
        plain[:, i * half : i * half + half] = side[:8, :half]
        long[:, i * hidden : i * hidden + hidden] = side[3:4]
    out_ref[...] = jnp.zeros_like(out_ref)
    for j in range(8):
        source = ((j // 2 + z) % 4) * 2 + (j % 2 + y) % 2
        part = plain[:, pl.ds(pl.multiple_of(source * 128, 128), 128)]
        part = jnp.where(turn, pltpu.roll(part, 64, 1), part)
        cols = slice(128 * j, 128 * j + 128)
        block[0:3, :] = part[0:3]
        block[3:4, :] = mid_ref[0:1, cols]
        block[4:5, :] = top_ref[0:1, cols]
        block[5:7, :] = mid_ref[1:3, cols]
        block[7:9, :] = top_ref[1:3, cols]
        block[9:16, :] = jnp.zeros((7, 128), WIDE)
        pair = block[...]
        for odd in range(2):
            owner = source * 2 + (odd + x) % 2
            block[...] = pltpu.roll(pair, 64, 1) if odd else pair
            for t in range(2):
                wide_row = long[:, pl.ds(pl.multiple_of(owner * 256 + t * 128, 128), 128)]
                block[9 + 2 * t : 10 + 2 * t, :] = wide_row
                block[10 + 2 * t : 11 + 2 * t, :] = pltpu.roll(wide_row, 64, 1)
            at = (2 * j + odd) * 64
            out_ref[at : at + 16, share - 64 : share] = jnp.where(core == 1, block[:, :64], 0.0).astype(LOW)


def spread_vector_grads(spot, mine, other, mid_sums, top_sums, share):
    width = mid_sums.shape[1]
    hidden = mine.shape[1]
    return call(
        functools.partial(vector_grads_kernel, share),
        shaped((width, share), LOW),
        (spot, mine, other, mid_sums, top_sums),
        [pl.BlockSpec(memory_space=pltpu.SMEM)] + [vmem_spec()] * 4,
        vmem_spec(),
        [pltpu.VMEM((8, width), WIDE), pltpu.VMEM((1, 2 * hidden), WIDE), pltpu.VMEM((16, 128), WIDE)],
        bytes_moved=400000,
        limit=60,
    )


def local(
    hidden_in,
    segment_ids,
    positions,
    query_weight,
    key_weight,
    value_weight,
    output_weight,
    up_weight,
    down_weight,
    query_bias,
    key_bias,
    value_bias,
    output_bias,
    up_bias,
    down_bias,
    attn_gain,
    attn_shift,
    ffn_gain,
    ffn_shift,
    proj_wide,
    proj_mid,
    proj_narrow,
    cot_wide,
    cot_mid,
    cot_narrow,
):
    tp_rank = lax.axis_index("tp")
    own_rows, width = hidden_in.shape
    head_width = query_weight.shape[1]
    heads_here = head_width // HD
    hidden_here = up_weight.shape[1]
    piece = query_bias.shape[0]
    low, wide = LOW, WIDE
    half = head_width // 2
    half_heads = heads_here // 2

    spot = jnp.concatenate([grid_place(), tp_rank[None].astype(jnp.int32)])
    first_core = tp_rank == 0

    small = small_pack(
        (
            query_bias, key_bias, value_bias, output_bias, down_bias,
            attn_gain, attn_shift, ffn_gain, ffn_shift, up_bias,
        ),
        (proj_wide, proj_mid, proj_narrow),
    )
    small_other = other_core(small)
    attn_weights = (query_weight, key_weight, value_weight, output_weight.T)
    if gridded():
        attn_group = Gather(pack_rows(spot, attn_weights, small, small_other))
        ffn_group = Gather(pack_heads(spot, up_weight, down_weight.T, small, small_other))
    else:
        small_zero = jnp.where(first_core, small, small_other)
        small_one = jnp.where(first_core, small_other, small)
        attn_group = Gather(pack([*attn_weights, jnp.zeros((2 * piece, 128), low)]))
        heads_pair = jnp.concatenate([small_zero[16:], small_one[16:]], axis=0)
        ffn_group = Gather(pack([up_weight, down_weight.T, heads_pair]))
    queue = Queue()
    queue.add(attn_group, (0,))
    queue.add(attn_group, (1, 2), ffn_group.have[OWN])
    queue.add(attn_group, range(3, 6), *queue.at(0))

    tags = after(jnp.stack([segment_ids, positions]), *queue.at(2))
    tags = jnp.concatenate([tags, other_core(tags)], axis=1)
    hidden_other = other_core(after(hidden_in, *queue.at(1)))
    x_all = reorder(jnp.concatenate([hidden_in, hidden_other], axis=0), False)
    cot_own = jnp.concatenate(
        [cot_wide, jnp.pad(cot_mid, ((0, 0), (0, 128 - cot_mid.shape[1]))), jnp.pad(cot_narrow, ((0, 0), (0, 128 - cot_narrow.shape[1])))],
        axis=1,
    )
    cot_all = jnp.concatenate([cot_own, other_core(after(cot_own, *queue.at(3)))], axis=0)
    column, row = tags[0].reshape(-1, 1), tags[0].reshape(1, -1)
    cos_table, sin_table = rope_tables(tags[1], HD)
    cos_table = jnp.concatenate([cos_table, cos_table], axis=1)
    sin_table = jnp.concatenate([-sin_table[:, : HD // 2], sin_table[:, HD // 2 :]] * 2, axis=1)

    queue.add(attn_group, range(6, 9), places=4)
    queue.add(attn_group, range(9, 12), x_all, cot_all, cos_table, sin_table, places=4)
    queue.add(attn_group, range(12, 15), places=4)
    queue.add(ffn_group, range(3), *queue.at(12, 13, 14))
    attn_pieces = attn_group.pieces()
    if gridded():
        vectors, qkv_shift, up_shift = read_vectors(
            spot, attn_pieces, 4 * head_width, width, head_width, hidden_here
        )
    else:
        pair = jnp.stack([small_zero[:16, :128], small_one[:16, :128]])
        pair = lax.all_gather(pair[None], "fsdp", axis=0, tiled=True).astype(wide)
        vectors = pair[..., :piece].transpose(2, 0, 1, 3).reshape(16, width)
        qkv_shift = lax.dynamic_slice_in_dim(vectors[:3], tp_rank * head_width, head_width, 1).reshape(1, -1)
        up_shift = lax.dynamic_slice_in_dim(
            pair[:, :, 9, : 4 * piece].reshape(1, -1), tp_rank * hidden_here, hidden_here, 1
        )

    query, key, value = project_qkv(x_all, qkv_shift, cos_table, sin_table, attn_pieces, head_width)
    first_half = attend(query, key, value, column, row, 0, half_heads)
    queue.add(ffn_group, range(3, 6), first_half[0], *queue.at(15, 16, 17))
    second_half = attend(after(query, first_half[0], *queue.at(15, 16, 17)), key, value, column, row, 1, half_heads)
    contexts, probs = zip(first_half, second_half)
    (attn_mine,) = spread(contexts, attn_pieces, 3 * head_width, head_width)
    unit_one, inv_one, mid_low = first_norm(
        x_all, attn_mine, other_core(after(attn_mine, *queue.at(18, 19, 20))), vectors
    )
    queue.add(ffn_group, range(6, 9), attn_mine, *queue.at(18, 19, 20))
    queue.add(ffn_group, range(9, 15), places=4)
    ffn_pieces = ffn_group.pieces()
    act_low, slope, ffn_mine = feed(mid_low, up_shift, ffn_pieces, 0, hidden_here, hidden_here)
    embed_wide, embed_mid, embed_narrow, grad_top, grad_top_low, top_low, top_sums = second_norm(
        unit_one, ffn_mine, other_core(ffn_mine), vectors, cot_all, ffn_pieces, 2 * hidden_here,
        (proj_wide.shape[1], proj_mid.shape[1], proj_narrow.shape[1]),
    )

    share = 192
    cot_share = lax.dynamic_slice_in_dim(cot_all, tp_rank * share, share, 1)
    grad_hidden_low, up_sums, mid_mine = feed_back(grad_top_low, slope, ffn_pieces, 0, hidden_here)
    mid_other = other_core(mid_mine)
    ffn_scatter = Scatter(fold([(after(grad_top_low, mid_mine), [act_low]), (mid_low, [grad_hidden_low])]))
    back = Queue()
    back.add(ffn_scatter, (0, 1, 2, 4, 3))
    grad_own, grad_mid_low, grad_context, mid_sums = middle_back(
        grad_top, mid_mine, mid_other, unit_one, inv_one, vectors, attn_pieces, 3 * head_width, head_width
    )
    back.add(ffn_scatter, (5,), grad_context)
    backs = []
    for i in range(2):
        ready = [backs[0][0]] if i else back.at(0, 1, 2)
        backs.append(
            attend_back(query, key, value, after(grad_context, *ready), probs[i], cos_table, sin_table, i, half_heads)
        )
        back.add(ffn_scatter, (8, 9) if i else (6, 7), backs[i][0])
    grads = [backs[i][j] for j in range(3) for i in range(2)]
    sums = pack_sums(backs[0][3], backs[1][3], up_sums)
    sums_other = other_core(sums)
    if gridded():
        extra = spread_vector_grads(spot, sums, sums_other, mid_sums, top_sums, share)
    else:
        extra = jnp.zeros((width, share), low)
    attn_scatter = Scatter(
        fold([(after(x_all, *back.at(3, 4, 5)), grads), (grad_mid_low, list(contexts)), (top_low, [cot_share])], extra)
    )
    back.add(attn_scatter, (0, 1, 2))
    back.add(ffn_scatter, (10,), attn_scatter.held[OWN])
    x_mine, x_sent = spread([after(grads[0], attn_scatter.held[OWN], *back.at(7, 8))] + grads[1:], attn_pieces, 0, 3 * head_width, 2)
    back.add(ffn_scatter, (11, 12), x_mine)
    back.add(attn_scatter, (3, 4), x_mine)
    x_other = other_core(x_sent)
    grad_hidden = finish(grad_own, x_mine, x_other)
    for group, number in (
        (attn_scatter, 5), (attn_scatter, 6), (ffn_scatter, 13), (attn_scatter, 7), (attn_scatter, 8), (ffn_scatter, 14),
    ):
        back.add(group, (number,), places=5)
    back.add(attn_scatter, range(9, 15), places=5)
    ffn_part = ffn_scatter.rows()
    attn_part = attn_scatter.rows()

    small_part = attn_part[:, 4 * head_width :]
    small_away = other_core(small_part)
    joined = jnp.where(
        first_core,
        jnp.concatenate([small_part, small_away], axis=1),
        jnp.concatenate([small_away, small_part], axis=1),
    ).astype(wide)
    own_heads = lax.dynamic_slice_in_dim(joined, tp_rank * piece, piece, 0)
    if gridded():
        block = joined[:16, 2 * share - 64 :]
        own_vectors = lax.dynamic_slice_in_dim(block[:9], tp_rank * piece, piece, 1)
        own_up = lax.dynamic_slice_in_dim(block, 9 + 2 * tp_rank, 2, 0).reshape(-1)
    else:
        both = jnp.concatenate(
            [
                jnp.where(first_core, sums, sums_other)[:3, :head_width],
                jnp.where(first_core, sums_other, sums)[:3, :head_width],
            ],
            axis=1,
        ).astype(wide)
        table = jnp.concatenate(
            [both, mid_sums[:1], top_sums[:1], mid_sums[1:3], top_sums[1:3], jnp.zeros((7, width), wide)], axis=0
        )
        table = lax.psum_scatter(table, "fsdp", scatter_dimension=1, tiled=True)
        own_vectors = lax.dynamic_slice_in_dim(table, tp_rank * piece, piece, 1)
        long = lax.dynamic_update_slice_in_dim(
            jnp.zeros((2 * hidden_here,), wide), up_sums.reshape(-1), tp_rank * hidden_here, 0
        )
        own_up = lax.psum_scatter(long, ("fsdp", "tp"), scatter_dimension=0, tiled=True)
    attn_part = attn_part.astype(wide)
    return (
        embed_wide,
        embed_mid.T,
        embed_narrow.T,
        grad_hidden,
        attn_part[:, :head_width],
        attn_part[:, head_width : 2 * head_width],
        attn_part[:, 2 * head_width : 3 * head_width],
        attn_part[:, 3 * head_width : 4 * head_width].T,
        ffn_part[:, hidden_here:].astype(wide),
        ffn_part[:, :hidden_here].astype(wide).T,
        own_vectors[0],
        own_vectors[1],
        own_vectors[2],
        own_vectors[3],
        own_up,
        own_vectors[4],
        own_vectors[5],
        own_vectors[6],
        own_vectors[7],
        own_vectors[8],
        own_heads[:, : proj_wide.shape[1]],
        own_heads[:, 128 : 128 + proj_mid.shape[1]],
        own_heads[:, 256 : 256 + proj_narrow.shape[1]],
    )


def solution(mesh):
    return jax.shard_map(
        local,
        mesh=mesh,
        in_specs=(
            P(("fsdp", "tp"), None),
            P(("fsdp", "tp")),
            P(("fsdp", "tp")),
            P("fsdp", "tp"),
            P("fsdp", "tp"),
            P("fsdp", "tp"),
            P("tp", "fsdp"),
            P("fsdp", "tp"),
            P("tp", "fsdp"),
            P(("fsdp", "tp")),
            P(("fsdp", "tp")),
            P(("fsdp", "tp")),
            P(("fsdp", "tp")),
            P(("fsdp", "tp")),
            P(("fsdp", "tp")),
            P(("fsdp", "tp")),
            P(("fsdp", "tp")),
            P(("fsdp", "tp")),
            P(("fsdp", "tp")),
            P(("fsdp", "tp"), None),
            P(("fsdp", "tp"), None),
            P(("fsdp", "tp"), None),
            P(("fsdp", "tp"), None),
            P(("fsdp", "tp"), None),
            P(("fsdp", "tp"), None),
        ),
        out_specs=(
            P(("fsdp", "tp"), None),
            P(("fsdp", "tp"), None),
            P(("fsdp", "tp"), None),
            P(("fsdp", "tp"), None),
            P("fsdp", "tp"),
            P("fsdp", "tp"),
            P("fsdp", "tp"),
            P("tp", "fsdp"),
            P("fsdp", "tp"),
            P("tp", "fsdp"),
            P(("fsdp", "tp")),
            P(("fsdp", "tp")),
            P(("fsdp", "tp")),
            P(("fsdp", "tp")),
            P(("fsdp", "tp")),
            P(("fsdp", "tp")),
            P(("fsdp", "tp")),
            P(("fsdp", "tp")),
            P(("fsdp", "tp")),
            P(("fsdp", "tp")),
            P(("fsdp", "tp"), None),
            P(("fsdp", "tp"), None),
            P(("fsdp", "tp"), None),
        ),
        check_vma=False,
    )
```
